32 devices in a mesh: branch: 8 (over y, x, core), dap: 4 (over z).
Axes of the slice: x: 2, y: 2, z: 4, core: 2. Of those that a mesh axis runs over, the one named last changes fastest.
Arguments:
- homolog_embedding: bfloat16 [128, 256, 256], P(('branch', 'dap')), may hold values from -6 to 6
- couple_embedding: bfloat16 [256, 256, 128], P(('branch', 'dap')), may hold values from -6 to 6
- homolog_present: int32 [128, 256], P(('branch', 'dap')), may hold values from 0 to 1
- observed_position: int32 [256], replicated, may hold values 0 or 1
- couple_logit_kernel: bfloat16 [128, 8], replicated, may hold values from -40 to 40
- lookup_kernels: bfloat16 [256, 768], replicated, may hold values from -0.375 to 0.375
- heads_sigmoid_kernel: bfloat16 [256, 256], replicated, may hold values from -0.375 to 0.375
- heads_merge_kernel: bfloat16 [256, 256], replicated, may hold values from -0.375 to 0.375
- tensor_halves_kernel: bfloat16 [256, 64], replicated, may hold values from -0.375 to 0.375
- tensor_merge_kernel: bfloat16 [1024, 128], replicated, may hold values from -0.1875 to 0.1875
- edge_entry_kernel: bfloat16 [128, 512], replicated, may hold values from -0.5 to 0.5
- closing_sigmoid_kernel: bfloat16 [128, 128], replicated, may hold values from -0.5 to 0.5
- closing_merge_kernel: bfloat16 [128, 128], replicated, may hold values from -0.5 to 0.5
Outputs:
- homolog_refreshed: bfloat16 [128, 256, 256], P(('branch', 'dap'))
- pair_output: bfloat16 [256, 256, 128], P(('branch', 'dap'))
The draws below stay inside these ranges and needn't reach their ends.
All inputs are finite; a program needn't handle non-finite values.
Results may differ from the reference program's by a relative error of at most 0.013.
The reference program's roundings to bfloat16 on the way count: a program that leaves them out, or rounds other values in their place, can miss the bound.
Values may be sent and summed in bfloat16 or wider, within the bound.
No kernel may reach another device: no remote copies, remote signals or barrier semaphores. Data moves between devices by JAX's collectives and lax.ppermute only.
A program may use at most 128 MiB of HBM per device.

```python
import jax
import jax.numpy as jnp
from jax import lax

FEATURE_DEPTH = 256
CZ = 128
ROW_HEAD_COUNT = 8
HEAD_SPAN = 32
PROJECTED_WIDTH = 32
CT = 128
CHAIN_LENGTH = 256
HOMOLOG_COUNT = 128


def draw_couple_logit_kernel(key, part):
    noise = jax.random.normal(jax.random.fold_in(key, 11), (CZ, ROW_HEAD_COUNT), jnp.float32)
    values = noise * CZ ** (-0.5)
    return jnp.clip(values, -40.0, 40.0).astype(jnp.bfloat16)


def draw_homolog_present(key, part):
    rank = jax.random.permutation(jax.random.fold_in(key, 21), CHAIN_LENGTH)
    absent = max(CHAIN_LENGTH // 64, 2)
    sparse = max(CHAIN_LENGTH // 32, 2)
    levels = jax.random.randint(jax.random.fold_in(key, 22), (CHAIN_LENGTH,), 8, 16)
    cyclic_shifts = jax.random.randint(jax.random.fold_in(key, 23), (HOMOLOG_COUNT, CHAIN_LENGTH), 0, 16)
    common = cyclic_shifts < levels[None, :]
    chosen_indices = jax.random.randint(jax.random.fold_in(key, 24), (HOMOLOG_COUNT, CHAIN_LENGTH), 0, HOMOLOG_COUNT)
    scarce = chosen_indices < 3
    present = jnp.where(rank[None, :] < absent, False, jnp.where(rank[None, :] < absent + sparse, scarce, common))
    return present.astype(jnp.int32)


def place_ends(values, stream_key, least, largest):
    spot = [jax.random.randint(jax.random.fold_in(stream_key, axis), (), 0, length) for axis, length in enumerate(values.shape)]
    main_axis = values.shape.index(max(values.shape))
    neighbour = spot[:main_axis] + [(spot[main_axis] + 1) % values.shape[main_axis]] + spot[main_axis + 1:]
    return values.at[tuple(spot)].set(least).at[tuple(neighbour)].set(largest)


def steps_of(own_key, extent, pieces, low, largest):
    factor_of, own = 1.0, jax.random.fold_in(own_key, 6)
    for axis_at, blocks in pieces:
        steps = jnp.exp(jax.random.uniform(jax.random.fold_in(own, axis_at), (blocks,), jnp.float32, low / len(pieces), largest / len(pieces)))
        factor_of = factor_of * jnp.repeat(steps, extent[axis_at] // blocks).reshape([-1 if axis == axis_at else 1 for axis in range(len(extent))])
    return factor_of


def scatter_about(own_key, extent, width, most, cuts=(), held_as=jnp.bfloat16):
    array = jax.random.normal(own_key, extent, jnp.float32) * width
    if len(cuts) > 0:
        array = steps_of(own_key, extent, cuts, -0.22, 0.18) * array
    return jnp.clip(array, min=-most, max=most).astype(held_as)


def setup_inputs(seed: int = 0) -> dict:
    streams_of = jax.random.split(jax.random.key(seed), 14)
    return {
        "homolog_embedding": scatter_about(streams_of[0], (HOMOLOG_COUNT, CHAIN_LENGTH, FEATURE_DEPTH), 1.0, 6.0, ((0, 32),)),
        "couple_embedding": scatter_about(streams_of[1], (CHAIN_LENGTH, CHAIN_LENGTH, CZ), 1.0, 6.0, ((0, 32),)),
        "homolog_present": draw_homolog_present(jax.random.fold_in(streams_of[13], 71), 0),
        "observed_position": place_ends((jax.random.randint(streams_of[3], (CHAIN_LENGTH,), 0, 16) < 15).astype(jnp.int32), jax.random.fold_in(streams_of[3], 1), 0, 1),
        "couple_logit_kernel": draw_couple_logit_kernel(jax.random.fold_in(streams_of[13], 71), 0),
        "lookup_kernels": scatter_about(streams_of[5], (FEATURE_DEPTH, 3 * ROW_HEAD_COUNT * HEAD_SPAN), FEATURE_DEPTH ** -0.5, 0.375),
        "heads_sigmoid_kernel": scatter_about(streams_of[6], (FEATURE_DEPTH, ROW_HEAD_COUNT * HEAD_SPAN), FEATURE_DEPTH ** -0.5, 0.375),
        "heads_merge_kernel": scatter_about(streams_of[7], (ROW_HEAD_COUNT * HEAD_SPAN, FEATURE_DEPTH), (ROW_HEAD_COUNT * HEAD_SPAN) ** -0.5, 0.375),
        "tensor_halves_kernel": scatter_about(streams_of[8], (FEATURE_DEPTH, 2 * PROJECTED_WIDTH), FEATURE_DEPTH ** -0.5, 0.375),
        "tensor_merge_kernel": scatter_about(streams_of[9], (PROJECTED_WIDTH * PROJECTED_WIDTH, CZ), (PROJECTED_WIDTH * PROJECTED_WIDTH) ** -0.5, 0.1875),
        "edge_entry_kernel": scatter_about(streams_of[10], (CZ, 4 * CT), CZ ** -0.5, 0.5),
        "closing_sigmoid_kernel": scatter_about(streams_of[11], (CZ, CZ), CZ ** -0.5, 0.5),
        "closing_merge_kernel": scatter_about(streams_of[12], (CT, CZ), CT ** -0.5, 0.5),
    }


epsilon = 1e-05

def normalize(values):
    values = values.astype(jnp.float32)
    centred = values - lax.optimization_barrier(jnp.mean(values, axis=-1, keepdims=True))
    spread = lax.optimization_barrier(jnp.mean(centred * centred, axis=-1, keepdims=True))
    return centred * lax.rsqrt(spread + epsilon)

def row_update(sequence, keep, bias_full, lookup_kernels, heads_sigmoid_kernel, heads_merge_kernel, tensor_halves_kernel):
    heads = bias_full.shape[0]
    inner = lookup_kernels.shape[1] // 3
    head_width = inner // heads
    normed = normalize(sequence).astype(jnp.bfloat16)
    projected = jnp.dot(normed, lookup_kernels, preferred_element_type=jnp.float32).astype(jnp.bfloat16)
    queries = projected[:, :inner].reshape(-1, heads, head_width).astype(jnp.float32)
    key_rows = projected[:, inner:2 * inner].reshape(-1, heads, head_width).astype(jnp.float32)
    value_rows = projected[:, 2 * inner:].reshape(-1, heads, head_width).astype(jnp.float32)
    gating = jax.nn.sigmoid(jnp.dot(normed, heads_sigmoid_kernel, preferred_element_type=jnp.float32)).reshape(-1, heads, head_width)
    logits = jnp.einsum('ihd,jhd->hij', queries, key_rows)
    masking = jnp.where(keep == 1, 0.0, -1000000000.0)
    logits = logits * head_width ** (-0.5) + bias_full.astype(jnp.float32) + masking[None, None, :]
    weights = jax.nn.softmax(logits, axis=-1).astype(jnp.bfloat16)
    mixed = jnp.einsum('hij,jhd->ihd', weights.astype(jnp.float32), value_rows)
    attended = (mixed * gating).astype(jnp.bfloat16).reshape(-1, inner)
    updated = sequence.astype(jnp.float32) + jnp.dot(attended, heads_merge_kernel, preferred_element_type=jnp.float32)
    updated = updated.astype(jnp.bfloat16)
    projected_halves = jnp.dot(normalize(updated).astype(jnp.bfloat16), tensor_halves_kernel, preferred_element_type=jnp.float32)
    projected_halves = (projected_halves * keep.astype(jnp.float32)[:, None]).astype(jnp.bfloat16)
    return (updated, projected_halves)

def edge_factors(normed, row_marks, observed_position, edge_entry_kernel):
    inner = edge_entry_kernel.shape[1] // 4
    projected = jnp.dot(normed, edge_entry_kernel, preferred_element_type=jnp.float32)
    pair_marks = (row_marks[:, None] * observed_position[None, :]).astype(jnp.float32)[:, :, None]
    left_edge = jax.nn.sigmoid(projected[..., inner:2 * inner]) * projected[..., :inner] * pair_marks
    right_edge = jax.nn.sigmoid(projected[..., 3 * inner:]) * projected[..., 2 * inner:3 * inner] * pair_marks
    return (left_edge.astype(jnp.bfloat16), right_edge.astype(jnp.bfloat16))

def finish_triangle(pair_next, normed_next, combined, closing_sigmoid_kernel, closing_merge_kernel):
    combined_normed = normalize(combined).astype(jnp.bfloat16)
    update = jnp.dot(combined_normed, closing_merge_kernel, preferred_element_type=jnp.float32)
    gating = jax.nn.sigmoid(jnp.dot(normed_next, closing_sigmoid_kernel, preferred_element_type=jnp.float32))
    return (pair_next.astype(jnp.float32) + gating * update).astype(jnp.bfloat16)

def reference(homolog_embedding, couple_embedding, homolog_present, observed_position, couple_logit_kernel, lookup_kernels, heads_sigmoid_kernel, heads_merge_kernel, tensor_halves_kernel, tensor_merge_kernel, edge_entry_kernel, closing_sigmoid_kernel, closing_merge_kernel):
    pair_normed = normalize(couple_embedding).astype(jnp.bfloat16)
    bias_full = jnp.einsum('ijc,ch->hij', pair_normed.astype(jnp.float32), couple_logit_kernel.astype(jnp.float32)).astype(jnp.bfloat16)

    def homolog_along(item):
        return row_update(item[0], item[1], bias_full, lookup_kernels, heads_sigmoid_kernel, heads_merge_kernel, tensor_halves_kernel)
    homolog_refreshed, projected_halves = lax.map(homolog_along, (homolog_embedding, homolog_present))
    leading_projected = projected_halves[..., :PROJECTED_WIDTH].astype(jnp.float32)
    right_factor = projected_halves[..., PROJECTED_WIDTH:].astype(jnp.float32)
    presence_indicators = homolog_present.astype(jnp.float32)
    tile_portion = 16
    leading_tiles = leading_projected.reshape(HOMOLOG_COUNT, CHAIN_LENGTH // tile_portion, tile_portion, PROJECTED_WIDTH).transpose(1, 0, 2, 3)
    presence_tiles = presence_indicators.reshape(HOMOLOG_COUNT, CHAIN_LENGTH // tile_portion, tile_portion).transpose(1, 0, 2)
    table = tensor_merge_kernel.astype(jnp.float32)

    def outer_block(item):
        outer_sum = jnp.einsum('sip,sjq->ijpq', item[0], right_factor, precision=lax.Precision.HIGHEST)
        outer_sum = outer_sum.reshape(tile_portion, CHAIN_LENGTH, PROJECTED_WIDTH * PROJECTED_WIDTH)
        counts = jnp.einsum('si,sj->ij', item[1], presence_indicators, precision=lax.Precision.HIGHEST)
        projected = jnp.dot(outer_sum, table, precision=lax.Precision.HIGHEST)
        return projected / jnp.maximum(counts, 1.0)[:, :, None]
    update = lax.map(outer_block, (leading_tiles, presence_tiles)).reshape(CHAIN_LENGTH, CHAIN_LENGTH, CZ)
    pair_next = (couple_embedding.astype(jnp.float32) + update).astype(jnp.bfloat16)
    normed_next = normalize(pair_next).astype(jnp.bfloat16)
    left_edge, right_edge = edge_factors(normed_next, observed_position, observed_position, edge_entry_kernel)
    combined = jnp.einsum('ikc,jkc->ijc', left_edge.astype(jnp.float32), right_edge.astype(jnp.float32), precision=lax.Precision.HIGHEST)
    pair_output = finish_triangle(pair_next, normed_next, combined, closing_sigmoid_kernel, closing_merge_kernel)
    return (homolog_refreshed, pair_output)
```

```python
import functools

import jax
import jax.numpy as jnp
from jax import lax
from jax.experimental import pallas as pl
from jax.experimental.pallas import tpu as pltpu
from jax.sharding import PartitionSpec as P

EPSILON = 1e-05
EVERY = ("branch", "dap")
VMEM = pltpu.VMEM
F32 = jnp.float32
BF16 = jnp.bfloat16

NT = (((1,), (1,)), ((), ()))
TN = (((0,), (0,)), ((), ()))
NN = (((1,), (0,)), ((), ()))


def mm(a, b, dims=NN):
    return lax.dot_general(a, b, dims, preferred_element_type=F32)


def normalize(values, axis=-1):
    values = values.astype(F32)
    centred = values - jnp.mean(values, axis=axis, keepdims=True)
    spread = jnp.mean(centred * centred, axis=axis, keepdims=True)
    return centred * lax.rsqrt(spread + EPSILON)


def vspec():
    return pl.BlockSpec(memory_space=VMEM)


def sspec():
    return pl.BlockSpec(memory_space=pltpu.SMEM)


LANES = 128


def sheets(rows, columns):
    return VMEM((columns // LANES, rows, LANES), F32)


def put(scr, start, values, stride):
    for k in range(scr.shape[0]):
        part = values[:, k * LANES : (k + 1) * LANES]
        scr[k, pl.ds(start, values.shape[0], stride=stride), :] = part


def take(scr, start, count, stride=1):
    parts = [scr[k, pl.ds(start, count, stride=stride), :] for k in range(scr.shape[0])]
    return parts[0] if len(parts) == 1 else jnp.concatenate(parts, axis=1)


def fill(scr, values):
    for k in range(scr.shape[0]):
        scr[k] = values[:, k * LANES : (k + 1) * LANES]


def call(body, out, args, scratch=(), name=None, in_specs=None, flops=0, **kw):
    single = not isinstance(out, (tuple, list))
    return pl.pallas_call(
        body,
        out_shape=out,
        in_specs=in_specs or [vspec() for _ in args],
        out_specs=vspec() if single else tuple(vspec() for _ in out),
        scratch_shapes=list(scratch),
        name=name,
        cost_estimate=pl.CostEstimate(flops=flops, bytes_accessed=2**20, transcendentals=0),
        **kw,
    )(*args)


def bias_kernel(cores, couple_ref, weight_ref, out_ref, scr):
    rows = couple_ref.shape[0]
    heads = weight_ref.shape[0]
    for i in range(rows):
        normed = normalize(couple_ref[i]).astype(BF16)
        put(scr, i, mm(weight_ref[...], normed, NT), rows)
    part = heads // 2 * rows
    halves = [take(scr, k * part, part).astype(BF16) for k in range(2)]
    for t, core in enumerate(cores):
        out_ref[t] = halves[core]


def project_kernel(seq_ref, qkv_w_ref, gate_w_ref, qkv_ref, gate_ref):
    normed = normalize(seq_ref[0]).astype(BF16)
    qkv_ref[0] = mm(normed, qkv_w_ref[...]).astype(BF16)
    gate_ref[0] = jax.nn.sigmoid(mm(normed, gate_w_ref[...]))


def attend_kernel(
    heads,
    core_ref,
    seq_ref,
    keep_ref,
    qkv_ref,
    gate_ref,
    own_ref,
    other_ref,
    merge_ref,
    halves_ref,
    new_ref,
    left_ref,
    right_ref,
):
    core = core_ref[0]
    inner = gate_ref.shape[2]
    residues = gate_ref.shape[1]
    head_width = inner // heads
    half = inner // 2
    scale = head_width ** (-0.5)
    queries = qkv_ref[0, :, :inner]
    key_rows = qkv_ref[0, :, inner : 2 * inner]
    value_rows = qkv_ref[0, :, 2 * inner :]
    keep = keep_ref[0]
    masking = jnp.where(keep == 1, 0.0, -1000000000.0).astype(F32)
    lane = lax.broadcasted_iota(jnp.int32, (residues, inner), 1) // head_width
    lane_half = lax.broadcasted_iota(jnp.int32, (residues, half), 1) // head_width
    zero = jnp.zeros((), BF16)
    mixed = []
    for bias_ref, group in ((own_ref, core), (other_ref, 1 - core)):
        values = jnp.where(group == 0, value_rows[:, :half], value_rows[:, half:])
        total = jnp.zeros((residues, inner), F32)
        for h in range(heads // 2):
            head = group * (heads // 2) + h
            keys = jnp.where(lane == head, key_rows, zero)
            logits = mm(queries, keys, NT)
            logits = logits * scale + bias_ref[h].astype(F32) + masking
            top = jnp.max(logits, axis=-1, keepdims=True)
            weights = jnp.exp(logits - top).astype(BF16)
            mine = lane_half == h
            table = jnp.concatenate(
                [
                    jnp.where(mine, values, zero),
                    jnp.where(mine, jnp.ones((), BF16), zero),
                ],
                axis=1,
            )
            total = total + mm(weights, table)
        mixed.append(total[:, :half] / total[:, half:])
    first = jnp.where(core == 0, mixed[0], mixed[1])
    second = jnp.where(core == 0, mixed[1], mixed[0])
    attended = (jnp.concatenate([first, second], axis=1) * gate_ref[0]).astype(BF16)
    updated = (seq_ref[0].astype(F32) + mm(attended, merge_ref[...])).astype(BF16)
    new_ref[0] = updated
    factors = mm(halves_ref[...], normalize(updated).astype(BF16), NT)
    factors = factors * keep.astype(F32)
    width = factors.shape[0] // 2
    right_ref[0] = factors[width:].astype(BF16)
    left_ref[0] = factors[:width].T.astype(BF16)


def outer_kernel(
    seqs,
    width,
    core_ref,
    first_ref,
    marks_ref,
    own_ref,
    other_ref,
    couple_ref,
    table_ref,
    value_w_ref,
    gate_w_ref,
    observed_ref,
    pair_ref,
    edges_ref,
    right_scr,
    right_all,
    small_scr,
    keep_scr,
    edge_scr,
):
    n = own_ref.shape[0]
    rows, residues, channels = couple_ref.shape
    span = seqs * width
    half = residues // 2
    total_seqs = n * seqs
    core = core_ref[0]

    def halves(own, other):
        own, other = own.astype(F32), other.astype(F32)
        return jnp.where(core == 0, own, other), jnp.where(core == 0, other, own)

    low, high = halves(own_ref[:, :span, :], other_ref[:, :span, :])
    fill(right_scr, jnp.concatenate([low, high], axis=2).reshape(n * span, residues))
    for q in range(width):
        parts = [take(right_scr, s * width + q, n, span) for s in range(seqs)]
        right_all[q * total_seqs : (q + 1) * total_seqs, :] = jnp.concatenate(parts, axis=0).astype(
            BF16
        )
    extra = own_ref.shape[1] - span
    low, high = halves(own_ref[:, span:, :], other_ref[:, span:, :])
    fill(small_scr, own_ref[:, span:, :].astype(F32).reshape(n * extra, half))
    fill(keep_scr, jnp.concatenate([low, high], axis=2).reshape(n * extra, residues))
    left_rows = []
    for i in range(rows):
        block = take(small_scr, i, n, extra)
        for s in range(seqs):
            left_rows.append(block[:, s * width : (s + 1) * width])
    left_all = jnp.concatenate(left_rows, axis=0).astype(BF16)
    keep = jnp.concatenate(
        [take(keep_scr, rows + s, n, extra) for s in range(seqs)], axis=0
    ).astype(BF16)
    row_ids = lax.broadcasted_iota(jnp.int32, (8, residues), 0) + first_ref[0]
    chosen = (row_ids == lax.broadcasted_iota(jnp.int32, (8, residues), 1)).astype(BF16)
    own_keep = mm(chosen, keep, NT).astype(BF16)
    counts = mm(own_keep, keep)
    scale = 1.0 / jnp.maximum(counts, 1.0)
    observed = observed_ref[...].astype(F32)
    step = 2 if rows % 2 == 0 else 1
    for i0 in range(0, rows, step):
        block = left_all[i0 * total_seqs : (i0 + step) * total_seqs, :]
        projected = mm(table_ref[...], block, NT).astype(BF16)
        for i in range(i0, i0 + step):
            at = (i - i0) * total_seqs
            lhs = jnp.concatenate(
                [
                    projected[q * channels : (q + 1) * channels, at : at + total_seqs]
                    for q in range(width)
                ],
                axis=1,
            )
            update = mm(lhs, right_all[...]) * scale[i : i + 1, :]
            pair = (couple_ref[i].astype(F32) + update.T).astype(BF16)
            pair_ref[i] = pair
            normed = normalize(pair).astype(BF16)
            value = mm(value_w_ref[...], normed, NT)
            gate = mm(gate_w_ref[...], normed, NT)
            mark = observed * marks_ref[i].astype(F32)
            put(edge_scr, i, jax.nn.sigmoid(gate) * value * mark, rows)
    edges_ref[...] = take(edge_scr, 0, edges_ref.shape[0]).astype(BF16)


def close_gate_kernel(pair_ref, weight_ref, gate_ref):
    for i in range(pair_ref.shape[0]):
        normed = normalize(pair_ref[i]).astype(BF16)
        gate_ref[i] = jax.nn.sigmoid(mm(normed, weight_ref[...]))


def triangle_kernel(per, rows, in_ref, out_ref, in_scr, out_scr):
    n = in_ref.shape[0]
    residues = in_ref.shape[2]
    in_scr[...] = in_ref[...].astype(F32)
    for c in range(per):
        left = in_scr[:, c * rows : (c + 1) * rows, :].reshape(n * rows, residues).astype(BF16)
        at = (per + c) * rows
        right = in_scr[:, at : at + rows, :].reshape(n * rows, residues).astype(BF16)
        out_scr[:, c * rows : (c + 1) * rows, :] = mm(left, right, NT).reshape(n, rows, residues)
    out_ref[...] = out_scr[...].astype(BF16)


def plain_triangle_kernel(left_ref, right_ref, out_ref):
    for c in range(left_ref.shape[0]):
        out_ref[c] = mm(left_ref[c], right_ref[c], NT).astype(BF16)


def close_kernel(in_ref, pair_ref, gate_ref, weight_ref, out_ref, scr):
    rows, residues, channels = pair_ref.shape
    fill(scr, in_ref[...].astype(F32))
    for i in range(rows):
        normed = normalize(take(scr, i, channels, rows), axis=0).astype(BF16)
        update = mm(normed, weight_ref[...], TN)
        out_ref[i] = (pair_ref[i].astype(F32) + gate_ref[i] * update).astype(BF16)


def per_device(
    branch,
    dap,
    homolog_embedding,
    couple_embedding,
    homolog_present,
    observed_position,
    couple_logit_kernel,
    lookup_kernels,
    heads_sigmoid_kernel,
    heads_merge_kernel,
    tensor_halves_kernel,
    tensor_merge_kernel,
    edge_entry_kernel,
    closing_sigmoid_kernel,
    closing_merge_kernel,
):
    n = branch * dap
    rows, residues, channels = couple_embedding.shape
    seqs = homolog_embedding.shape[0]
    features = homolog_embedding.shape[2]
    heads = couple_logit_kernel.shape[1]
    inner = heads_sigmoid_kernel.shape[1]
    width = tensor_halves_kernel.shape[1] // 2
    per = channels // n
    half = residues // 2
    cores = [(t // dap) % 2 for t in range(n)]
    core = (lax.axis_index("branch") % 2).astype(jnp.int32).reshape(1)
    first_row = lax.axis_index(EVERY) * rows
    partner = [(b, b ^ 1) for b in range(branch)]

    def exchange(values):
        return lax.all_to_all(values, EVERY, split_axis=0, concat_axis=0, tiled=True)

    def swap(values):
        return lax.ppermute(values, "branch", partner)

    table = (
        tensor_merge_kernel.reshape(width, width, channels)
        .transpose(1, 2, 0)
        .reshape(width * channels, width)
    )
    entry = edge_entry_kernel.reshape(channels, 2, 2, n, per)
    value_w = entry[:, :, 0].transpose(2, 1, 3, 0).reshape(2 * channels, channels)
    gate_w = entry[:, :, 1].transpose(2, 1, 3, 0).reshape(2 * channels, channels)

    half_heads = heads // 2
    message = call(
        functools.partial(bias_kernel, cores),
        jax.ShapeDtypeStruct((n, half_heads * rows, residues), BF16),
        (couple_embedding, couple_logit_kernel.T),
        [sheets(heads * rows, residues)],
        name="bias",
    )
    own_bias = exchange(message).reshape(n, half_heads, rows, residues)
    own_bias = own_bias.transpose(1, 0, 2, 3).reshape(half_heads, residues, residues)
    other_bias = swap(own_bias)

    def whole(*shape):
        return pl.BlockSpec(shape, lambda s: (0,) * len(shape))

    def per_seq(*shape):
        return pl.BlockSpec((1, *shape), lambda s: (s,) + (0,) * len(shape))

    qkv, gates = pl.pallas_call(
        project_kernel,
        grid=(seqs,),
        out_shape=(
            jax.ShapeDtypeStruct((seqs, residues, 3 * inner), BF16),
            jax.ShapeDtypeStruct((seqs, residues, inner), F32),
        ),
        in_specs=[
            per_seq(residues, features),
            whole(features, 3 * inner),
            whole(features, inner),
        ],
        out_specs=(per_seq(residues, 3 * inner), per_seq(residues, inner)),
        name="project",
        cost_estimate=pl.CostEstimate(flops=2**29, bytes_accessed=2**22, transcendentals=0),
    )(homolog_embedding, lookup_kernels, heads_sigmoid_kernel)
    homolog_refreshed, left, right = pl.pallas_call(
        functools.partial(attend_kernel, heads),
        grid=(seqs,),
        out_shape=(
            jax.ShapeDtypeStruct((seqs, residues, features), BF16),
            jax.ShapeDtypeStruct((seqs, residues, width), BF16),
            jax.ShapeDtypeStruct((seqs, width, residues), BF16),
        ),
        in_specs=[
            sspec(),
            per_seq(residues, features),
            per_seq(1, residues),
            per_seq(residues, 3 * inner),
            per_seq(residues, inner),
            whole(half_heads, residues, residues),
            whole(half_heads, residues, residues),
            whole(inner, features),
            whole(2 * width, features),
        ],
        out_specs=(
            per_seq(residues, features),
            per_seq(residues, width),
            per_seq(width, residues),
        ),
        name="attend",
        cost_estimate=pl.CostEstimate(flops=2**31, bytes_accessed=2**22, transcendentals=0),
    )(
        core,
        homolog_embedding,
        homolog_present.reshape(seqs, 1, residues),
        qkv,
        gates,
        own_bias,
        other_bias,
        heads_merge_kernel,
        tensor_halves_kernel.T,
    )

    span = seqs * width
    right_halves = right.reshape(span, 2, half).transpose(1, 0, 2)
    keep_halves = homolog_present.astype(BF16).reshape(seqs, 2, half).transpose(1, 0, 2)
    left_part = left.reshape(seqs, n, rows, width).transpose(1, 2, 0, 3).reshape(n, rows, span)
    extra = -(-(rows + seqs) // 16) * 16
    pad = jnp.zeros((n, extra - rows - seqs, half), BF16)

    def spread(parts):
        return jnp.broadcast_to(
            parts[None, :, None], (branch // 2, 2, dap) + parts.shape[1:]
        ).reshape((n,) + parts.shape[1:])

    message = jnp.concatenate([spread(right_halves), left_part, spread(keep_halves), pad], axis=1)
    own = exchange(message)
    other = swap(own)
    pair_next, edges = call(
        functools.partial(outer_kernel, seqs, width),
        (
            jax.ShapeDtypeStruct((rows, residues, channels), BF16),
            jax.ShapeDtypeStruct((2 * channels * rows, residues), BF16),
        ),
        (
            core,
            first_row.astype(jnp.int32).reshape(1),
            lax.dynamic_slice_in_dim(observed_position, first_row, rows, 0),
            own,
            other,
            couple_embedding,
            table,
            value_w,
            gate_w,
            observed_position.reshape(1, residues),
        ),
        [
            sheets(n * span, residues),
            VMEM((width * n * seqs, residues), BF16),
            sheets(n * extra, half),
            sheets(n * extra, residues),
            sheets(2 * channels * rows, residues),
        ],
        name="outer",
        in_specs=[sspec(), sspec(), sspec()] + [vspec()] * 7,
        flops=2**31,
    )

    received = exchange(edges.reshape(n, 2 * per * rows, residues))
    gate = call(
        close_gate_kernel,
        jax.ShapeDtypeStruct((rows, residues, channels), F32),
        (pair_next, closing_sigmoid_kernel),
        name="close_gate",
        flops=2**27,
    )
    if rows % 8 == 0:
        combined = call(
            functools.partial(triangle_kernel, per, rows),
            jax.ShapeDtypeStruct((n, per * rows, residues), BF16),
            (received,),
            [
                VMEM((n, 2 * per * rows, residues), F32),
                VMEM((n, per * rows, residues), F32),
            ],
            name="triangle",
            flops=2**28,
        )
    else:
        both = received.reshape(n, 2, per, rows, residues).transpose(1, 2, 0, 3, 4)
        both = both.reshape(2, per, residues, residues)
        combined = call(
            plain_triangle_kernel,
            jax.ShapeDtypeStruct((per, residues, residues), BF16),
            (both[0], both[1]),
            name="triangle",
            flops=2**28,
        )
        combined = combined.reshape(per, n, rows, residues).transpose(1, 0, 2, 3)
        combined = combined.reshape(n, per * rows, residues)
    combined = exchange(combined).reshape(channels * rows, residues)
    pair_output = call(
        close_kernel,
        jax.ShapeDtypeStruct((rows, residues, channels), BF16),
        (combined, pair_next, gate, closing_merge_kernel),
        [sheets(channels * rows, residues)],
        name="close",
        flops=2**27,
    )
    return (homolog_refreshed, pair_output)


def solution(mesh):
    split = P(EVERY, None, None)
    in_specs = (split, split, P(EVERY, None)) + (P(),) * 10
    return jax.shard_map(
        functools.partial(per_device, mesh.shape["branch"], mesh.shape["dap"]),
        mesh=mesh,
        in_specs=in_specs,
        out_specs=(split, split),
        check_vma=False,
    )
```

```python
import functools

import jax
import jax.numpy as jnp
from jax import lax
from jax.experimental import pallas as pl
from jax.experimental.pallas import tpu as pltpu
from jax.sharding import PartitionSpec as P


EPSILON = 1e-05
EVERY = ("branch", "dap")
VMEM = pltpu.VMEM
F32 = jnp.float32
BF16 = jnp.bfloat16

NT = (((1,), (1,)), ((), ()))
TN = (((0,), (0,)), ((), ()))
NN = (((1,), (0,)), ((), ()))


def mm(a, b, dims=NN):
    return lax.dot_general(a, b, dims, preferred_element_type=F32)


def normalize(values, axis=-1):
    values = values.astype(F32)
    centred = values - jnp.mean(values, axis=axis, keepdims=True)
    spread = jnp.mean(centred * centred, axis=axis, keepdims=True)
    return centred * lax.rsqrt(spread + EPSILON)


def vspec():
    return pl.BlockSpec(memory_space=VMEM)


def sspec():
    return pl.BlockSpec(memory_space=pltpu.SMEM)


LANES = 128


def sheets(rows, columns):
    return VMEM((columns // LANES, rows, LANES), F32)


def put(scr, start, values, stride):
    for k in range(scr.shape[0]):
        part = values[:, k * LANES : (k + 1) * LANES]
        scr[k, pl.ds(start, values.shape[0], stride=stride), :] = part


def take(scr, start, count, stride=1):
    parts = [scr[k, pl.ds(start, count, stride=stride), :] for k in range(scr.shape[0])]
    return parts[0] if len(parts) == 1 else jnp.concatenate(parts, axis=1)


def fill(scr, values):
    for k in range(scr.shape[0]):
        scr[k] = values[:, k * LANES : (k + 1) * LANES]


def call(body, out, args, scratch=(), in_specs=None, flops=0, **kw):
    single = not isinstance(out, (tuple, list))
    return pl.pallas_call(
        body,
        out_shape=out,
        in_specs=in_specs or [vspec() for _ in args],
        out_specs=vspec() if single else tuple(vspec() for _ in out),
        scratch_shapes=list(scratch),
        cost_estimate=pl.CostEstimate(flops=flops, bytes_accessed=2**20, transcendentals=0),
        **kw,
    )(*args)


def sigmoid(values):
    return 0.5 * jnp.tanh(0.5 * values) + 0.5


def bias_kernel(cores, side_ref, couple_ref, weight_ref, out_ref, mine_ref, theirs_ref, scr):
    rows, residues, _ = couple_ref.shape
    heads = weight_ref.shape[0]
    half = residues // 2
    mine = pl.multiple_of(side_ref[0] * half, half)
    theirs = pl.multiple_of((1 - side_ref[0]) * half, half)
    for i in range(rows):
        normed = normalize(couple_ref[i]).astype(BF16)
        put(scr, i, mm(weight_ref[...], normed, NT), rows)
        mine_ref[i] = couple_ref[i, pl.ds(mine, half), :]
        theirs_ref[i] = couple_ref[i, pl.ds(theirs, half), :]
    part = heads // 2 * rows
    halves = [take(scr, k * part, part).astype(BF16) for k in range(2)]
    for t, core in enumerate(cores):
        out_ref[t] = halves[core]


def prepare_kernel(
    seqs, per, merge_ref, entry_ref, halves_ref, table_ref, value_ref, gate_ref, left_ref, right_ref,
    merge_scr, entry_scr, edge_scr,
):
    channels = merge_ref.shape[1]
    width = halves_ref.shape[0] // 2
    part = width // 2
    merge_scr[...] = merge_ref[...].astype(F32)
    for k in range(2):
        rows = [merge_scr[pl.ds(k * part + q, width, stride=width), :] for q in range(part)]
        table_ref[k] = jnp.concatenate(rows, axis=0).T.astype(BF16)
    for k in range(4):
        entry_scr[k * channels : (k + 1) * channels, :] = (
            entry_ref[:, k * channels : (k + 1) * channels].astype(F32).T
        )
    for kind, ref in enumerate((value_ref, gate_ref)):
        for k in range(2):
            for c in range(per):
                at = (2 * k + kind) * channels + c
                edge_scr[pl.ds(k * per + c, channels // per, stride=2 * per), :] = entry_scr[
                    pl.ds(at, channels // per, stride=per), :
                ]
        ref[...] = edge_scr[...].astype(BF16)
    left = halves_ref[:width].astype(F32).T.astype(BF16)
    for s in range(seqs):
        parts = [left if u == s else jnp.zeros_like(left) for u in range(seqs)]
        left_ref[s] = jnp.concatenate(parts, axis=1)
    right_ref[...] = halves_ref[width:]


def project_kernel(heads, seq_ref, qkv_w_ref, gate_w_ref, logit_ref, value_ref, gate_ref):
    residues = seq_ref.shape[1]
    inner = gate_w_ref.shape[1]
    head_width = inner // heads
    normed = normalize(seq_ref[0]).astype(BF16)
    projected = mm(normed, qkv_w_ref[...]).astype(BF16)
    queries = projected[:, :inner]
    key_rows = projected[:, inner : 2 * inner]
    value_ref[0] = projected[:, 2 * inner :]
    gate_ref[0] = sigmoid(mm(normed, gate_w_ref[...]))
    lane = lax.broadcasted_iota(jnp.int32, (residues, inner), 1) // head_width
    for h in range(heads):
        keys = jnp.where(lane == h, key_rows, jnp.zeros((), BF16))
        logit_ref[0, h] = mm(queries, keys, NT) * head_width ** (-0.5)


def attend_kernel(
    heads,
    places,
    core_ref,
    seq_ref,
    keep_ref,
    logit_ref,
    value_ref,
    gate_ref,
    own_ref,
    other_ref,
    merge_ref,
    left_w_ref,
    right_w_ref,
    new_ref,
    message_ref,
    left_scr,
):
    s = pl.program_id(0)
    seqs = keep_ref.shape[0]
    core = core_ref[0]
    inner = gate_ref.shape[2]
    residues = gate_ref.shape[1]
    head_width = inner // heads
    half = inner // 2
    value_rows = value_ref[0]
    keep = keep_ref[pl.ds(s, 1), :]
    masking = jnp.where(keep == 1, 0.0, -1000000000.0).astype(F32)
    lane_half = lax.broadcasted_iota(jnp.int32, (residues, half), 1) // head_width
    zero = jnp.zeros((), BF16)
    mixed = []
    for bias_ref, group in ((own_ref, core), (other_ref, 1 - core)):
        values = jnp.where(group == 0, value_rows[:, :half], value_rows[:, half:])
        total = jnp.zeros((residues, inner), F32)
        for h in range(heads // 2):
            head = group * (heads // 2) + h
            logits = logit_ref[0, head] + bias_ref[h].astype(F32) + masking
            top = jnp.max(logits, axis=-1, keepdims=True)
            weights = jnp.exp(logits - top).astype(BF16)
            mine = lane_half == h
            table = jnp.concatenate(
                [
                    jnp.where(mine, values, zero),
                    jnp.where(mine, jnp.ones((), BF16), zero),
                ],
                axis=1,
            )
            total = total + mm(weights, table)
        mixed.append(total[:, :half] / total[:, half:])
    first = jnp.where(core == 0, mixed[0], mixed[1])
    second = jnp.where(core == 0, mixed[1], mixed[0])
    attended = (jnp.concatenate([first, second], axis=1) * gate_ref[0]).astype(BF16)
    updated = (seq_ref[0].astype(F32) + mm(attended, merge_ref[...])).astype(BF16)
    new_ref[0] = updated
    normed = normalize(updated).astype(BF16)
    present = keep.astype(F32)
    width = right_w_ref.shape[0]
    part = width // 2
    columns = message_ref.shape[2]
    span = seqs * part
    right = (mm(right_w_ref[...], normed, NT) * present).astype(BF16)
    at = pl.multiple_of(s * part, part)
    for t, (core_of, side, _) in enumerate(places):
        message_ref[t, pl.ds(at, part), :] = right[
            core_of * part : (core_of + 1) * part, side * columns : (side + 1) * columns
        ]
    present_column = jnp.broadcast_to(present, (8, residues)).T[:, :1]
    left = mm(normed, left_w_ref[s]) * present_column

    @pl.when(s == 0)
    def _():
        left_scr[...] = left

    @pl.when(s > 0)
    def _():
        left_scr[...] += left

    @pl.when(s == seqs - 1)
    def _():
        rows = residues // len(places)
        marks = keep_ref[...].astype(F32)
        marks = jnp.concatenate(
            [marks[:, k * columns : (k + 1) * columns] for k in range(2)], axis=0
        ).astype(BF16)
        for t, (_, _, mate) in enumerate(places):
            block = jnp.concatenate(
                [left_scr[u * rows : (u + 1) * rows, :] for u in (t, mate)], axis=0
            )
            message_ref[t, span : span + 2 * rows, :] = block.astype(BF16)
            message_ref[t, span + 2 * rows :, :] = marks


def outer_kernel(
    seqs,
    width,
    core_ref,
    side_ref,
    first_mine_ref,
    first_theirs_ref,
    marks_ref,
    own_ref,
    other_ref,
    couple_mine_ref,
    couple_theirs_ref,
    table_ref,
    value_w_ref,
    gate_w_ref,
    observed_ref,
    pair_mine_ref,
    pair_theirs_ref,
    edges_ref,
    right_scr,
    small_scr,
    products,
    edge_scr,
):
    n = own_ref.shape[0]
    rows, columns, channels = couple_mine_ref.shape
    block = 2 * rows
    part = width // 2
    span = seqs * part
    total_seqs = n * seqs
    core, side = core_ref[0], side_ref[0]
    first_mine, first_theirs = first_mine_ref[0], first_theirs_ref[0]

    extra = own_ref.shape[1] - span
    small_scr[...] = own_ref[:, span:, :].astype(F32).reshape(n * extra, columns)
    left_rows = []
    for i in range(block):
        piece = small_scr[pl.ds(i, n, stride=extra), :]
        for s in range(seqs):
            left_rows.append(piece[:, s * width : (s + 1) * width])
    left_all = jnp.concatenate(left_rows, axis=0).T
    left = jnp.concatenate(
        [left_all[:, i * total_seqs : (i + 1) * total_seqs] for i in range(block)], axis=0
    ).astype(BF16)
    keep_halves = []
    for k in range(2):
        at = block + k * seqs
        keep_halves.append(
            jnp.concatenate(
                [small_scr[pl.ds(at + s, n, stride=extra), :] for s in range(seqs)], axis=0
            )
        )
    keep_columns = jnp.where(side == 0, keep_halves[0], keep_halves[1]).astype(BF16)
    keep = jnp.concatenate(keep_halves, axis=1).astype(BF16)
    pad = -(-block // 8) * 8
    order = lax.broadcasted_iota(jnp.int32, (pad, 2 * columns), 0)
    row_ids = jnp.where(order < rows, first_mine + order, first_theirs + order - rows)
    chosen = (row_ids == lax.broadcasted_iota(jnp.int32, (pad, 2 * columns), 1)).astype(BF16)
    counts = mm(mm(chosen, keep, NT).astype(BF16), keep_columns)
    scale = 1.0 / jnp.maximum(counts, 1.0)

    for k, ref in enumerate((own_ref, other_ref)):
        right_scr[...] = ref[:, :span, :].astype(F32).reshape(n * span, columns)
        for q in range(0, part, 2):
            pair = [
                jnp.concatenate(
                    [
                        right_scr[pl.ds(s * part + q + d, n, stride=span), :]
                        for s in range(seqs)
                    ],
                    axis=0,
                ).astype(BF16)
                for d in range(2)
            ]
            outer = mm(left, jnp.concatenate(pair, axis=1)).astype(BF16)
            for d in range(2):
                at = (k * part + q + d) * width
                for i in range(block):
                    products[i, at : at + width, :] = outer[
                        i * width : (i + 1) * width, d * columns : (d + 1) * columns
                    ]
    table = jnp.concatenate([table_ref[core], table_ref[1 - core]], axis=1)
    half = pl.multiple_of(side * columns, columns)
    observed = observed_ref[:, pl.ds(half, columns)].astype(F32)
    row_marks = [marks_ref[first_mine + r] for r in range(rows)]
    row_marks += [marks_ref[first_theirs + r] for r in range(rows)]
    for i in range(0, block, 2):
        update = mm(table, jnp.concatenate([products[i], products[i + 1]], axis=1))
        normed = []
        for d in range(2):
            piece = update[:, d * columns : (d + 1) * columns] * scale[i + d : i + d + 1, :]
            couple_ref, pair_ref = (
                (couple_mine_ref, pair_mine_ref)
                if i + d < rows
                else (couple_theirs_ref, pair_theirs_ref)
            )
            r = (i + d) % rows
            pair = (couple_ref[r].astype(F32) + piece.T).astype(BF16)
            pair_ref[r] = pair
            normed.append(normalize(pair).astype(BF16))
        normed = jnp.concatenate(normed, axis=0)
        edge = mm(value_w_ref[...], normed, NT) * sigmoid(mm(gate_w_ref[...], normed, NT))
        for d in range(2):
            mark = observed * row_marks[i + d].astype(F32)
            edge_scr[pl.ds(i + d, 2 * channels, stride=block), :] = (
                edge[:, d * columns : (d + 1) * columns] * mark
            )
    edges_ref[...] = edge_scr[...].astype(BF16)


def close_gate_kernel(mine_ref, theirs_ref, weight_ref, mine_gate_ref, theirs_gate_ref):
    for pair_ref, gate_ref in ((mine_ref, mine_gate_ref), (theirs_ref, theirs_gate_ref)):
        for i in range(pair_ref.shape[0]):
            normed = normalize(pair_ref[i]).astype(BF16)
            gate_ref[i] = sigmoid(mm(normed, weight_ref[...]))


def triangle_kernel(per, rows, places, in_ref, out_ref, in_scr, out_scr):
    n = in_ref.shape[0]
    residues = n * rows
    in_scr[...] = in_ref[...].astype(F32)

    def whole(at):
        tiles = []
        for t, (_, side, mate) in enumerate(places):
            pair = []
            for k in range(2):
                source, shift = (t, 0) if side == k else (mate, rows)
                pair.append(in_scr[source, at + shift : at + shift + rows, :])
            tiles.append(jnp.concatenate(pair, axis=1))
        return jnp.concatenate(tiles, axis=0).astype(BF16)

    for c in range(per):
        left = whole(c * 2 * rows)
        right = whole((per + c) * 2 * rows)
        out_scr[:, c * rows : (c + 1) * rows, :] = mm(left, right, NT).reshape(n, rows, residues)
    out_ref[...] = out_scr[...].astype(BF16)


def plain_triangle_kernel(left_ref, right_ref, out_ref):
    for c in range(left_ref.shape[0]):
        out_ref[c] = mm(left_ref[c], right_ref[c], NT).astype(BF16)


def close_kernel(
    side_ref, in_ref, mine_ref, theirs_ref, mine_gate_ref, theirs_gate_ref, weight_ref, out_ref, scr
):
    rows, columns, channels = mine_ref.shape
    fill(scr, in_ref[...].astype(F32))
    side = side_ref[0]
    for half, pair_ref, gate_ref in (
        (side, mine_ref, mine_gate_ref),
        (1 - side, theirs_ref, theirs_gate_ref),
    ):
        at = pl.multiple_of(half * columns, columns)
        for i in range(rows):
            piece = scr[half, pl.ds(i, channels, stride=rows), :]
            update = mm(normalize(piece, axis=0).astype(BF16), weight_ref[...], TN)
            out_ref[i, pl.ds(at, columns), :] = (
                pair_ref[i].astype(F32) + gate_ref[i] * update
            ).astype(BF16)


def per_device(
    branch,
    dap,
    homolog_embedding,
    couple_embedding,
    homolog_present,
    observed_position,
    couple_logit_kernel,
    lookup_kernels,
    heads_sigmoid_kernel,
    heads_merge_kernel,
    tensor_halves_kernel,
    tensor_merge_kernel,
    edge_entry_kernel,
    closing_sigmoid_kernel,
    closing_merge_kernel,
):
    n = branch * dap
    rows, residues, channels = couple_embedding.shape
    seqs = homolog_embedding.shape[0]
    features = homolog_embedding.shape[2]
    heads = couple_logit_kernel.shape[1]
    inner = heads_sigmoid_kernel.shape[1]
    width = tensor_halves_kernel.shape[1] // 2
    per = channels // n
    half = residues // 2
    block = 2 * rows
    places = [((t // dap) % 2, (t // dap // 2) % 2, (t // dap ^ 2) * dap + t % dap) for t in range(n)]
    me = lax.axis_index("branch").astype(jnp.int32)
    core = (me % 2).reshape(1)
    side = (me // 2 % 2).reshape(1)
    place = lax.axis_index("dap").astype(jnp.int32)
    first_mine = (me * dap + place) * rows
    first_theirs = ((me ^ 2) * dap + place) * rows
    chip = [(b, b ^ 1) for b in range(branch)]
    across = [(b, b ^ 2) for b in range(branch)]

    def exchange(values):
        return lax.all_to_all(values, EVERY, split_axis=0, concat_axis=0, tiled=True)

    def permute(values, pairs):
        return lax.ppermute(values, "branch", pairs)

    table, value_w, gate_w, left_w, right_w = call(
        functools.partial(prepare_kernel, seqs, per),
        (
            jax.ShapeDtypeStruct((2, channels, width // 2 * width), BF16),
            jax.ShapeDtypeStruct((2 * channels, channels), BF16),
            jax.ShapeDtypeStruct((2 * channels, channels), BF16),
            jax.ShapeDtypeStruct((seqs, features, seqs * width), BF16),
            jax.ShapeDtypeStruct((width, features), BF16),
        ),
        (tensor_merge_kernel, edge_entry_kernel, tensor_halves_kernel.T),
        [
            VMEM((width * width, channels), F32),
            VMEM((4 * channels, channels), F32),
            VMEM((2 * channels, channels), F32),
        ],
    )

    half_heads = heads // 2
    message, couple_mine, couple_send = call(
        functools.partial(bias_kernel, [place[0] for place in places]),
        (
            jax.ShapeDtypeStruct((n, half_heads * rows, residues), BF16),
            jax.ShapeDtypeStruct((rows, half, channels), BF16),
            jax.ShapeDtypeStruct((rows, half, channels), BF16),
        ),
        (side, couple_embedding, couple_logit_kernel.T),
        [sheets(heads * rows, residues)],
        in_specs=[sspec(), vspec(), vspec()],
    )
    own_bias = exchange(message).reshape(n, half_heads, rows, residues)
    own_bias = own_bias.transpose(1, 0, 2, 3).reshape(half_heads, residues, residues)
    other_bias = permute(own_bias, chip)
    couple_theirs = permute(couple_send, across)

    def whole(*shape):
        return pl.BlockSpec(shape, lambda s: (0,) * len(shape))

    def per_seq(*shape):
        return pl.BlockSpec((1, *shape), lambda s: (s,) + (0,) * len(shape))

    logits, values, gates = pl.pallas_call(
        functools.partial(project_kernel, heads),
        grid=(seqs,),
        out_shape=(
            jax.ShapeDtypeStruct((seqs, heads, residues, residues), F32),
            jax.ShapeDtypeStruct((seqs, residues, inner), BF16),
            jax.ShapeDtypeStruct((seqs, residues, inner), F32),
        ),
        in_specs=[per_seq(residues, features), whole(features, 3 * inner), whole(features, inner)],
        out_specs=(
            per_seq(heads, residues, residues),
            per_seq(residues, inner),
            per_seq(residues, inner),
        ),
        name="project",
        cost_estimate=pl.CostEstimate(flops=2**29, bytes_accessed=2**22, transcendentals=0),
    )(homolog_embedding, lookup_kernels, heads_sigmoid_kernel)
    span = seqs * width // 2
    depth = span + block + 2 * seqs
    homolog_refreshed, message = pl.pallas_call(
        functools.partial(attend_kernel, heads, places),
        grid=(seqs,),
        out_shape=(
            jax.ShapeDtypeStruct((seqs, residues, features), BF16),
            jax.ShapeDtypeStruct((n, depth, half), BF16),
        ),
        in_specs=[
            sspec(),
            per_seq(residues, features),
            whole(seqs, residues),
            per_seq(heads, residues, residues),
            per_seq(residues, inner),
            per_seq(residues, inner),
            whole(half_heads, residues, residues),
            whole(half_heads, residues, residues),
            whole(inner, features),
            whole(seqs, features, seqs * width),
            whole(width, features),
        ],
        out_specs=(per_seq(residues, features), whole(n, depth, half)),
        scratch_shapes=[VMEM((residues, seqs * width), F32)],
        name="attend",
        cost_estimate=pl.CostEstimate(flops=2**31, bytes_accessed=2**22, transcendentals=0),
    )(
        core,
        homolog_embedding,
        homolog_present,
        logits,
        values,
        gates,
        own_bias,
        other_bias,
        heads_merge_kernel,
        left_w,
        right_w,
    )

    own = exchange(message)
    other = permute(own, chip)
    piece = jax.ShapeDtypeStruct((rows, half, channels), BF16)
    pair_mine, pair_send, edges = call(
        functools.partial(outer_kernel, seqs, width),
        (piece, piece, jax.ShapeDtypeStruct((2 * channels * block, half), BF16)),
        (
            core,
            side,
            first_mine.reshape(1),
            first_theirs.reshape(1),
            observed_position,
            own,
            other,
            couple_mine,
            couple_theirs,
            table,
            value_w,
            gate_w,
            observed_position.reshape(1, residues),
        ),
        [
            VMEM((n * span, half), F32),
            VMEM((n * (depth - span), half), F32),
            VMEM((block, width * width, half), BF16),
            VMEM((2 * channels * block, half), F32),
        ],
        in_specs=[sspec()] * 5 + [vspec()] * 8,
        flops=2**31,
    )

    received = exchange(edges.reshape(n, 2 * per * block, half))
    pair_theirs = permute(pair_send, across)
    gate_piece = jax.ShapeDtypeStruct((rows, half, channels), F32)
    gate_mine, gate_theirs = call(
        close_gate_kernel,
        (gate_piece, gate_piece),
        (pair_mine, pair_theirs, closing_sigmoid_kernel),
        flops=2**27,
    )
    if rows % 8 == 0:
        combined = call(
            functools.partial(triangle_kernel, per, rows, places),
            jax.ShapeDtypeStruct((n, per * rows, residues), BF16),
            (received,),
            [
                VMEM((n, 2 * per * block, half), F32),
                VMEM((n, per * rows, residues), F32),
            ],
            flops=2**28,
        )
    else:
        both = received.reshape(branch // 4, 2, 2, dap, 2, per, 2, rows, half)
        both = jnp.stack([both[:, 0], both[:, 1, :, :, :, :, ::-1]], axis=1)
        both = both.transpose(4, 5, 0, 6, 2, 3, 7, 1, 8).reshape(2, per, residues, residues)
        combined = call(
            plain_triangle_kernel,
            jax.ShapeDtypeStruct((per, residues, residues), BF16),
            (both[0], both[1]),
            flops=2**28,
        )
        combined = combined.reshape(per, n, rows, residues).transpose(1, 0, 2, 3)
        combined = combined.reshape(n, per * rows, residues)
    combined = exchange(combined).reshape(channels * rows, residues)
    pair_output = call(
        close_kernel,
        jax.ShapeDtypeStruct((rows, residues, channels), BF16),
        (side, combined, pair_mine, pair_theirs, gate_mine, gate_theirs, closing_merge_kernel),
        [sheets(channels * rows, residues)],
        in_specs=[sspec()] + [vspec()] * 6,
        flops=2**27,
    )
    return (homolog_refreshed, pair_output)


def solution(mesh):
    split = P(EVERY, None, None)
    in_specs = (split, split, P(EVERY, None)) + (P(),) * 10

    def body(*args):
        return per_device(mesh.shape["branch"], mesh.shape["dap"], *args)

    return jax.shard_map(
        body, mesh=mesh, in_specs=in_specs, out_specs=(split, split), check_vma=False
    )
```

```python
import functools
import math

import jax
import jax.numpy as jnp
from jax import lax
from jax.experimental import pallas as pl
from jax.experimental.pallas import tpu as pltpu
from jax.sharding import PartitionSpec as P


EPSILON = 1e-05
EVERY = ("branch", "dap")
VMEM = pltpu.VMEM
F32 = jnp.float32
BF16 = jnp.bfloat16

NT = (((1,), (1,)), ((), ()))
TN = (((0,), (0,)), ((), ()))
NN = (((1,), (0,)), ((), ()))


def mm(a, b, dims=NN):
    return lax.dot_general(a, b, dims, preferred_element_type=F32)


def normalize(values, axis=-1):
    values = values.astype(F32)
    centred = values - jnp.mean(values, axis=axis, keepdims=True)
    spread = jnp.mean(centred * centred, axis=axis, keepdims=True)
    return centred * lax.rsqrt(spread + EPSILON)


def vspec():
    return pl.BlockSpec(memory_space=VMEM)


def sspec():
    return pl.BlockSpec(memory_space=pltpu.SMEM)


LANES = 128


def room(mebibytes):
    return pltpu.CompilerParams(vmem_limit_bytes=mebibytes * 2**20)


def sheets(rows, columns):
    return VMEM((columns // LANES, rows, LANES), F32)


def put(scr, start, values, stride):
    for k in range(scr.shape[0]):
        part = values[:, k * LANES : (k + 1) * LANES]
        scr[k, pl.ds(start, values.shape[0], stride=stride), :] = part


def take(scr, start, count, stride=1):
    parts = [scr[k, pl.ds(start, count, stride=stride), :] for k in range(scr.shape[0])]
    return parts[0] if len(parts) == 1 else jnp.concatenate(parts, axis=1)


def fill(scr, values):
    for k in range(scr.shape[0]):
        scr[k] = values[:, k * LANES : (k + 1) * LANES]


def stay(values):
    return pltpu.with_memory_space_constraint(values, pltpu.MemorySpace.HBM)


def call(body, out, args, scratch=(), in_specs=None, flops=0, need=8, **kw):
    single = not isinstance(out, (tuple, list))
    return pl.pallas_call(
        body,
        out_shape=out,
        in_specs=in_specs or [vspec() for _ in args],
        out_specs=vspec() if single else tuple(vspec() for _ in out),
        scratch_shapes=list(scratch),
        cost_estimate=pl.CostEstimate(flops=flops, bytes_accessed=2**20, transcendentals=0),
        compiler_params=room(need),
        **kw,
    )(*args)


def sigmoid(values):
    return 0.5 * jnp.tanh(0.5 * values) + 0.5


def bias_kernel(cores, side_ref, couple_ref, weight_ref, out_ref, mine_ref, theirs_ref, scr):
    rows, residues, _ = couple_ref.shape
    heads = weight_ref.shape[0]
    half = residues // 2
    mine = pl.multiple_of(side_ref[0] * half, half)
    theirs = pl.multiple_of((1 - side_ref[0]) * half, half)
    for i in range(rows):
        normed = normalize(couple_ref[i]).astype(BF16)
        put(scr, i, mm(weight_ref[...], normed, NT), rows)
        mine_ref[i] = couple_ref[i, pl.ds(mine, half), :]
        theirs_ref[i] = couple_ref[i, pl.ds(theirs, half), :]
    part = heads // 2 * rows
    halves = [take(scr, k * part, part).astype(BF16) for k in range(2)]
    for t, core in enumerate(cores):
        out_ref[t] = halves[core]


def prepare_small_kernel(seqs, halves_ref, left_ref, right_ref):
    width = halves_ref.shape[0] // 2
    left = halves_ref[:width].astype(F32).T.astype(BF16)
    for s in range(seqs):
        parts = [left if u == s else jnp.zeros_like(left) for u in range(seqs)]
        left_ref[s] = jnp.concatenate(parts, axis=1)
    right_ref[...] = halves_ref[width:]


def prepare_large_kernel(
    chunks,
    per,
    merge_ref,
    entry_ref,
    close_ref,
    table_ref,
    value_ref,
    gate_ref,
    final_ref,
    merge_scr,
    entry_scr,
    edge_scr,
):
    channels = merge_ref.shape[1]
    width = math.isqrt(merge_ref.shape[0])
    part = width // 2
    merge_scr[...] = merge_ref[...].astype(F32)
    for k in range(2):
        rows = [merge_scr[pl.ds(k * part + q, width, stride=width), :] for q in range(part)]
        table_ref[k] = jnp.concatenate(rows, axis=0).T.astype(BF16)
    for k in range(4):
        entry_scr[k * channels : (k + 1) * channels, :] = (
            entry_ref[:, k * channels : (k + 1) * channels].astype(F32).T
        )
    some = per // chunks
    n = channels // per
    for kind, ref in enumerate((value_ref, gate_ref)):
        for k in range(2):
            for c in range(per):
                source = (2 * k + kind) * channels + c
                at = c // some * n * 2 * some + k * some + c % some
                edge_scr[pl.ds(at, n, stride=2 * some), :] = entry_scr[
                    pl.ds(source, n, stride=per), :
                ]
        ref[...] = edge_scr[...].astype(BF16)
    entry_scr[:channels, :] = close_ref[...].astype(F32)
    for c in range(per):
        at = c // some * n * some + c % some
        edge_scr[pl.ds(at, n, stride=some), :] = entry_scr[pl.ds(c, n, stride=per), :]
    final_ref[...] = edge_scr[:channels, :].astype(BF16)


def project_kernel(seq_ref, qkv_w_ref, gate_w_ref, query_ref, key_ref, value_ref, gate_ref):
    inner = gate_w_ref.shape[1]
    normed = normalize(seq_ref[0]).astype(BF16)
    projected = mm(normed, qkv_w_ref[...])
    query_ref[0] = projected[:, :inner].astype(BF16)
    key_ref[0] = projected[:, inner : 2 * inner].T.astype(BF16)
    value_ref[0] = projected[:, 2 * inner :].astype(BF16)
    gate_ref[0] = sigmoid(mm(normed, gate_w_ref[...]))


def attend_kernel(
    heads,
    places,
    raw,
    core_ref,
    seq_ref,
    keep_ref,
    query_ref,
    key_ref,
    value_ref,
    gate_ref,
    own_ref,
    other_ref,
    merge_ref,
    left_w_ref,
    right_w_ref,
    new_ref,
    message_ref,
    left_scr,
    bias_scr,
    ones_scr,
):
    step = pl.program_id(0)
    batch = seq_ref.shape[0]
    seqs = keep_ref.shape[0]
    core = core_ref[0]
    inner = gate_ref.shape[2]
    residues = gate_ref.shape[1]
    half = inner // 2
    head_width = inner // heads
    scale = head_width ** (-0.5)
    some_heads = heads // 2
    zero = jnp.zeros((), BF16)
    blank = jnp.zeros((head_width, residues), BF16)
    lane_half = lax.broadcasted_iota(jnp.int32, (residues, half), 1) // head_width

    @pl.when(step == 0)
    def _():
        left_scr[...] = jnp.zeros_like(left_scr)
        for h in range(some_heads):
            ones_scr[h * residues : (h + 1) * residues, :] = jnp.where(
                lane_half == h, jnp.ones((), BF16), zero
            )
        for k, ref in enumerate((own_ref, other_ref)):
            for h in range(some_heads):
                if raw:
                    rows = residues // len(places)
                    tile = ref[:, h * rows : (h + 1) * rows, :].astype(F32)
                    tile = tile.reshape(residues, residues)
                else:
                    tile = ref[h].astype(F32)
                bias_scr[k * some_heads + h] = tile

    width = right_w_ref.shape[0]
    part = width // 2
    columns = message_ref.shape[2]
    span = seqs * part
    for u in range(batch):
        s = step * batch + u
        keep = keep_ref[pl.ds(s, 1), :]
        present = keep.astype(F32)
        masking = jnp.where(keep == 1, 0.0, -1000000000.0).astype(F32)
        mixed = []
        for k, group in ((0, core), (1, 1 - core)):
            queries, values = (
                jnp.where(group == 0, ref[u, :, :half], ref[u, :, half:])
                for ref in (query_ref, value_ref)
            )
            keys = jnp.where(group == 0, key_ref[u, :half, :], key_ref[u, half:, :])
            weights, tables = [], []
            for h in range(some_heads):
                only = [
                    keys[g * head_width : (g + 1) * head_width] if g == h else blank
                    for g in range(some_heads)
                ]
                logits = mm(queries, jnp.concatenate(only, axis=0)) * scale
                logits = logits + bias_scr[k * some_heads + h] + masking
                logits = logits - jnp.max(logits, axis=-1, keepdims=True)
                weights.append(jnp.exp(logits).astype(BF16))
                tables.append(jnp.where(lane_half == h, values, zero))
            table = jnp.concatenate([jnp.concatenate(tables, axis=0), ones_scr[...]], axis=1)
            total = mm(jnp.concatenate(weights, axis=1), table)
            mixed.append(total[:, :half] / total[:, half:])
        first = jnp.where(core == 0, mixed[0], mixed[1])
        second = jnp.where(core == 0, mixed[1], mixed[0])
        attended = (jnp.concatenate([first, second], axis=1) * gate_ref[u]).astype(BF16)
        updated = (seq_ref[u].astype(F32) + mm(attended, merge_ref[...])).astype(BF16)
        new_ref[u] = updated
        normed = normalize(updated).astype(BF16)
        right = (mm(right_w_ref[...], normed, NT) * present).astype(BF16)
        at = pl.multiple_of(s * part, part)
        for t, (core_of, side, _) in enumerate(places):
            message_ref[t, pl.ds(at, part), :] = right[
                core_of * part : (core_of + 1) * part, side * columns : (side + 1) * columns
            ]
        present_column = jnp.broadcast_to(present, (8, residues)).T[:, :1]
        left_scr[...] += mm(normed, left_w_ref[s]) * present_column

    @pl.when(step == pl.num_programs(0) - 1)
    def _():
        rows = residues // len(places)
        marks = keep_ref[...].astype(F32)
        marks = jnp.concatenate(
            [marks[:, k * columns : (k + 1) * columns] for k in range(2)], axis=0
        ).astype(BF16)
        for t, (_, _, mate) in enumerate(places):
            block = jnp.concatenate(
                [left_scr[u * rows : (u + 1) * rows, :] for u in (t, mate)], axis=0
            )
            message_ref[t, span : span + 2 * rows, :] = block.astype(BF16)
            message_ref[t, span + 2 * rows :, :] = marks


def multiply(seqs, width, left, ref, scr, products):
    n, _, columns = ref.shape
    part = width // 2
    span = seqs * part
    block = left.shape[0] // width
    scr[...] = ref[:, :span, :].astype(F32).reshape(n * span, columns)
    for q in range(0, part, 2):
        pair = [
            jnp.concatenate(
                [scr[pl.ds(s * part + q + d, n, stride=span), :] for s in range(seqs)], axis=0
            ).astype(BF16)
            for d in range(2)
        ]
        outer = mm(left, jnp.concatenate(pair, axis=1)).astype(BF16)
        for d in range(2):
            at = (q + d) * width
            for i in range(block):
                products[i, at : at + width, :] = outer[
                    i * width : (i + 1) * width, d * columns : (d + 1) * columns
                ]


def outer_own_kernel(
    seqs,
    width,
    rows,
    side_ref,
    first_mine_ref,
    first_theirs_ref,
    own_ref,
    left_ref,
    scale_ref,
    products_ref,
    right_scr,
    small_scr,
):
    n, depth, columns = own_ref.shape
    block = 2 * rows
    total_seqs = n * seqs
    span = seqs * width // 2
    side, first_mine, first_theirs = side_ref[0], first_mine_ref[0], first_theirs_ref[0]
    extra = depth - span
    small_scr[...] = own_ref[:, span:, :].astype(F32).reshape(n * extra, columns)
    left_rows = []
    for i in range(block):
        piece = small_scr[pl.ds(i, n, stride=extra), :]
        for s in range(seqs):
            left_rows.append(piece[:, s * width : (s + 1) * width])
    left_all = jnp.concatenate(left_rows, axis=0).T
    left = jnp.concatenate(
        [left_all[:, i * total_seqs : (i + 1) * total_seqs] for i in range(block)], axis=0
    ).astype(BF16)
    left_ref[...] = left
    keep_halves = []
    for k in range(2):
        at = block + k * seqs
        keep_halves.append(
            jnp.concatenate(
                [small_scr[pl.ds(at + s, n, stride=extra), :] for s in range(seqs)], axis=0
            )
        )
    keep_columns = jnp.where(side == 0, keep_halves[0], keep_halves[1]).astype(BF16)
    keep = jnp.concatenate(keep_halves, axis=1).astype(BF16)
    pad = scale_ref.shape[0]
    order = lax.broadcasted_iota(jnp.int32, (pad, 2 * columns), 0)
    row_ids = jnp.where(order < rows, first_mine + order, first_theirs + order - rows)
    chosen = (row_ids == lax.broadcasted_iota(jnp.int32, (pad, 2 * columns), 1)).astype(BF16)
    counts = mm(mm(chosen, keep, NT).astype(BF16), keep_columns)
    scale_ref[...] = 1.0 / jnp.maximum(counts, 1.0)
    multiply(seqs, width, left, own_ref, right_scr, products_ref)


def outer_kernel(
    seqs,
    width,
    core_ref,
    side_ref,
    first_mine_ref,
    first_theirs_ref,
    marks_ref,
    other_ref,
    left_ref,
    scale_ref,
    own_products_ref,
    couple_mine_ref,
    couple_theirs_ref,
    table_ref,
    value_w_ref,
    gate_w_ref,
    observed_ref,
    pair_mine_ref,
    pair_theirs_ref,
    *rest,
):
    edges_refs, (right_scr, products, edge_scr) = rest[:-3], rest[-3:]
    rows, columns, channels = couple_mine_ref.shape
    block = 2 * rows
    core, side = core_ref[0], side_ref[0]
    first_mine, first_theirs = first_mine_ref[0], first_theirs_ref[0]
    multiply(seqs, width, left_ref[...], other_ref, right_scr, products)
    scale = scale_ref[...]
    tables = ((table_ref[core], own_products_ref), (table_ref[1 - core], products))
    half = pl.multiple_of(side * columns, columns)
    observed = observed_ref[:, pl.ds(half, columns)].astype(F32)
    row_marks = [marks_ref[first_mine + r] for r in range(rows)]
    row_marks += [marks_ref[first_theirs + r] for r in range(rows)]
    for i in range(0, block, 2):
        update = sum(
            mm(table, jnp.concatenate([values[i], values[i + 1]], axis=1))
            for table, values in tables
        )
        normed = []
        for d in range(2):
            piece = update[:, d * columns : (d + 1) * columns] * scale[i + d : i + d + 1, :]
            couple_ref, pair_ref = (
                (couple_mine_ref, pair_mine_ref)
                if i + d < rows
                else (couple_theirs_ref, pair_theirs_ref)
            )
            r = (i + d) % rows
            pair = (couple_ref[r].astype(F32) + piece.T).astype(BF16)
            pair_ref[r] = pair
            normed.append(normalize(pair).astype(BF16))
        normed = jnp.concatenate(normed, axis=0)
        edge = mm(value_w_ref[...], normed, NT) * sigmoid(mm(gate_w_ref[...], normed, NT))
        for d in range(2):
            mark = observed * row_marks[i + d].astype(F32)
            edge_scr[pl.ds(i + d, 2 * channels, stride=block), :] = (
                edge[:, d * columns : (d + 1) * columns] * mark
            )
    size = edges_refs[0].shape[0]
    for k, ref in enumerate(edges_refs):
        ref[...] = edge_scr[k * size : (k + 1) * size, :].astype(BF16)


def close_gate_kernel(mine_ref, theirs_ref, weight_ref, mine_gate_ref, theirs_gate_ref):
    for pair_ref, gate_ref in ((mine_ref, mine_gate_ref), (theirs_ref, theirs_gate_ref)):
        for i in range(pair_ref.shape[0]):
            normed = normalize(pair_ref[i]).astype(BF16)
            gate_ref[i] = sigmoid(mm(normed, weight_ref[...]))


def triangle_kernel(per, rows, places, in_ref, out_ref, in_scr, out_scr):
    n = in_ref.shape[0]
    residues = n * rows
    in_scr[...] = in_ref[...].astype(F32)

    def whole(at):
        tiles = []
        for t, (_, side, mate) in enumerate(places):
            pair = []
            for k in range(2):
                source, shift = (t, 0) if side == k else (mate, rows)
                pair.append(in_scr[source, at + shift : at + shift + rows, :])
            tiles.append(jnp.concatenate(pair, axis=1))
        return jnp.concatenate(tiles, axis=0).astype(BF16)

    for c in range(per):
        left = whole(c * 2 * rows)
        right = whole((per + c) * 2 * rows)
        out_scr[:, c * rows : (c + 1) * rows, :] = mm(left, right, NT).reshape(n, rows, residues)
    out_ref[...] = out_scr[...].astype(BF16)


def plain_triangle_kernel(left_ref, right_ref, out_ref):
    for c in range(left_ref.shape[0]):
        out_ref[c] = mm(left_ref[c], right_ref[c], NT).astype(BF16)


def close_kernel(
    side_ref, mine_ref, theirs_ref, mine_gate_ref, theirs_gate_ref, weight_ref, *rest
):
    count = (len(rest) - 1) // 2
    in_refs, out_ref, scrs = rest[:count], rest[count], rest[count + 1 :]
    rows, columns, channels = mine_ref.shape
    for ref, scr in zip(in_refs, scrs):
        fill(scr, ref[...].astype(F32))
    side = side_ref[0]
    for half, pair_ref, gate_ref in (
        (side, mine_ref, mine_gate_ref),
        (1 - side, theirs_ref, theirs_gate_ref),
    ):
        at = pl.multiple_of(half * columns, columns)
        for i in range(rows):
            piece = [scr[half, pl.ds(i, channels // count, stride=rows), :] for scr in scrs]
            piece = jnp.concatenate(piece, axis=0)
            update = mm(normalize(piece, axis=0).astype(BF16), weight_ref[...], TN)
            out_ref[i, pl.ds(at, columns), :] = (
                pair_ref[i].astype(F32) + gate_ref[i] * update
            ).astype(BF16)


def per_device(
    branch,
    dap,
    homolog_embedding,
    couple_embedding,
    homolog_present,
    observed_position,
    couple_logit_kernel,
    lookup_kernels,
    heads_sigmoid_kernel,
    heads_merge_kernel,
    tensor_halves_kernel,
    tensor_merge_kernel,
    edge_entry_kernel,
    closing_sigmoid_kernel,
    closing_merge_kernel,
):
    n = branch * dap
    rows, residues, channels = couple_embedding.shape
    seqs = homolog_embedding.shape[0]
    features = homolog_embedding.shape[2]
    heads = couple_logit_kernel.shape[1]
    inner = heads_sigmoid_kernel.shape[1]
    width = tensor_halves_kernel.shape[1] // 2
    per = channels // n
    half = residues // 2
    block = 2 * rows

    chunks = 1
    some = per // chunks
    places = [((t // dap) % 2, (t // dap // 2) % 2, (t // dap ^ 2) * dap + t % dap) for t in range(n)]
    me = lax.axis_index("branch").astype(jnp.int32)
    core = (me % 2).reshape(1)
    side = (me // 2 % 2).reshape(1)
    place = lax.axis_index("dap").astype(jnp.int32)
    first_mine = (me * dap + place) * rows
    first_theirs = ((me ^ 2) * dap + place) * rows
    chip = [(b, b ^ 1) for b in range(branch)]
    across = [(b, b ^ 2) for b in range(branch)]

    def exchange(values):
        return lax.all_to_all(values, EVERY, split_axis=0, concat_axis=0, tiled=True)

    def permute(values, pairs):
        return lax.ppermute(values, "branch", pairs)

    left_w, right_w = call(
        functools.partial(prepare_small_kernel, seqs),
        (
            jax.ShapeDtypeStruct((seqs, features, seqs * width), BF16),
            jax.ShapeDtypeStruct((width, features), BF16),
        ),
        (tensor_halves_kernel.T,),
    )
    table, value_w, gate_w, final_w = call(
        functools.partial(prepare_large_kernel, chunks, per),
        (
            jax.ShapeDtypeStruct((2, channels, width // 2 * width), BF16),
            jax.ShapeDtypeStruct((2 * channels, channels), BF16),
            jax.ShapeDtypeStruct((2 * channels, channels), BF16),
            jax.ShapeDtypeStruct((channels, channels), BF16),
        ),
        (tensor_merge_kernel, edge_entry_kernel, closing_merge_kernel),
        [
            VMEM((width * width, channels), F32),
            VMEM((4 * channels, channels), F32),
            VMEM((2 * channels, channels), F32),
        ],
    )

    half_heads = heads // 2
    message, couple_mine, couple_send = call(
        functools.partial(bias_kernel, [place[0] for place in places]),
        (
            jax.ShapeDtypeStruct((n, half_heads * rows, residues), BF16),
            jax.ShapeDtypeStruct((rows, half, channels), BF16),
            jax.ShapeDtypeStruct((rows, half, channels), BF16),
        ),
        (side, stay(couple_embedding), stay(couple_logit_kernel.T)),
        [sheets(heads * rows, residues)],
        in_specs=[sspec(), vspec(), vspec()],
    )
    own_bias = exchange(message)
    raw = rows % 8 == 0
    if not raw:
        own_bias = own_bias.reshape(n, half_heads, rows, residues)
        own_bias = own_bias.transpose(1, 0, 2, 3).reshape(half_heads, residues, residues)
    other_bias = permute(own_bias, chip)
    couple_theirs = permute(couple_send, across)

    def whole(*shape):
        return pl.BlockSpec(shape, lambda s: (0,) * len(shape))

    def per_seq(batch, *shape):
        return pl.BlockSpec((batch, *shape), lambda s: (s,) + (0,) * len(shape))

    *parts, gates = pl.pallas_call(
        project_kernel,
        grid=(seqs,),
        out_shape=(
            jax.ShapeDtypeStruct((seqs, residues, inner), BF16),
            jax.ShapeDtypeStruct((seqs, inner, residues), BF16),
            jax.ShapeDtypeStruct((seqs, residues, inner), BF16),
            jax.ShapeDtypeStruct((seqs, residues, inner), F32),
        ),
        in_specs=[
            per_seq(1, residues, features),
            whole(features, 3 * inner),
            whole(features, inner),
        ],
        out_specs=(
            per_seq(1, residues, inner),
            per_seq(1, inner, residues),
            per_seq(1, residues, inner),
            per_seq(1, residues, inner),
        ),
        name="project",
        compiler_params=room(16),
        cost_estimate=pl.CostEstimate(flops=2**29, bytes_accessed=2**22, transcendentals=0),
    )(stay(homolog_embedding), stay(lookup_kernels), stay(heads_sigmoid_kernel))
    span = seqs * width // 2
    depth = span + block + 2 * seqs
    batch = 2 if seqs % 2 == 0 else 1
    homolog_refreshed, message = pl.pallas_call(
        functools.partial(attend_kernel, heads, places, raw),
        grid=(seqs // batch,),
        out_shape=(
            jax.ShapeDtypeStruct((seqs, residues, features), BF16),
            jax.ShapeDtypeStruct((n, depth, half), BF16),
        ),
        in_specs=[
            sspec(),
            per_seq(batch, residues, features),
            whole(seqs, residues),
            per_seq(batch, residues, inner),
            per_seq(batch, inner, residues),
            per_seq(batch, residues, inner),
            per_seq(batch, residues, inner),
            whole(*own_bias.shape),
            whole(*own_bias.shape),
            whole(inner, features),
            whole(seqs, features, seqs * width),
            whole(width, features),
        ],
        out_specs=(per_seq(batch, residues, features), whole(n, depth, half)),
        scratch_shapes=[
            VMEM((residues, seqs * width), F32),
            VMEM((heads, residues, residues), F32),
            VMEM((half_heads * residues, half), BF16),
        ],
        name="attend",
        compiler_params=room(24),
        cost_estimate=pl.CostEstimate(flops=2**31, bytes_accessed=2**22, transcendentals=0),
    )(
        core,
        stay(homolog_embedding),
        stay(homolog_present),
        *(stay(values) for values in parts),
        stay(gates),
        own_bias,
        other_bias,
        stay(heads_merge_kernel),
        left_w,
        right_w,
    )

    own = exchange(message)
    other = permute(own, chip)
    firsts = (first_mine.reshape(1), first_theirs.reshape(1))
    left, scale, products = call(
        functools.partial(outer_own_kernel, seqs, width, rows),
        (
            jax.ShapeDtypeStruct((block * width, n * seqs), BF16),
            jax.ShapeDtypeStruct((-(-block // 8) * 8, half), F32),
            jax.ShapeDtypeStruct((block, width // 2 * width, half), BF16),
        ),
        (side, *firsts, own),
        [VMEM((n * span, half), F32), VMEM((n * (depth - span), half), F32)],
        need=16,
        in_specs=[sspec()] * 3 + [vspec()],
        flops=2**30,
    )
    piece = jax.ShapeDtypeStruct((rows, half, channels), BF16)
    pair_mine, pair_send, *edges = call(
        functools.partial(outer_kernel, seqs, width),
        (piece, piece)
        + (jax.ShapeDtypeStruct((2 * channels * block // chunks, half), BF16),) * chunks,
        (
            core,
            side,
            *firsts,
            observed_position,
            other,
            left,
            scale,
            products,
            couple_mine,
            couple_theirs,
            table,
            value_w,
            gate_w,
            observed_position.reshape(1, residues),
        ),
        [
            VMEM((n * span, half), F32),
            VMEM((block, width // 2 * width, half), BF16),
            VMEM((2 * channels * block, half), F32),
        ],
        need=20,
        in_specs=[sspec()] * 5 + [vspec()] * 10,
        flops=2**31,
    )

    received = [exchange(values.reshape(n, 2 * some * block, half)) for values in edges]
    pair_theirs = permute(pair_send, across)
    gate_piece = jax.ShapeDtypeStruct((rows, half, channels), F32)
    gate_mine, gate_theirs = call(
        close_gate_kernel,
        (gate_piece, gate_piece),
        (pair_mine, pair_theirs, closing_sigmoid_kernel),
        flops=2**27,
    )

    def triangle(values):
        if rows % 8 == 0:
            return call(
                functools.partial(triangle_kernel, some, rows, places),
                jax.ShapeDtypeStruct((n, some * rows, residues), BF16),
                (values,),
                [
                    VMEM((n, 2 * some * block, half), F32),
                    VMEM((n, some * rows, residues), F32),
                ],
                need=12,
                flops=2**28,
            )
        both = values.reshape(branch // 4, 2, 2, dap, 2, some, 2, rows, half)
        both = jnp.stack([both[:, 0], both[:, 1, :, :, :, :, ::-1]], axis=1)
        both = both.transpose(4, 5, 0, 6, 2, 3, 7, 1, 8).reshape(2, some, residues, residues)
        combined = call(
            plain_triangle_kernel,
            jax.ShapeDtypeStruct((some, residues, residues), BF16),
            (both[0], both[1]),
            need=12,
            flops=2**28,
        )
        combined = combined.reshape(some, n, rows, residues).transpose(1, 0, 2, 3)
        return combined.reshape(n, some * rows, residues)

    returned = []
    for values in received:
        combined = triangle(values)
        combined = exchange(combined)
        returned.append(combined.reshape(n * some * rows, residues))
    pair_output = call(
        close_kernel,
        jax.ShapeDtypeStruct((rows, residues, channels), BF16),
        (side, pair_mine, pair_theirs, gate_mine, gate_theirs, final_w, *returned),
        [sheets(n * some * rows, residues) for _ in returned],
        in_specs=[sspec()] + [vspec()] * (5 + len(returned)),
        flops=2**27,
    )
    return (homolog_refreshed, pair_output)


def solution(mesh):
    split = P(EVERY, None, None)
    in_specs = (split, split, P(EVERY, None)) + (P(),) * 10

    def body(*args):
        return per_device(mesh.shape["branch"], mesh.shape["dap"], *args)

    return jax.shard_map(
        body, mesh=mesh, in_specs=in_specs, out_specs=(split, split), check_vma=False
    )
```

```python
import functools
import math

import jax
import jax.numpy as jnp
from jax import lax
from jax.experimental import pallas as pl
from jax.experimental.pallas import tpu as pltpu
from jax.sharding import PartitionSpec as P


EPSILON = 1e-05
LOG2E = 1.4426950408889634
EVERY = ("branch", "dap")
VMEM = pltpu.VMEM
F32 = jnp.float32
BF16 = jnp.bfloat16

NT = (((1,), (1,)), ((), ()))
TN = (((0,), (0,)), ((), ()))
NN = (((1,), (0,)), ((), ()))


def mm(a, b, dims=NN):
    return lax.dot_general(a, b, dims, preferred_element_type=F32)


def normalize(values, axis=-1):
    values = values.astype(F32)
    centred = values - jnp.mean(values, axis=axis, keepdims=True)
    spread = jnp.mean(centred * centred, axis=axis, keepdims=True)
    return centred * lax.rsqrt(spread + EPSILON)


def vspec():
    return pl.BlockSpec(memory_space=VMEM)


def sspec():
    return pl.BlockSpec(memory_space=pltpu.SMEM)


LANES = 128


def room(mebibytes):
    return pltpu.CompilerParams(vmem_limit_bytes=mebibytes * 2**20)


def sheets(rows, columns):
    return VMEM((columns // LANES, rows, LANES), F32)


def put(scr, start, values, stride):
    for k in range(scr.shape[0]):
        part = values[:, k * LANES : (k + 1) * LANES]
        scr[k, pl.ds(start, values.shape[0], stride=stride), :] = part


def take(scr, start, count, stride=1):
    parts = [scr[k, pl.ds(start, count, stride=stride), :] for k in range(scr.shape[0])]
    return parts[0] if len(parts) == 1 else jnp.concatenate(parts, axis=1)


def fill(scr, values):
    for k in range(scr.shape[0]):
        scr[k] = values[:, k * LANES : (k + 1) * LANES]


def stay(values):
    return pltpu.with_memory_space_constraint(values, pltpu.MemorySpace.HBM)


def call(body, out, args, scratch=(), in_specs=None, flops=0, need=8, **kw):
    single = not isinstance(out, (tuple, list))
    return pl.pallas_call(
        body,
        out_shape=out,
        in_specs=in_specs or [vspec() for _ in args],
        out_specs=vspec() if single else tuple(vspec() for _ in out),
        scratch_shapes=list(scratch),
        cost_estimate=pl.CostEstimate(flops=flops, bytes_accessed=2**20, transcendentals=0),
        compiler_params=room(need),
        **kw,
    )(*args)


def sigmoid(values):
    return 0.5 * jnp.tanh(0.5 * values) + 0.5


def bias_kernel(cores, side_ref, couple_ref, weight_ref, out_ref, mine_ref, theirs_ref, scr):
    rows, residues, _ = couple_ref.shape
    heads = weight_ref.shape[0]
    half = residues // 2
    mine = pl.multiple_of(side_ref[0] * half, half)
    theirs = pl.multiple_of((1 - side_ref[0]) * half, half)
    for i in range(rows):
        normed = normalize(couple_ref[i]).astype(BF16)
        put(scr, i, mm(weight_ref[...], normed, NT), rows)
        mine_ref[i] = couple_ref[i, pl.ds(mine, half), :]
        theirs_ref[i] = couple_ref[i, pl.ds(theirs, half), :]
    part = heads // 2 * rows
    halves = [take(scr, k * part, part).astype(BF16) for k in range(2)]
    for t, core in enumerate(cores):
        out_ref[t] = halves[core]


def prepare_small_kernel(seqs, halves_ref, left_ref, right_ref):
    width = halves_ref.shape[0] // 2
    left = halves_ref[:width].astype(F32).T.astype(BF16)
    for s in range(seqs):
        parts = [left if u == s else jnp.zeros_like(left) for u in range(seqs)]
        left_ref[s] = jnp.concatenate(parts, axis=1)
    right_ref[...] = halves_ref[width:]


def prepare_large_kernel(
    chunks,
    per,
    merge_ref,
    entry_ref,
    close_ref,
    table_ref,
    value_ref,
    gate_ref,
    final_ref,
    merge_scr,
    entry_scr,
    edge_scr,
):
    channels = merge_ref.shape[1]
    width = math.isqrt(merge_ref.shape[0])
    part = width // 2
    merge_scr[...] = merge_ref[...].astype(F32)
    for k in range(2):
        rows = [merge_scr[pl.ds(k * part + q, width, stride=width), :] for q in range(part)]
        table_ref[k] = jnp.concatenate(rows, axis=0).T.astype(BF16)
    for k in range(4):
        entry_scr[k * channels : (k + 1) * channels, :] = (
            entry_ref[:, k * channels : (k + 1) * channels].astype(F32).T
        )
    some = per // chunks
    n = channels // per
    for kind, ref in enumerate((value_ref, gate_ref)):
        for k in range(2):
            for c in range(per):
                source = (2 * k + kind) * channels + c
                at = c // some * n * 2 * some + k * some + c % some
                edge_scr[pl.ds(at, n, stride=2 * some), :] = entry_scr[
                    pl.ds(source, n, stride=per), :
                ]
        ref[...] = edge_scr[...].astype(BF16)
    entry_scr[:channels, :] = close_ref[...].astype(F32)
    for c in range(per):
        at = c // some * n * some + c % some
        edge_scr[pl.ds(at, n, stride=some), :] = entry_scr[pl.ds(c, n, stride=per), :]
    final_ref[...] = edge_scr[:channels, :].astype(BF16)


def project_kernel(seq_ref, qkv_w_ref, gate_w_ref, query_ref, key_ref, value_ref, gate_ref):
    inner = gate_w_ref.shape[1]
    normed = normalize(seq_ref[0]).astype(BF16)
    projected = mm(normed, qkv_w_ref[...])
    query_ref[0] = projected[:, :inner].astype(BF16)
    key_ref[0] = projected[:, inner : 2 * inner].T.astype(BF16)
    value_ref[0] = projected[:, 2 * inner :].astype(BF16)
    gate_ref[0] = sigmoid(mm(normed, gate_w_ref[...]))


def attend_kernel(
    heads,
    places,
    raw,
    core_ref,
    seq_ref,
    keep_ref,
    query_ref,
    key_ref,
    value_ref,
    gate_ref,
    own_ref,
    other_ref,
    merge_ref,
    left_w_ref,
    right_w_ref,
    new_ref,
    message_ref,
    left_scr,
    bias_scr,
    ones_scr,
):
    step = pl.program_id(0)
    batch = seq_ref.shape[0]
    seqs = keep_ref.shape[0]
    core = core_ref[0]
    inner = gate_ref.shape[2]
    residues = gate_ref.shape[1]
    half = inner // 2
    head_width = inner // heads
    scale = head_width ** (-0.5)
    some_heads = heads // 2
    zero = jnp.zeros((), BF16)
    blank = jnp.zeros((head_width, residues), BF16)
    lane_half = lax.broadcasted_iota(jnp.int32, (residues, half), 1) // head_width

    width = right_w_ref.shape[0]
    part = width // 2
    columns = message_ref.shape[2]
    span = seqs * part
    first_lane = lax.broadcasted_iota(jnp.int32, (residues, half), 1) == 0
    flat = jnp.where(first_lane, jnp.ones((), BF16), zero)
    first_row = lax.broadcasted_iota(jnp.int32, (head_width, residues), 0) == 0

    def run(plain):
        waiting = []

        def advance():
            if waiting:
                waiting.pop(0)()

        def finish(u, mixed):
            s = step * batch + u
            present = keep_ref[pl.ds(s, 1), :].astype(F32)
            held = {}

            def merge():
                first = jnp.where(core == 0, mixed[0], mixed[1])
                second = jnp.where(core == 0, mixed[1], mixed[0])
                attended = (jnp.concatenate([first, second], axis=1) * gate_ref[u]).astype(BF16)
                updated = seq_ref[u].astype(F32) + mm(attended, merge_ref[...])
                held["updated"] = updated.astype(BF16)
                new_ref[u] = held["updated"]

            def norm():
                held["normed"] = normalize(held["updated"]).astype(BF16)

            def right():
                values = (mm(right_w_ref[...], held["normed"], NT) * present).astype(BF16)
                at = pl.multiple_of(s * part, part)
                for t, (core_of, side, _) in enumerate(places):
                    message_ref[t, pl.ds(at, part), :] = values[
                        core_of * part : (core_of + 1) * part, side * columns : (side + 1) * columns
                    ]

            def left():
                present_column = jnp.broadcast_to(present, (8, residues)).T[:, :1]
                left_scr[...] += mm(held["normed"], left_w_ref[s]) * present_column

            waiting.extend([merge, norm, right, left])

        for u in range(batch):
            keep = keep_ref[pl.ds(step * batch + u, 1), :]
            if plain:
                masking = jnp.where(keep == 1, 0.0, -1000000000.0).astype(F32)
            else:
                mask = jnp.where(first_row & (keep == 0), -1e30, 0.0).astype(BF16)
            mixed = []
            for k, group in ((0, core), (1, 1 - core)):
                queries, values = (
                    jnp.where(group == 0, ref[u, :, :half], ref[u, :, half:])
                    for ref in (query_ref, value_ref)
                )
                keys = jnp.where(group == 0, key_ref[u, :half, :], key_ref[u, half:, :])
                if not plain:
                    queries = jnp.concatenate([queries, flat], axis=1)
                weights, tables = [], []
                for h in range(some_heads):
                    only = [
                        keys[g * head_width : (g + 1) * head_width] if g == h else blank
                        for g in range(some_heads)
                    ]
                    bias = bias_scr[k * some_heads + h]
                    if plain:
                        logits = mm(queries, jnp.concatenate(only, axis=0)) * scale
                        logits = logits + bias + masking
                        logits = logits - jnp.max(logits, axis=-1, keepdims=True)
                        weights.append(jnp.exp(logits).astype(BF16))
                    else:
                        only += [mask] + [blank] * (some_heads - 1)
                        logits = mm(queries, jnp.concatenate(only, axis=0)) * (scale * LOG2E)
                        logits = logits + bias
                        logits = logits - jnp.max(logits, axis=-1, keepdims=True)
                        weights.append(jnp.exp2(logits).astype(BF16))
                    tables.append(jnp.where(lane_half == h, values, zero))
                    if h % 2 == 1:
                        advance()
                table = jnp.concatenate([jnp.concatenate(tables, axis=0), ones_scr[...]], axis=1)
                total = mm(jnp.concatenate(weights, axis=1), table)
                mixed.append(total[:, :half] * (1.0 / total[:, half:]))
            finish(u, mixed)
        while waiting:
            advance()

    some = jnp.max(keep_ref[...].astype(F32), axis=1, keepdims=True)
    plain = jnp.min(some) == 0.0

    @pl.when(step == 0)
    def _():
        left_scr[...] = jnp.zeros_like(left_scr)
        for h in range(some_heads):
            ones_scr[h * residues : (h + 1) * residues, :] = jnp.where(
                lane_half == h, jnp.ones((), BF16), zero
            )
        unit = jnp.where(plain, 1.0, LOG2E)
        for k, ref in enumerate((own_ref, other_ref)):
            for h in range(some_heads):
                if raw:
                    rows = residues // len(places)
                    tile = ref[:, h * rows : (h + 1) * rows, :].astype(F32)
                    tile = tile.reshape(residues, residues)
                else:
                    tile = ref[h].astype(F32)
                bias_scr[k * some_heads + h] = tile * unit

    pl.when(plain)(functools.partial(run, True))
    pl.when(jnp.logical_not(plain))(functools.partial(run, False))

    @pl.when(step == pl.num_programs(0) - 1)
    def _():
        rows = residues // len(places)
        marks = keep_ref[...].astype(F32)
        marks = jnp.concatenate(
            [marks[:, k * columns : (k + 1) * columns] for k in range(2)], axis=0
        ).astype(BF16)
        for t, (_, _, mate) in enumerate(places):
            block = jnp.concatenate(
                [left_scr[u * rows : (u + 1) * rows, :] for u in (t, mate)], axis=0
            )
            message_ref[t, span : span + 2 * rows, :] = block.astype(BF16)
            message_ref[t, span + 2 * rows :, :] = marks


def multiply(seqs, width, left, ref, scr, products):
    n, _, columns = ref.shape
    part = width // 2
    span = seqs * part
    block = left.shape[0] // width
    scr[...] = ref[:, :span, :].astype(F32).reshape(n * span, columns)
    for q in range(0, part, 2):
        pair = [
            jnp.concatenate(
                [scr[pl.ds(s * part + q + d, n, stride=span), :] for s in range(seqs)], axis=0
            ).astype(BF16)
            for d in range(2)
        ]
        outer = mm(left, jnp.concatenate(pair, axis=1)).astype(BF16)
        for d in range(2):
            at = (q + d) * width
            for i in range(block):
                products[i, at : at + width, :] = outer[
                    i * width : (i + 1) * width, d * columns : (d + 1) * columns
                ]


def outer_own_kernel(
    seqs,
    width,
    rows,
    side_ref,
    first_mine_ref,
    first_theirs_ref,
    own_ref,
    left_ref,
    scale_ref,
    products_ref,
    right_scr,
    small_scr,
):
    n, depth, columns = own_ref.shape
    block = 2 * rows
    total_seqs = n * seqs
    span = seqs * width // 2
    side, first_mine, first_theirs = side_ref[0], first_mine_ref[0], first_theirs_ref[0]
    extra = depth - span
    small_scr[...] = own_ref[:, span:, :].astype(F32).reshape(n * extra, columns)
    left_rows = []
    for i in range(block):
        piece = small_scr[pl.ds(i, n, stride=extra), :]
        for s in range(seqs):
            left_rows.append(piece[:, s * width : (s + 1) * width])
    left_all = jnp.concatenate(left_rows, axis=0).T
    left = jnp.concatenate(
        [left_all[:, i * total_seqs : (i + 1) * total_seqs] for i in range(block)], axis=0
    ).astype(BF16)
    left_ref[...] = left
    keep_halves = []
    for k in range(2):
        at = block + k * seqs
        keep_halves.append(
            jnp.concatenate(
                [small_scr[pl.ds(at + s, n, stride=extra), :] for s in range(seqs)], axis=0
            )
        )
    keep_columns = jnp.where(side == 0, keep_halves[0], keep_halves[1]).astype(BF16)
    keep = jnp.concatenate(keep_halves, axis=1).astype(BF16)
    pad = scale_ref.shape[0]
    order = lax.broadcasted_iota(jnp.int32, (pad, 2 * columns), 0)
    row_ids = jnp.where(order < rows, first_mine + order, first_theirs + order - rows)
    chosen = (row_ids == lax.broadcasted_iota(jnp.int32, (pad, 2 * columns), 1)).astype(BF16)
    counts = mm(mm(chosen, keep, NT).astype(BF16), keep_columns)
    scale_ref[...] = 1.0 / jnp.maximum(counts, 1.0)
    multiply(seqs, width, left, own_ref, right_scr, products_ref)


def outer_kernel(
    seqs,
    width,
    core_ref,
    side_ref,
    first_mine_ref,
    first_theirs_ref,
    marks_ref,
    other_ref,
    left_ref,
    scale_ref,
    own_products_ref,
    couple_mine_ref,
    couple_theirs_ref,
    table_ref,
    value_w_ref,
    gate_w_ref,
    observed_ref,
    pair_mine_ref,
    pair_theirs_ref,
    *rest,
):
    edges_refs, (right_scr, products, edge_scr) = rest[:-3], rest[-3:]
    rows, columns, channels = couple_mine_ref.shape
    block = 2 * rows
    core, side = core_ref[0], side_ref[0]
    first_mine, first_theirs = first_mine_ref[0], first_theirs_ref[0]
    multiply(seqs, width, left_ref[...], other_ref, right_scr, products)
    scale = scale_ref[...]
    tables = ((table_ref[core], own_products_ref), (table_ref[1 - core], products))
    half = pl.multiple_of(side * columns, columns)
    observed = observed_ref[:, pl.ds(half, columns)].astype(F32)
    row_marks = [marks_ref[first_mine + r] for r in range(rows)]
    row_marks += [marks_ref[first_theirs + r] for r in range(rows)]
    updates, norms = {}, {}

    def project(i):
        updates[i] = sum(
            mm(table, jnp.concatenate([values[i], values[i + 1]], axis=1))
            for table, values in tables
        )

    def add(i):
        normed = []
        for d in range(2):
            piece = updates[i][:, d * columns : (d + 1) * columns] * scale[i + d : i + d + 1, :]
            couple_ref, pair_ref = (
                (couple_mine_ref, pair_mine_ref)
                if i + d < rows
                else (couple_theirs_ref, pair_theirs_ref)
            )
            r = (i + d) % rows
            pair = (couple_ref[r].astype(F32) + piece.T).astype(BF16)
            pair_ref[r] = pair
            normed.append(normalize(pair).astype(BF16))
        norms[i] = jnp.concatenate(normed, axis=0)

    def edge(i):
        values = mm(value_w_ref[...], norms[i], NT) * sigmoid(mm(gate_w_ref[...], norms[i], NT))
        for d in range(2):
            mark = observed * row_marks[i + d].astype(F32)
            edge_scr[pl.ds(i + d, 2 * channels, stride=block), :] = (
                values[:, d * columns : (d + 1) * columns] * mark
            )

    for i in range(0, block + 4, 2):
        for stage, late in ((project, 0), (add, 2), (edge, 4)):
            if 0 <= i - late < block:
                stage(i - late)
    size = edges_refs[0].shape[0]
    for k, ref in enumerate(edges_refs):
        ref[...] = edge_scr[k * size : (k + 1) * size, :].astype(BF16)


def close_gate_kernel(mine_ref, theirs_ref, weight_ref, mine_gate_ref, theirs_gate_ref):
    for pair_ref, gate_ref in ((mine_ref, mine_gate_ref), (theirs_ref, theirs_gate_ref)):
        for i in range(pair_ref.shape[0]):
            normed = normalize(pair_ref[i]).astype(BF16)
            gate_ref[i] = sigmoid(mm(normed, weight_ref[...]))


def triangle_kernel(per, rows, places, in_ref, out_ref, in_scr, out_scr):
    n = in_ref.shape[0]
    residues = n * rows
    in_scr[...] = in_ref[...].astype(F32)

    def whole(at):
        tiles = []
        for t, (_, side, mate) in enumerate(places):
            pair = []
            for k in range(2):
                source, shift = (t, 0) if side == k else (mate, rows)
                pair.append(in_scr[source, at + shift : at + shift + rows, :])
            tiles.append(jnp.concatenate(pair, axis=1))
        return jnp.concatenate(tiles, axis=0).astype(BF16)

    for c in range(per):
        left = whole(c * 2 * rows)
        right = whole((per + c) * 2 * rows)
        out_scr[:, c * rows : (c + 1) * rows, :] = mm(left, right, NT).reshape(n, rows, residues)
    out_ref[...] = out_scr[...].astype(BF16)


def plain_triangle_kernel(left_ref, right_ref, out_ref):
    for c in range(left_ref.shape[0]):
        out_ref[c] = mm(left_ref[c], right_ref[c], NT).astype(BF16)


def close_kernel(
    side_ref, mine_ref, theirs_ref, mine_gate_ref, theirs_gate_ref, weight_ref, *rest
):
    count = (len(rest) - 1) // 2
    in_refs, out_ref, scrs = rest[:count], rest[count], rest[count + 1 :]
    rows, columns, channels = mine_ref.shape
    for ref, scr in zip(in_refs, scrs):
        fill(scr, ref[...].astype(F32))
    side = side_ref[0]
    for half, pair_ref, gate_ref in (
        (side, mine_ref, mine_gate_ref),
        (1 - side, theirs_ref, theirs_gate_ref),
    ):
        at = pl.multiple_of(half * columns, columns)
        for i in range(rows):
            piece = [scr[half, pl.ds(i, channels // count, stride=rows), :] for scr in scrs]
            piece = jnp.concatenate(piece, axis=0)
            update = mm(normalize(piece, axis=0).astype(BF16), weight_ref[...], TN)
            out_ref[i, pl.ds(at, columns), :] = (
                pair_ref[i].astype(F32) + gate_ref[i] * update
            ).astype(BF16)


def per_device(
    branch,
    dap,
    homolog_embedding,
    couple_embedding,
    homolog_present,
    observed_position,
    couple_logit_kernel,
    lookup_kernels,
    heads_sigmoid_kernel,
    heads_merge_kernel,
    tensor_halves_kernel,
    tensor_merge_kernel,
    edge_entry_kernel,
    closing_sigmoid_kernel,
    closing_merge_kernel,
):
    n = branch * dap
    rows, residues, channels = couple_embedding.shape
    seqs = homolog_embedding.shape[0]
    features = homolog_embedding.shape[2]
    heads = couple_logit_kernel.shape[1]
    inner = heads_sigmoid_kernel.shape[1]
    width = tensor_halves_kernel.shape[1] // 2
    per = channels // n
    half = residues // 2
    block = 2 * rows

    chunks = 1
    some = per // chunks
    places = [((t // dap) % 2, (t // dap // 2) % 2, (t // dap ^ 2) * dap + t % dap) for t in range(n)]
    me = lax.axis_index("branch").astype(jnp.int32)
    core = (me % 2).reshape(1)
    side = (me // 2 % 2).reshape(1)
    place = lax.axis_index("dap").astype(jnp.int32)
    first_mine = (me * dap + place) * rows
    first_theirs = ((me ^ 2) * dap + place) * rows
    chip = [(b, b ^ 1) for b in range(branch)]
    across = [(b, b ^ 2) for b in range(branch)]

    def exchange(values):
        return lax.all_to_all(values, EVERY, split_axis=0, concat_axis=0, tiled=True)

    def permute(values, pairs):
        return lax.ppermute(values, "branch", pairs)

    left_w, right_w = call(
        functools.partial(prepare_small_kernel, seqs),
        (
            jax.ShapeDtypeStruct((seqs, features, seqs * width), BF16),
            jax.ShapeDtypeStruct((width, features), BF16),
        ),
        (tensor_halves_kernel.T,),
    )
    table, value_w, gate_w, final_w = call(
        functools.partial(prepare_large_kernel, chunks, per),
        (
            jax.ShapeDtypeStruct((2, channels, width // 2 * width), BF16),
            jax.ShapeDtypeStruct((2 * channels, channels), BF16),
            jax.ShapeDtypeStruct((2 * channels, channels), BF16),
            jax.ShapeDtypeStruct((channels, channels), BF16),
        ),
        (tensor_merge_kernel, edge_entry_kernel, closing_merge_kernel),
        [
            VMEM((width * width, channels), F32),
            VMEM((4 * channels, channels), F32),
            VMEM((2 * channels, channels), F32),
        ],
    )

    half_heads = heads // 2
    message, couple_mine, couple_send = call(
        functools.partial(bias_kernel, [place[0] for place in places]),
        (
            jax.ShapeDtypeStruct((n, half_heads * rows, residues), BF16),
            jax.ShapeDtypeStruct((rows, half, channels), BF16),
            jax.ShapeDtypeStruct((rows, half, channels), BF16),
        ),
        (side, stay(couple_embedding), stay(couple_logit_kernel.T)),
        [sheets(heads * rows, residues)],
        in_specs=[sspec(), vspec(), vspec()],
    )
    own_bias = exchange(message)
    raw = rows % 8 == 0
    if not raw:
        own_bias = own_bias.reshape(n, half_heads, rows, residues)
        own_bias = own_bias.transpose(1, 0, 2, 3).reshape(half_heads, residues, residues)
    other_bias = permute(own_bias, chip)
    couple_theirs = permute(couple_send, across)

    def whole(*shape):
        return pl.BlockSpec(shape, lambda s: (0,) * len(shape))

    def per_seq(batch, *shape):
        return pl.BlockSpec((batch, *shape), lambda s: (s,) + (0,) * len(shape))

    *parts, gates = pl.pallas_call(
        project_kernel,
        grid=(seqs,),
        out_shape=(
            jax.ShapeDtypeStruct((seqs, residues, inner), BF16),
            jax.ShapeDtypeStruct((seqs, inner, residues), BF16),
            jax.ShapeDtypeStruct((seqs, residues, inner), BF16),
            jax.ShapeDtypeStruct((seqs, residues, inner), F32),
        ),
        in_specs=[
            per_seq(1, residues, features),
            whole(features, 3 * inner),
            whole(features, inner),
        ],
        out_specs=(
            per_seq(1, residues, inner),
            per_seq(1, inner, residues),
            per_seq(1, residues, inner),
            per_seq(1, residues, inner),
        ),
        name="project",
        compiler_params=room(16),
        cost_estimate=pl.CostEstimate(flops=2**29, bytes_accessed=2**22, transcendentals=0),
    )(stay(homolog_embedding), stay(lookup_kernels), stay(heads_sigmoid_kernel))
    span = seqs * width // 2
    depth = span + block + 2 * seqs
    batch = seqs
    homolog_refreshed, message = pl.pallas_call(
        functools.partial(attend_kernel, heads, places, raw),
        grid=(seqs // batch,),
        out_shape=(
            jax.ShapeDtypeStruct((seqs, residues, features), BF16),
            jax.ShapeDtypeStruct((n, depth, half), BF16),
        ),
        in_specs=[
            sspec(),
            per_seq(batch, residues, features),
            whole(seqs, residues),
            per_seq(batch, residues, inner),
            per_seq(batch, inner, residues),
            per_seq(batch, residues, inner),
            per_seq(batch, residues, inner),
            whole(*own_bias.shape),
            whole(*own_bias.shape),
            whole(inner, features),
            whole(seqs, features, seqs * width),
            whole(width, features),
        ],
        out_specs=(per_seq(batch, residues, features), whole(n, depth, half)),
        scratch_shapes=[
            VMEM((residues, seqs * width), F32),
            VMEM((heads, residues, residues), F32),
            VMEM((half_heads * residues, half), BF16),
        ],
        name="attend",
        compiler_params=room(24),
        cost_estimate=pl.CostEstimate(flops=2**31, bytes_accessed=2**22, transcendentals=0),
    )(
        core,
        stay(homolog_embedding),
        stay(homolog_present),
        *(stay(values) for values in parts),
        stay(gates),
        own_bias,
        other_bias,
        stay(heads_merge_kernel),
        left_w,
        right_w,
    )

    own = exchange(message)
    other = permute(own, chip)
    firsts = (first_mine.reshape(1), first_theirs.reshape(1))
    left, scale, products = call(
        functools.partial(outer_own_kernel, seqs, width, rows),
        (
            jax.ShapeDtypeStruct((block * width, n * seqs), BF16),
            jax.ShapeDtypeStruct((-(-block // 8) * 8, half), F32),
            jax.ShapeDtypeStruct((block, width // 2 * width, half), BF16),
        ),
        (side, *firsts, own),
        [VMEM((n * span, half), F32), VMEM((n * (depth - span), half), F32)],
        need=16,
        in_specs=[sspec()] * 3 + [vspec()],
        flops=2**30,
    )
    piece = jax.ShapeDtypeStruct((rows, half, channels), BF16)
    pair_mine, pair_send, *edges = call(
        functools.partial(outer_kernel, seqs, width),
        (piece, piece)
        + (jax.ShapeDtypeStruct((2 * channels * block // chunks, half), BF16),) * chunks,
        (
            core,
            side,
            *firsts,
            observed_position,
            other,
            left,
            scale,
            products,
            couple_mine,
            couple_theirs,
            table,
            value_w,
            gate_w,
            observed_position.reshape(1, residues),
        ),
        [
            VMEM((n * span, half), F32),
            VMEM((block, width // 2 * width, half), BF16),
            VMEM((2 * channels * block, half), F32),
        ],
        need=20,
        in_specs=[sspec()] * 5 + [vspec()] * 10,
        flops=2**31,
    )

    received = [exchange(values.reshape(n, 2 * some * block, half)) for values in edges]
    pair_theirs = permute(pair_send, across)
    gate_piece = jax.ShapeDtypeStruct((rows, half, channels), F32)
    gate_mine, gate_theirs = call(
        close_gate_kernel,
        (gate_piece, gate_piece),
        (pair_mine, pair_theirs, closing_sigmoid_kernel),
        flops=2**27,
    )

    def triangle(values):
        if rows % 8 == 0:
            return call(
                functools.partial(triangle_kernel, some, rows, places),
                jax.ShapeDtypeStruct((n, some * rows, residues), BF16),
                (values,),
                [
                    VMEM((n, 2 * some * block, half), F32),
                    VMEM((n, some * rows, residues), F32),
                ],
                need=12,
                flops=2**28,
            )
        both = values.reshape(branch // 4, 2, 2, dap, 2, some, 2, rows, half)
        both = jnp.stack([both[:, 0], both[:, 1, :, :, :, :, ::-1]], axis=1)
        both = both.transpose(4, 5, 0, 6, 2, 3, 7, 1, 8).reshape(2, some, residues, residues)
        combined = call(
            plain_triangle_kernel,
            jax.ShapeDtypeStruct((some, residues, residues), BF16),
            (both[0], both[1]),
            need=12,
            flops=2**28,
        )
        combined = combined.reshape(some, n, rows, residues).transpose(1, 0, 2, 3)
        return combined.reshape(n, some * rows, residues)

    returned = []
    for values in received:
        combined = triangle(values)
        combined = exchange(combined)
        returned.append(combined.reshape(n * some * rows, residues))
    pair_output = call(
        close_kernel,
        jax.ShapeDtypeStruct((rows, residues, channels), BF16),
        (side, pair_mine, pair_theirs, gate_mine, gate_theirs, final_w, *returned),
        [sheets(n * some * rows, residues) for _ in returned],
        in_specs=[sspec()] + [vspec()] * (5 + len(returned)),
        flops=2**27,
    )
    return (homolog_refreshed, pair_output)


def solution(mesh):
    split = P(EVERY, None, None)
    in_specs = (split, split, P(EVERY, None)) + (P(),) * 10

    def body(*args):
        return per_device(mesh.shape["branch"], mesh.shape["dap"], *args)

    return jax.shard_map(
        body, mesh=mesh, in_specs=in_specs, out_specs=(split, split), check_vma=False
    )
```

```python
import functools
import math

import jax
import jax.numpy as jnp
from jax import lax
from jax.experimental import pallas as pl
from jax.experimental.pallas import tpu as pltpu
from jax.sharding import PartitionSpec as P


EPSILON = 1e-05
LOG2E = 1.4426950408889634
EVERY = ("branch", "dap")
VMEM = pltpu.VMEM
F32 = jnp.float32
BF16 = jnp.bfloat16

NT = (((1,), (1,)), ((), ()))
TN = (((0,), (0,)), ((), ()))
NN = (((1,), (0,)), ((), ()))


def mm(a, b, dims=NN):
    return lax.dot_general(a, b, dims, preferred_element_type=F32)


def normalize(values, axis=-1):
    values = values.astype(F32)
    centred = values - jnp.mean(values, axis=axis, keepdims=True)
    spread = jnp.mean(centred * centred, axis=axis, keepdims=True)
    return centred * lax.rsqrt(spread + EPSILON)


def vspec():
    return pl.BlockSpec(memory_space=VMEM)


def sspec():
    return pl.BlockSpec(memory_space=pltpu.SMEM)


LANES = 128


def room(mebibytes):
    return pltpu.CompilerParams(vmem_limit_bytes=mebibytes * 2**20)


def sheets(rows, columns):
    return VMEM((columns // LANES, rows, LANES), F32)


def put(scr, start, values, stride):
    for k in range(scr.shape[0]):
        part = values[:, k * LANES : (k + 1) * LANES]
        scr[k, pl.ds(start, values.shape[0], stride=stride), :] = part


def take(scr, start, count, stride=1):
    parts = [scr[k, pl.ds(start, count, stride=stride), :] for k in range(scr.shape[0])]
    return parts[0] if len(parts) == 1 else jnp.concatenate(parts, axis=1)


def fill(scr, values):
    for k in range(scr.shape[0]):
        scr[k] = values[:, k * LANES : (k + 1) * LANES]


def stay(values):
    return pltpu.with_memory_space_constraint(values, pltpu.MemorySpace.HBM)


def call(body, out, args, scratch=(), in_specs=None, flops=0, need=8, **kw):
    single = not isinstance(out, (tuple, list))
    return pl.pallas_call(
        body,
        out_shape=out,
        in_specs=in_specs or [vspec() for _ in args],
        out_specs=vspec() if single else tuple(vspec() for _ in out),
        scratch_shapes=list(scratch),
        cost_estimate=pl.CostEstimate(flops=flops, bytes_accessed=2**20, transcendentals=0),
        compiler_params=room(need),
        **kw,
    )(*args)


def sigmoid(values):
    return 0.5 * jnp.tanh(0.5 * values) + 0.5


def bias_kernel(cores, side_ref, couple_ref, weight_ref, out_ref, mine_ref, theirs_ref, scr):
    rows, residues, _ = couple_ref.shape
    heads = weight_ref.shape[0]
    half = residues // 2
    mine = pl.multiple_of(side_ref[0] * half, half)
    theirs = pl.multiple_of((1 - side_ref[0]) * half, half)
    for i in range(rows):
        normed = normalize(couple_ref[i]).astype(BF16)
        put(scr, i, mm(weight_ref[...], normed, NT), rows)
        mine_ref[i] = couple_ref[i, pl.ds(mine, half), :]
        theirs_ref[i] = couple_ref[i, pl.ds(theirs, half), :]
    part = heads // 2 * rows
    halves = [take(scr, k * part, part).astype(BF16) for k in range(2)]
    for t, core in enumerate(cores):
        out_ref[t] = halves[core]


def prepare_small_kernel(seqs, halves_ref, present_ref, left_ref, right_ref, keep_ref):
    keep_ref[...] = present_ref[...]
    width = halves_ref.shape[0] // 2
    left = halves_ref[:width].astype(F32).T.astype(BF16)
    for s in range(seqs):
        parts = [left if u == s else jnp.zeros_like(left) for u in range(seqs)]
        left_ref[s] = jnp.concatenate(parts, axis=1)
    right_ref[...] = halves_ref[width:]


def prepare_large_kernel(
    chunks,
    per,
    merge_ref,
    entry_ref,
    close_ref,
    table_ref,
    value_ref,
    gate_ref,
    final_ref,
    merge_scr,
    entry_scr,
    edge_scr,
):
    channels = merge_ref.shape[1]
    width = math.isqrt(merge_ref.shape[0])
    part = width // 2
    merge_scr[...] = merge_ref[...].astype(F32)
    for k in range(2):
        rows = [merge_scr[pl.ds(k * part + q, width, stride=width), :] for q in range(part)]
        table_ref[k] = jnp.concatenate(rows, axis=0).T.astype(BF16)
    for k in range(4):
        entry_scr[k * channels : (k + 1) * channels, :] = (
            entry_ref[:, k * channels : (k + 1) * channels].astype(F32).T
        )
    some = per // chunks
    n = channels // per
    for kind, ref in enumerate((value_ref, gate_ref)):
        for k in range(2):
            for c in range(per):
                source = (2 * k + kind) * channels + c
                at = c // some * n * 2 * some + k * some + c % some
                edge_scr[pl.ds(at, n, stride=2 * some), :] = entry_scr[
                    pl.ds(source, n, stride=per), :
                ]
        ref[...] = edge_scr[...].astype(BF16)
    entry_scr[:channels, :] = close_ref[...].astype(F32)
    for c in range(per):
        at = c // some * n * some + c % some
        edge_scr[pl.ds(at, n, stride=some), :] = entry_scr[pl.ds(c, n, stride=per), :]
    final_ref[...] = edge_scr[:channels, :].astype(BF16)


def project_kernel(seq_ref, qkv_w_ref, gate_w_ref, query_ref, key_ref, value_ref, gate_ref):
    inner = gate_w_ref.shape[1]
    normed = normalize(seq_ref[0]).astype(BF16)
    projected = mm(normed, qkv_w_ref[...])
    query_ref[0] = projected[:, :inner].astype(BF16)
    key_ref[0] = projected[:, inner : 2 * inner].T.astype(BF16)
    value_ref[0] = projected[:, 2 * inner :].astype(BF16)
    gate_ref[0] = sigmoid(mm(normed, gate_w_ref[...]))


def attend_kernel(
    heads,
    places,
    raw,
    core_ref,
    keep_ref,
    own_ref,
    other_ref,
    merge_ref,
    left_w_ref,
    right_w_ref,
    *rest,
):
    sources, (new_out, message_out) = rest[:5], rest[5:7]
    seq_ref, query_ref, key_ref, value_ref, gate_ref = held_refs = rest[7:12]
    new_ref, message_ref, left_scr, bias_scr, ones_scr, in_sems, new_sems, message_sems = rest[12:]
    batch = seqs = keep_ref.shape[0]
    arrivals = [
        [
            pltpu.make_async_copy(source.at[u], held.at[u], in_sems.at[k, u])
            for k, (source, held) in enumerate(zip(sources, held_refs))
        ]
        for u in range(seqs)
    ]
    for copies in arrivals:
        for copy in copies:
            copy.start()
    core = core_ref[0]
    inner = gate_ref.shape[2]
    residues = gate_ref.shape[1]
    half = inner // 2
    head_width = inner // heads
    scale = head_width ** (-0.5)
    some_heads = heads // 2
    zero = jnp.zeros((), BF16)
    blank = jnp.zeros((head_width, residues), BF16)
    lane_half = lax.broadcasted_iota(jnp.int32, (residues, half), 1) // head_width

    width = right_w_ref.shape[0]
    part = width // 2
    columns = message_ref.shape[2]
    span = seqs * part
    first_lane = lax.broadcasted_iota(jnp.int32, (residues, half), 1) == 0
    flat = jnp.where(first_lane, jnp.ones((), BF16), zero)
    first_row = lax.broadcasted_iota(jnp.int32, (head_width, residues), 0) == 0

    pieces = message_ref.shape[1] % 8 == 0 and part % 16 == 0

    def departure(u):
        rows = pl.ds(u * part, part)
        return pltpu.make_async_copy(
            message_ref.at[:, rows, :], message_out.at[:, rows, :], message_sems.at[u]
        )

    def run(plain):
        waiting = []

        def advance():
            if waiting:
                waiting.pop(0)()

        def finish(u, mixed):
            s = u
            present = keep_ref[pl.ds(s, 1), :].astype(F32)
            held = {}

            def merge():
                first = jnp.where(core == 0, mixed[0], mixed[1])
                second = jnp.where(core == 0, mixed[1], mixed[0])
                attended = (jnp.concatenate([first, second], axis=1) * gate_ref[u]).astype(BF16)
                updated = seq_ref[u].astype(F32) + mm(attended, merge_ref[...])
                held["updated"] = updated.astype(BF16)
                new_ref[u] = held["updated"]
                pltpu.make_async_copy(new_ref.at[u], new_out.at[u], new_sems.at[u]).start()

            def norm():
                held["normed"] = normalize(held["updated"]).astype(BF16)

            def right():
                values = (mm(right_w_ref[...], held["normed"], NT) * present).astype(BF16)
                for t, (core_of, side, _) in enumerate(places):
                    message_ref[t, s * part : (s + 1) * part, :] = values[
                        core_of * part : (core_of + 1) * part, side * columns : (side + 1) * columns
                    ]
                if pieces:
                    departure(s).start()

            def left():
                present_column = jnp.broadcast_to(present, (8, residues)).T[:, :1]
                left_scr[...] += mm(held["normed"], left_w_ref[s]) * present_column

            waiting.extend([merge, norm, right, left])

        for u in range(batch):
            for copy in arrivals[u]:
                copy.wait()
            keep = keep_ref[pl.ds(u, 1), :]
            if plain:
                masking = jnp.where(keep == 1, 0.0, -1000000000.0).astype(F32)
            else:
                mask = jnp.where(first_row & (keep == 0), -1e30, 0.0).astype(BF16)
            mixed = []
            for k, group in ((0, core), (1, 1 - core)):
                queries, values = (
                    jnp.where(group == 0, ref[u, :, :half], ref[u, :, half:])
                    for ref in (query_ref, value_ref)
                )
                keys = jnp.where(group == 0, key_ref[u, :half, :], key_ref[u, half:, :])
                if not plain:
                    queries = jnp.concatenate([queries, flat], axis=1)
                weights, tables = [], []
                for h in range(some_heads):
                    only = [
                        keys[g * head_width : (g + 1) * head_width] if g == h else blank
                        for g in range(some_heads)
                    ]
                    bias = bias_scr[k * some_heads + h]
                    if plain:
                        logits = mm(queries, jnp.concatenate(only, axis=0)) * scale
                        logits = logits + bias + masking
                        logits = logits - jnp.max(logits, axis=-1, keepdims=True)
                        weights.append(jnp.exp(logits).astype(BF16))
                    else:
                        only += [mask] + [blank] * (some_heads - 1)
                        logits = mm(queries, jnp.concatenate(only, axis=0)) * (scale * LOG2E)
                        logits = logits + bias
                        logits = logits - jnp.max(logits, axis=-1, keepdims=True)
                        weights.append(jnp.exp2(logits).astype(BF16))
                    tables.append(jnp.where(lane_half == h, values, zero))
                    if h % 2 == 1:
                        advance()
                table = jnp.concatenate([jnp.concatenate(tables, axis=0), ones_scr[...]], axis=1)
                total = mm(jnp.concatenate(weights, axis=1), table)
                mixed.append(total[:, :half] * (1.0 / total[:, half:]))
            finish(u, mixed)
        while waiting:
            advance()

    some = jnp.max(keep_ref[...].astype(F32), axis=1, keepdims=True)
    plain = jnp.min(some) == 0.0

    left_scr[...] = jnp.zeros_like(left_scr)
    for h in range(some_heads):
        ones_scr[h * residues : (h + 1) * residues, :] = jnp.where(
            lane_half == h, jnp.ones((), BF16), zero
        )
    unit = jnp.where(plain, 1.0, LOG2E)
    for k, ref in enumerate((own_ref, other_ref)):
        for h in range(some_heads):
            if raw:
                rows = residues // len(places)
                tile = ref[:, h * rows : (h + 1) * rows, :].astype(F32)
                tile = tile.reshape(residues, residues)
            else:
                tile = ref[h].astype(F32)
            bias_scr[k * some_heads + h] = tile * unit

    pl.when(plain)(functools.partial(run, True))
    pl.when(jnp.logical_not(plain))(functools.partial(run, False))

    rows = residues // len(places)
    marks = keep_ref[...].astype(F32)
    marks = jnp.concatenate(
        [marks[:, k * columns : (k + 1) * columns] for k in range(2)], axis=0
    ).astype(BF16)
    for t, (_, _, mate) in enumerate(places):
        tile = jnp.concatenate([left_scr[u * rows : (u + 1) * rows, :] for u in (t, mate)], axis=0)
        message_ref[t, span : span + 2 * rows, :] = tile.astype(BF16)
        message_ref[t, span + 2 * rows :, :] = marks
    if pieces:
        last = pltpu.make_async_copy(
            message_ref.at[:, span:, :], message_out.at[:, span:, :], message_sems.at[seqs]
        )
    else:
        last = pltpu.make_async_copy(message_ref, message_out, message_sems.at[seqs])
    last.start()
    for u in range(seqs):
        pltpu.make_async_copy(new_ref.at[u], new_out.at[u], new_sems.at[u]).wait()
        if pieces:
            departure(u).wait()
    last.wait()


def multiply(seqs, width, left, ref, scr, products):
    n, _, columns = ref.shape
    part = width // 2
    span = seqs * part
    block = left.shape[0] // width
    scr[...] = ref[:, :span, :].astype(F32).reshape(n * span, columns)
    for q in range(0, part, 2):
        pair = [
            jnp.concatenate(
                [scr[pl.ds(s * part + q + d, n, stride=span), :] for s in range(seqs)], axis=0
            ).astype(BF16)
            for d in range(2)
        ]
        outer = mm(left, jnp.concatenate(pair, axis=1)).astype(BF16)
        for d in range(2):
            at = (q + d) * width
            for i in range(block):
                products[i, at : at + width, :] = outer[
                    i * width : (i + 1) * width, d * columns : (d + 1) * columns
                ]


def outer_own_kernel(
    seqs,
    width,
    rows,
    core_ref,
    side_ref,
    first_mine_ref,
    first_theirs_ref,
    own_ref,
    table_ref,
    observed_ref,
    left_ref,
    scale_ref,
    marks_ref,
    update_ref,
    right_scr,
    small_scr,
    products,
):
    n, depth, columns = own_ref.shape
    block = 2 * rows
    total_seqs = n * seqs
    span = seqs * width // 2
    side, first_mine, first_theirs = side_ref[0], first_mine_ref[0], first_theirs_ref[0]
    extra = depth - span
    small_scr[...] = own_ref[:, span:, :].astype(F32).reshape(n * extra, columns)
    left_rows = []
    for i in range(block):
        piece = small_scr[pl.ds(i, n, stride=extra), :]
        for s in range(seqs):
            left_rows.append(piece[:, s * width : (s + 1) * width])
    left_all = jnp.concatenate(left_rows, axis=0).T
    left = jnp.concatenate(
        [left_all[:, i * total_seqs : (i + 1) * total_seqs] for i in range(block)], axis=0
    ).astype(BF16)
    left_ref[...] = left
    keep_halves = []
    for k in range(2):
        at = block + k * seqs
        keep_halves.append(
            jnp.concatenate(
                [small_scr[pl.ds(at + s, n, stride=extra), :] for s in range(seqs)], axis=0
            )
        )
    keep_columns = jnp.where(side == 0, keep_halves[0], keep_halves[1]).astype(BF16)
    keep = jnp.concatenate(keep_halves, axis=1).astype(BF16)
    pad = scale_ref.shape[0]
    order = lax.broadcasted_iota(jnp.int32, (pad, 2 * columns), 0)
    row_ids = jnp.where(order < rows, first_mine + order, first_theirs + order - rows)
    chosen = (row_ids == lax.broadcasted_iota(jnp.int32, (pad, 2 * columns), 1)).astype(BF16)
    counts = mm(mm(chosen, keep, NT).astype(BF16), keep_columns)
    scale_ref[...] = 1.0 / jnp.maximum(counts, 1.0)
    observed = observed_ref[...].astype(F32)
    row_marks = mm(chosen, jnp.broadcast_to(observed, (8, 2 * columns)).astype(BF16), NT)[:, :1]
    column_marks = jnp.where(side == 0, observed[:, :columns], observed[:, columns:])
    marks_ref[...] = row_marks * column_marks
    multiply(seqs, width, left, own_ref, right_scr, products)
    table = table_ref[core_ref[0]]
    for i in range(0, block, 2):
        update_ref[i // 2] = mm(table, jnp.concatenate([products[i], products[i + 1]], axis=1))


def outer_kernel(
    seqs,
    width,
    core_ref,
    other_ref,
    left_ref,
    scale_ref,
    marks_ref,
    own_update_ref,
    couple_mine_ref,
    couple_theirs_ref,
    table_ref,
    value_w_ref,
    gate_w_ref,
    pair_mine_ref,
    pair_theirs_ref,
    *rest,
):
    edges_refs, (right_scr, products, edge_scr) = rest[:-3], rest[-3:]
    rows, columns, channels = couple_mine_ref.shape
    block = 2 * rows
    multiply(seqs, width, left_ref[...], other_ref, right_scr, products)
    scale = scale_ref[...]
    table = table_ref[1 - core_ref[0]]
    updates, norms = {}, {}

    def project(i):
        part = mm(table, jnp.concatenate([products[i], products[i + 1]], axis=1))
        updates[i] = own_update_ref[i // 2] + part

    def add(i):
        normed = []
        for d in range(2):
            piece = updates[i][:, d * columns : (d + 1) * columns] * scale[i + d : i + d + 1, :]
            couple_ref, pair_ref = (
                (couple_mine_ref, pair_mine_ref)
                if i + d < rows
                else (couple_theirs_ref, pair_theirs_ref)
            )
            r = (i + d) % rows
            pair = (couple_ref[r].astype(F32) + piece.T).astype(BF16)
            pair_ref[r] = pair
            normed.append(normalize(pair).astype(BF16))
        norms[i] = jnp.concatenate(normed, axis=0)

    def edge(i):
        values = mm(value_w_ref[...], norms[i], NT) * sigmoid(mm(gate_w_ref[...], norms[i], NT))
        for d in range(2):
            mark = marks_ref[i + d : i + d + 1, :]
            edge_scr[pl.ds(i + d, 2 * channels, stride=block), :] = (
                values[:, d * columns : (d + 1) * columns] * mark
            )

    for i in range(0, block + 4, 2):
        for stage, late in ((project, 0), (add, 2), (edge, 4)):
            if 0 <= i - late < block:
                stage(i - late)
    size = edges_refs[0].shape[0]
    for k, ref in enumerate(edges_refs):
        ref[...] = edge_scr[k * size : (k + 1) * size, :].astype(BF16)


def close_gate_kernel(mine_ref, theirs_ref, weight_ref, mine_gate_ref, theirs_gate_ref):
    for pair_ref, gate_ref in ((mine_ref, mine_gate_ref), (theirs_ref, theirs_gate_ref)):
        for i in range(pair_ref.shape[0]):
            normed = normalize(pair_ref[i]).astype(BF16)
            gate_ref[i] = sigmoid(mm(normed, weight_ref[...]))


def triangle_kernel(per, rows, places, in_ref, out_ref, in_scr, out_scr):
    n = in_ref.shape[0]
    residues = n * rows
    in_scr[...] = in_ref[...].astype(F32)

    def whole(at):
        tiles = []
        for t, (_, side, mate) in enumerate(places):
            pair = []
            for k in range(2):
                source, shift = (t, 0) if side == k else (mate, rows)
                pair.append(in_scr[source, at + shift : at + shift + rows, :])
            tiles.append(jnp.concatenate(pair, axis=1))
        return jnp.concatenate(tiles, axis=0).astype(BF16)

    for c in range(per):
        left = whole(c * 2 * rows)
        right = whole((per + c) * 2 * rows)
        out_scr[:, c * rows : (c + 1) * rows, :] = mm(left, right, NT).reshape(n, rows, residues)
    out_ref[...] = out_scr[...].astype(BF16)


def plain_triangle_kernel(left_ref, right_ref, out_ref):
    for c in range(left_ref.shape[0]):
        out_ref[c] = mm(left_ref[c], right_ref[c], NT).astype(BF16)


def close_kernel(
    side_ref, mine_ref, theirs_ref, mine_gate_ref, theirs_gate_ref, weight_ref, *rest
):
    count = (len(rest) - 1) // 2
    in_refs, out_ref, scrs = rest[:count], rest[count], rest[count + 1 :]
    rows, columns, channels = mine_ref.shape
    for ref, scr in zip(in_refs, scrs):
        fill(scr, ref[...].astype(F32))
    side = side_ref[0]
    for half, pair_ref, gate_ref in (
        (side, mine_ref, mine_gate_ref),
        (1 - side, theirs_ref, theirs_gate_ref),
    ):
        at = pl.multiple_of(half * columns, columns)
        for i in range(rows):
            piece = [scr[half, pl.ds(i, channels // count, stride=rows), :] for scr in scrs]
            piece = jnp.concatenate(piece, axis=0)
            update = mm(normalize(piece, axis=0).astype(BF16), weight_ref[...], TN)
            out_ref[i, pl.ds(at, columns), :] = (
                pair_ref[i].astype(F32) + gate_ref[i] * update
            ).astype(BF16)


def per_device(
    branch,
    dap,
    homolog_embedding,
    couple_embedding,
    homolog_present,
    observed_position,
    couple_logit_kernel,
    lookup_kernels,
    heads_sigmoid_kernel,
    heads_merge_kernel,
    tensor_halves_kernel,
    tensor_merge_kernel,
    edge_entry_kernel,
    closing_sigmoid_kernel,
    closing_merge_kernel,
):
    n = branch * dap
    rows, residues, channels = couple_embedding.shape
    seqs = homolog_embedding.shape[0]
    features = homolog_embedding.shape[2]
    heads = couple_logit_kernel.shape[1]
    inner = heads_sigmoid_kernel.shape[1]
    width = tensor_halves_kernel.shape[1] // 2
    per = channels // n
    half = residues // 2
    block = 2 * rows

    chunks = 1
    some = per // chunks
    places = [((t // dap) % 2, (t // dap // 2) % 2, (t // dap ^ 2) * dap + t % dap) for t in range(n)]
    me = lax.axis_index("branch").astype(jnp.int32)
    core = (me % 2).reshape(1)
    side = (me // 2 % 2).reshape(1)
    place = lax.axis_index("dap").astype(jnp.int32)
    first_mine = (me * dap + place) * rows
    first_theirs = ((me ^ 2) * dap + place) * rows
    chip = [(b, b ^ 1) for b in range(branch)]
    across = [(b, b ^ 2) for b in range(branch)]

    def exchange(values):
        return lax.all_to_all(values, EVERY, split_axis=0, concat_axis=0, tiled=True)

    def permute(values, pairs):
        return lax.ppermute(values, "branch", pairs)

    left_w, right_w, keep = call(
        functools.partial(prepare_small_kernel, seqs),
        (
            jax.ShapeDtypeStruct((seqs, features, seqs * width), BF16),
            jax.ShapeDtypeStruct((width, features), BF16),
            jax.ShapeDtypeStruct(homolog_present.shape, homolog_present.dtype),
        ),
        (tensor_halves_kernel.T, stay(homolog_present)),
    )
    table, value_w, gate_w, final_w = call(
        functools.partial(prepare_large_kernel, chunks, per),
        (
            jax.ShapeDtypeStruct((2, channels, width // 2 * width), BF16),
            jax.ShapeDtypeStruct((2 * channels, channels), BF16),
            jax.ShapeDtypeStruct((2 * channels, channels), BF16),
            jax.ShapeDtypeStruct((channels, channels), BF16),
        ),
        (tensor_merge_kernel, edge_entry_kernel, closing_merge_kernel),
        [
            VMEM((width * width, channels), F32),
            VMEM((4 * channels, channels), F32),
            VMEM((2 * channels, channels), F32),
        ],
    )

    half_heads = heads // 2
    message, couple_mine, couple_send = call(
        functools.partial(bias_kernel, [place[0] for place in places]),
        (
            jax.ShapeDtypeStruct((n, half_heads * rows, residues), BF16),
            jax.ShapeDtypeStruct((rows, half, channels), BF16),
            jax.ShapeDtypeStruct((rows, half, channels), BF16),
        ),
        (side, stay(couple_embedding), stay(couple_logit_kernel.T)),
        [sheets(heads * rows, residues)],
        in_specs=[sspec(), vspec(), vspec()],
    )
    own_bias = exchange(message)
    raw = rows % 8 == 0
    if not raw:
        own_bias = own_bias.reshape(n, half_heads, rows, residues)
        own_bias = own_bias.transpose(1, 0, 2, 3).reshape(half_heads, residues, residues)
    other_bias = permute(own_bias, chip)
    couple_theirs = permute(couple_send, across)

    def whole(*shape):
        return pl.BlockSpec(shape, lambda s: (0,) * len(shape))

    def per_seq(batch, *shape):
        return pl.BlockSpec((batch, *shape), lambda s: (s,) + (0,) * len(shape))

    *parts, gates = pl.pallas_call(
        project_kernel,
        grid=(seqs,),
        out_shape=(
            jax.ShapeDtypeStruct((seqs, residues, inner), BF16),
            jax.ShapeDtypeStruct((seqs, inner, residues), BF16),
            jax.ShapeDtypeStruct((seqs, residues, inner), BF16),
            jax.ShapeDtypeStruct((seqs, residues, inner), F32),
        ),
        in_specs=[
            per_seq(1, residues, features),
            whole(features, 3 * inner),
            whole(features, inner),
        ],
        out_specs=(
            per_seq(1, residues, inner),
            per_seq(1, inner, residues),
            per_seq(1, residues, inner),
            per_seq(1, residues, inner),
        ),
        name="project",
        compiler_params=room(16),
        cost_estimate=pl.CostEstimate(flops=2**29, bytes_accessed=2**22, transcendentals=0),
    )(stay(homolog_embedding), stay(lookup_kernels), stay(heads_sigmoid_kernel))
    span = seqs * width // 2
    depth = span + block + 2 * seqs
    anywhere = pl.BlockSpec(memory_space=pl.ANY)
    new_shape = (seqs, residues, features)
    homolog_refreshed, message = pl.pallas_call(
        functools.partial(attend_kernel, heads, places, raw),
        out_shape=(
            jax.ShapeDtypeStruct(new_shape, BF16),
            jax.ShapeDtypeStruct((n, depth, half), BF16),
        ),
        in_specs=[sspec()] + [vspec()] * 6 + [anywhere] * 5,
        out_specs=(anywhere, anywhere),
        scratch_shapes=[
            VMEM(new_shape, BF16),
            VMEM((seqs, residues, inner), BF16),
            VMEM((seqs, inner, residues), BF16),
            VMEM((seqs, residues, inner), BF16),
            VMEM((seqs, residues, inner), F32),
            VMEM(new_shape, BF16),
            VMEM((n, depth, half), BF16),
            VMEM((residues, seqs * width), F32),
            VMEM((heads, residues, residues), F32),
            VMEM((half_heads * residues, half), BF16),
            pltpu.SemaphoreType.DMA((5, seqs)),
            pltpu.SemaphoreType.DMA((seqs,)),
            pltpu.SemaphoreType.DMA((seqs + 1,)),
        ],
        name="attend",
        compiler_params=room(24),
        cost_estimate=pl.CostEstimate(flops=2**31, bytes_accessed=2**22, transcendentals=0),
    )(
        core,
        keep,
        own_bias,
        other_bias,
        heads_merge_kernel,
        left_w,
        right_w,
        stay(homolog_embedding),
        *(stay(values) for values in parts),
        stay(gates),
    )

    own = exchange(message)
    other = permute(own, chip)
    firsts = (first_mine.reshape(1), first_theirs.reshape(1))
    left, scale, marks, update = call(
        functools.partial(outer_own_kernel, seqs, width, rows),
        (
            jax.ShapeDtypeStruct((block * width, n * seqs), BF16),
            jax.ShapeDtypeStruct((-(-block // 8) * 8, half), F32),
            jax.ShapeDtypeStruct((-(-block // 8) * 8, half), F32),
            jax.ShapeDtypeStruct((block // 2, channels, 2 * half), F32),
        ),
        (core, side, *firsts, own, table, stay(observed_position.reshape(1, residues))),
        [
            VMEM((n * span, half), F32),
            VMEM((n * (depth - span), half), F32),
            VMEM((block, width // 2 * width, half), BF16),
        ],
        need=16,
        in_specs=[sspec()] * 4 + [vspec()] * 3,
        flops=2**30,
    )
    piece = jax.ShapeDtypeStruct((rows, half, channels), BF16)
    pair_mine, pair_send, *edges = call(
        functools.partial(outer_kernel, seqs, width),
        (piece, piece)
        + (jax.ShapeDtypeStruct((2 * channels * block // chunks, half), BF16),) * chunks,
        (
            core,
            other,
            left,
            scale,
            marks,
            update,
            couple_mine,
            couple_theirs,
            table,
            value_w,
            gate_w,
        ),
        [
            VMEM((n * span, half), F32),
            VMEM((block, width // 2 * width, half), BF16),
            VMEM((2 * channels * block, half), F32),
        ],
        need=20,
        in_specs=[sspec()] + [vspec()] * 10,
        flops=2**31,
    )

    received = [exchange(values.reshape(n, 2 * some * block, half)) for values in edges]
    pair_theirs = permute(pair_send, across)
    gate_piece = jax.ShapeDtypeStruct((rows, half, channels), F32)
    gate_mine, gate_theirs = call(
        close_gate_kernel,
        (gate_piece, gate_piece),
        (pair_mine, pair_theirs, closing_sigmoid_kernel),
        flops=2**27,
    )

    def triangle(values):
        if rows % 8 == 0:
            return call(
                functools.partial(triangle_kernel, some, rows, places),
                jax.ShapeDtypeStruct((n, some * rows, residues), BF16),
                (values,),
                [
                    VMEM((n, 2 * some * block, half), F32),
                    VMEM((n, some * rows, residues), F32),
                ],
                need=12,
                flops=2**28,
            )
        both = values.reshape(branch // 4, 2, 2, dap, 2, some, 2, rows, half)
        both = jnp.stack([both[:, 0], both[:, 1, :, :, :, :, ::-1]], axis=1)
        both = both.transpose(4, 5, 0, 6, 2, 3, 7, 1, 8).reshape(2, some, residues, residues)
        combined = call(
            plain_triangle_kernel,
            jax.ShapeDtypeStruct((some, residues, residues), BF16),
            (both[0], both[1]),
            need=12,
            flops=2**28,
        )
        combined = combined.reshape(some, n, rows, residues).transpose(1, 0, 2, 3)
        return combined.reshape(n, some * rows, residues)

    returned = []
    for values in received:
        combined = triangle(values)
        combined = exchange(combined)
        returned.append(combined.reshape(n * some * rows, residues))
    pair_output = call(
        close_kernel,
        jax.ShapeDtypeStruct((rows, residues, channels), BF16),
        (side, pair_mine, pair_theirs, gate_mine, gate_theirs, final_w, *returned),
        [sheets(n * some * rows, residues) for _ in returned],
        in_specs=[sspec()] + [vspec()] * (5 + len(returned)),
        flops=2**27,
    )
    return (homolog_refreshed, pair_output)


def solution(mesh):
    split = P(EVERY, None, None)
    in_specs = (split, split, P(EVERY, None)) + (P(),) * 10

    def body(*args):
        return per_device(mesh.shape["branch"], mesh.shape["dap"], *args)

    return jax.shard_map(
        body, mesh=mesh, in_specs=in_specs, out_specs=(split, split), check_vma=False
    )
```

```python
import functools
import math

import jax
import jax.numpy as jnp
from jax import lax
from jax.experimental import pallas as pl
from jax.experimental.pallas import tpu as pltpu
from jax.sharding import PartitionSpec as P


EPSILON = 1e-05
LOG2E = 1.4426950408889634
EVERY = ("branch", "dap")
VMEM = pltpu.VMEM
F32 = jnp.float32
BF16 = jnp.bfloat16

NT = (((1,), (1,)), ((), ()))
TN = (((0,), (0,)), ((), ()))
NN = (((1,), (0,)), ((), ()))


def mm(a, b, dims=NN):
    return lax.dot_general(a, b, dims, preferred_element_type=F32)


def normalize(values, axis=-1):
    values = values.astype(F32)
    centred = values - jnp.mean(values, axis=axis, keepdims=True)
    spread = jnp.mean(centred * centred, axis=axis, keepdims=True)
    return centred * lax.rsqrt(spread + EPSILON)


def vspec():
    return pl.BlockSpec(memory_space=VMEM)


def sspec():
    return pl.BlockSpec(memory_space=pltpu.SMEM)


LANES = 128


def room(mebibytes):
    return pltpu.CompilerParams(vmem_limit_bytes=mebibytes * 2**20)


def sheets(rows, columns):
    return VMEM((columns // LANES, rows, LANES), F32)


def put(scr, start, values, stride):
    for k in range(scr.shape[0]):
        part = values[:, k * LANES : (k + 1) * LANES]
        scr[k, pl.ds(start, values.shape[0], stride=stride), :] = part


def take(scr, start, count, stride=1):
    parts = [scr[k, pl.ds(start, count, stride=stride), :] for k in range(scr.shape[0])]
    return parts[0] if len(parts) == 1 else jnp.concatenate(parts, axis=1)


def fill(scr, values):
    for k in range(scr.shape[0]):
        scr[k] = values[:, k * LANES : (k + 1) * LANES]


def stay(values):
    return pltpu.with_memory_space_constraint(values, pltpu.MemorySpace.HBM)


def call(body, out, args, scratch=(), in_specs=None, flops=0, need=8, **kw):
    single = not isinstance(out, (tuple, list))
    return pl.pallas_call(
        body,
        out_shape=out,
        in_specs=in_specs or [vspec() for _ in args],
        out_specs=vspec() if single else tuple(vspec() for _ in out),
        scratch_shapes=list(scratch),
        cost_estimate=pl.CostEstimate(flops=flops, bytes_accessed=2**20, transcendentals=0),
        compiler_params=room(need),
        **kw,
    )(*args)


def sigmoid(values):
    return 0.5 * jnp.tanh(0.5 * values) + 0.5


def bias_kernel(cores, side_ref, couple_ref, weight_ref, out_ref, mine_ref, theirs_ref, scr):
    rows, residues, _ = couple_ref.shape
    heads = weight_ref.shape[0]
    half = residues // 2
    mine = pl.multiple_of(side_ref[0] * half, half)
    theirs = pl.multiple_of((1 - side_ref[0]) * half, half)
    channels = couple_ref.shape[2]
    exact = channels & (channels - 1) == 0
    share = jnp.full((channels, channels), 1.0 / channels, BF16)
    for i in range(rows):
        if exact:
            centred = couple_ref[i].astype(F32) - mm(couple_ref[i], share)
            spread = jnp.mean(centred * centred, axis=-1, keepdims=True)
            normed = (centred * lax.rsqrt(spread + EPSILON)).astype(BF16)
        else:
            normed = normalize(couple_ref[i]).astype(BF16)
        put(scr, i, mm(weight_ref[...], normed, NT), rows)
        mine_ref[i] = couple_ref[i, pl.ds(mine, half), :]
        theirs_ref[i] = couple_ref[i, pl.ds(theirs, half), :]
    part = heads // 2 * rows
    halves = [take(scr, k * part, part).astype(BF16) for k in range(2)]
    for t, core in enumerate(cores):
        out_ref[t] = halves[core]


def prepare_small_kernel(
    seqs, heads, halves_ref, present_ref, left_ref, right_ref, keep_ref, ones_ref
):
    keep_ref[...] = present_ref[...]
    residues, half = ones_ref.shape[0] // (heads // 2), ones_ref.shape[1]
    lane = lax.broadcasted_iota(jnp.int32, (residues, half), 1) // (half // (heads // 2))
    for h in range(heads // 2):
        mine = jnp.where(lane == h, jnp.ones((), BF16), jnp.zeros((), BF16))
        ones_ref[h * residues : (h + 1) * residues, :] = mine
    width = halves_ref.shape[0] // 2
    left = halves_ref[:width].astype(F32).T.astype(BF16)
    for s in range(seqs):
        parts = [left if u == s else jnp.zeros_like(left) for u in range(seqs)]
        left_ref[s] = jnp.concatenate(parts, axis=1)
    right_ref[...] = halves_ref[width:]


def prepare_large_kernel(
    chunks,
    per,
    merge_ref,
    entry_ref,
    close_ref,
    table_ref,
    value_ref,
    gate_ref,
    final_ref,
    merge_scr,
    entry_scr,
    edge_scr,
):
    channels = merge_ref.shape[1]
    width = math.isqrt(merge_ref.shape[0])
    part = width // 2
    merge_scr[...] = merge_ref[...].astype(F32)
    for k in range(2):
        rows = [merge_scr[pl.ds(k * part + q, width, stride=width), :] for q in range(part)]
        table_ref[k] = jnp.concatenate(rows, axis=0).T.astype(BF16)
    for k in range(4):
        entry_scr[k * channels : (k + 1) * channels, :] = (
            entry_ref[:, k * channels : (k + 1) * channels].astype(F32).T
        )
    some = per // chunks
    n = channels // per
    for kind, ref in enumerate((value_ref, gate_ref)):
        for k in range(2):
            for c in range(per):
                source = (2 * k + kind) * channels + c
                at = c // some * n * 2 * some + k * some + c % some
                edge_scr[pl.ds(at, n, stride=2 * some), :] = entry_scr[
                    pl.ds(source, n, stride=per), :
                ]
        ref[...] = edge_scr[...].astype(BF16)
    entry_scr[:channels, :] = close_ref[...].astype(F32)
    for c in range(per):
        at = c // some * n * some + c % some
        edge_scr[pl.ds(at, n, stride=some), :] = entry_scr[pl.ds(c, n, stride=per), :]
    final_ref[...] = edge_scr[:channels, :].astype(BF16)


def project_kernel(seq_ref, qkv_w_ref, gate_w_ref, query_ref, key_ref, value_ref, gate_ref):
    inner = gate_w_ref.shape[1]
    normed = normalize(seq_ref[0]).astype(BF16)
    projected = mm(normed, qkv_w_ref[...])
    query_ref[0] = projected[:, :inner].astype(BF16)
    key_ref[0] = projected[:, inner : 2 * inner].T.astype(BF16)
    value_ref[0] = projected[:, 2 * inner :].astype(BF16)
    gate_ref[0] = sigmoid(mm(normed, gate_w_ref[...]))


def attend_kernel(
    heads,
    places,
    raw,
    core_ref,
    keep_ref,
    own_ref,
    other_ref,
    merge_ref,
    left_w_ref,
    right_w_ref,
    ones_scr,
    *rest,
):
    sources, (new_out, message_out) = rest[:5], rest[5:7]
    seq_ref, query_ref, key_ref, value_ref, gate_ref = held_refs = rest[7:12]
    new_ref, message_ref, left_scr, bias_scr, in_sems, new_sems, message_sems = rest[12:]
    batch = seqs = keep_ref.shape[0]
    arrivals = [
        [
            pltpu.make_async_copy(source.at[u], held.at[u], in_sems.at[k, u])
            for k, (source, held) in enumerate(zip(sources, held_refs))
        ]
        for u in range(seqs)
    ]
    for copies in arrivals:
        for copy in copies:
            copy.start()
    core = core_ref[0]
    inner = gate_ref.shape[2]
    residues = gate_ref.shape[1]
    half = inner // 2
    head_width = inner // heads
    scale = head_width ** (-0.5)
    some_heads = heads // 2
    zero = jnp.zeros((), BF16)
    blank = jnp.zeros((head_width, residues), BF16)
    lane_half = lax.broadcasted_iota(jnp.int32, (residues, half), 1) // head_width

    width = right_w_ref.shape[0]
    part = width // 2
    columns = message_ref.shape[2]
    span = seqs * part
    first_lane = lax.broadcasted_iota(jnp.int32, (residues, half), 1) == 0
    flat = jnp.where(first_lane, jnp.ones((), BF16), zero)
    first_row = lax.broadcasted_iota(jnp.int32, (head_width, residues), 0) == 0

    pieces = message_ref.shape[1] % 8 == 0 and part % 16 == 0

    def departure(u):
        rows = pl.ds(u * part, part)
        return pltpu.make_async_copy(
            message_ref.at[:, rows, :], message_out.at[:, rows, :], message_sems.at[u]
        )

    def run(plain):
        waiting = []

        def advance():
            if waiting:
                waiting.pop(0)()

        def finish(u, mixed):
            s = u
            present = keep_ref[pl.ds(s, 1), :].astype(F32)
            held = {}

            def merge():
                first = jnp.where(core == 0, mixed[0], mixed[1])
                second = jnp.where(core == 0, mixed[1], mixed[0])
                attended = (jnp.concatenate([first, second], axis=1) * gate_ref[u]).astype(BF16)
                updated = seq_ref[u].astype(F32) + mm(attended, merge_ref[...])
                held["updated"] = updated.astype(BF16)
                new_ref[u] = held["updated"]
                pltpu.make_async_copy(new_ref.at[u], new_out.at[u], new_sems.at[u]).start()

            def norm():
                held["normed"] = normalize(held["updated"]).astype(BF16)

            def right():
                values = (mm(right_w_ref[...], held["normed"], NT) * present).astype(BF16)
                for t, (core_of, side, _) in enumerate(places):
                    message_ref[t, s * part : (s + 1) * part, :] = values[
                        core_of * part : (core_of + 1) * part, side * columns : (side + 1) * columns
                    ]
                if pieces:
                    departure(s).start()

            def left():
                present_column = jnp.broadcast_to(present, (8, residues)).T[:, :1]
                left_scr[...] += mm(held["normed"], left_w_ref[s]) * present_column

            waiting.extend([merge, norm, right, left])

        for u in range(batch):
            for copy in arrivals[u]:
                copy.wait()
            keep = keep_ref[pl.ds(u, 1), :]
            if plain:
                masking = jnp.where(keep == 1, 0.0, -1000000000.0).astype(F32)
            else:
                mask = jnp.where(first_row & (keep == 0), -1e30, 0.0).astype(BF16)
            mixed = []
            for k, group in ((0, core), (1, 1 - core)):
                queries, values = (
                    jnp.where(group == 0, ref[u, :, :half], ref[u, :, half:])
                    for ref in (query_ref, value_ref)
                )
                keys = jnp.where(group == 0, key_ref[u, :half, :], key_ref[u, half:, :])
                if not plain:
                    queries = jnp.concatenate([queries, flat], axis=1)
                weights, tables = [], []
                for h in range(some_heads):
                    only = [
                        keys[g * head_width : (g + 1) * head_width] if g == h else blank
                        for g in range(some_heads)
                    ]
                    bias = bias_scr[k * some_heads + h]
                    if plain:
                        logits = mm(queries, jnp.concatenate(only, axis=0)) * scale
                        logits = logits + bias + masking
                        logits = logits - jnp.max(logits, axis=-1, keepdims=True)
                        weights.append(jnp.exp(logits).astype(BF16))
                    else:
                        only += [mask] + [blank] * (some_heads - 1)
                        logits = mm(queries, jnp.concatenate(only, axis=0)) * (scale * LOG2E)
                        logits = logits + bias
                        logits = logits - jnp.max(logits, axis=-1, keepdims=True)
                        weights.append(jnp.exp2(logits).astype(BF16))
                    tables.append(jnp.where(lane_half == h, values, zero))
                    if h % 2 == 1:
                        advance()
                table = jnp.concatenate([jnp.concatenate(tables, axis=0), ones_scr[...]], axis=1)
                total = mm(jnp.concatenate(weights, axis=1), table)
                mixed.append(total[:, :half] * (1.0 / total[:, half:]))
            finish(u, mixed)
        while waiting:
            advance()

    some = jnp.max(keep_ref[...].astype(F32), axis=1, keepdims=True)
    plain = jnp.min(some) == 0.0

    left_scr[...] = jnp.zeros_like(left_scr)
    unit = jnp.where(plain, 1.0, LOG2E)
    for k, ref in enumerate((own_ref, other_ref)):
        for h in range(some_heads):
            if raw:
                rows = residues // len(places)
                tile = ref[:, h * rows : (h + 1) * rows, :].astype(F32)
                tile = tile.reshape(residues, residues)
            else:
                tile = ref[h].astype(F32)
            bias_scr[k * some_heads + h] = tile * unit

    pl.when(plain)(functools.partial(run, True))
    pl.when(jnp.logical_not(plain))(functools.partial(run, False))

    rows = residues // len(places)
    marks = keep_ref[...].astype(F32)
    marks = jnp.concatenate(
        [marks[:, k * columns : (k + 1) * columns] for k in range(2)], axis=0
    ).astype(BF16)
    for t, (_, _, mate) in enumerate(places):
        tile = jnp.concatenate([left_scr[u * rows : (u + 1) * rows, :] for u in (t, mate)], axis=0)
        message_ref[t, span : span + 2 * rows, :] = tile.astype(BF16)
        message_ref[t, span + 2 * rows :, :] = marks
    if pieces:
        last = pltpu.make_async_copy(
            message_ref.at[:, span:, :], message_out.at[:, span:, :], message_sems.at[seqs]
        )
    else:
        last = pltpu.make_async_copy(message_ref, message_out, message_sems.at[seqs])
    last.start()
    for u in range(seqs):
        pltpu.make_async_copy(new_ref.at[u], new_out.at[u], new_sems.at[u]).wait()
        if pieces:
            departure(u).wait()
    last.wait()


def multiply(seqs, width, left, ref, scr, products):
    n, _, columns = ref.shape
    part = width // 2
    span = seqs * part
    block = left.shape[0] // width
    scr[...] = ref[:, :span, :].astype(F32).reshape(n * span, columns)
    for q in range(0, part, 2):
        pair = [
            jnp.concatenate(
                [scr[pl.ds(s * part + q + d, n, stride=span), :] for s in range(seqs)], axis=0
            ).astype(BF16)
            for d in range(2)
        ]
        outer = mm(left, jnp.concatenate(pair, axis=1)).astype(BF16)
        for d in range(2):
            at = (q + d) * width
            for i in range(block):
                products[i, at : at + width, :] = outer[
                    i * width : (i + 1) * width, d * columns : (d + 1) * columns
                ]


def outer_own_kernel(
    seqs,
    width,
    rows,
    core_ref,
    side_ref,
    first_mine_ref,
    first_theirs_ref,
    own_ref,
    table_ref,
    observed_ref,
    left_ref,
    scale_ref,
    marks_ref,
    update_ref,
    right_scr,
    small_scr,
    products,
):
    n, depth, columns = own_ref.shape
    block = 2 * rows
    total_seqs = n * seqs
    span = seqs * width // 2
    side, first_mine, first_theirs = side_ref[0], first_mine_ref[0], first_theirs_ref[0]
    extra = depth - span
    small_scr[...] = own_ref[:, span:, :].astype(F32).reshape(n * extra, columns)
    left_rows = []
    for i in range(block):
        piece = small_scr[pl.ds(i, n, stride=extra), :]
        for s in range(seqs):
            left_rows.append(piece[:, s * width : (s + 1) * width])
    left_all = jnp.concatenate(left_rows, axis=0).T
    left = jnp.concatenate(
        [left_all[:, i * total_seqs : (i + 1) * total_seqs] for i in range(block)], axis=0
    ).astype(BF16)
    left_ref[...] = left
    keep_halves = []
    for k in range(2):
        at = block + k * seqs
        keep_halves.append(
            jnp.concatenate(
                [small_scr[pl.ds(at + s, n, stride=extra), :] for s in range(seqs)], axis=0
            )
        )
    keep_columns = jnp.where(side == 0, keep_halves[0], keep_halves[1]).astype(BF16)
    keep = jnp.concatenate(keep_halves, axis=1).astype(BF16)
    pad = scale_ref.shape[0]
    order = lax.broadcasted_iota(jnp.int32, (pad, 2 * columns), 0)
    row_ids = jnp.where(order < rows, first_mine + order, first_theirs + order - rows)
    chosen = (row_ids == lax.broadcasted_iota(jnp.int32, (pad, 2 * columns), 1)).astype(BF16)
    counts = mm(mm(chosen, keep, NT).astype(BF16), keep_columns)
    scale_ref[...] = 1.0 / jnp.maximum(counts, 1.0)
    observed = observed_ref[...].astype(F32)
    row_marks = mm(chosen, jnp.broadcast_to(observed, (8, 2 * columns)).astype(BF16), NT)[:, :1]
    column_marks = jnp.where(side == 0, observed[:, :columns], observed[:, columns:])
    marks_ref[...] = row_marks * column_marks
    multiply(seqs, width, left, own_ref, right_scr, products)
    table = table_ref[core_ref[0]]
    for i in range(0, block, 2):
        update_ref[i // 2] = mm(table, jnp.concatenate([products[i], products[i + 1]], axis=1))


def outer_kernel(
    seqs,
    width,
    core_ref,
    other_ref,
    left_ref,
    scale_ref,
    marks_ref,
    own_update_ref,
    couple_mine_ref,
    couple_theirs_ref,
    table_ref,
    value_w_ref,
    gate_w_ref,
    pair_mine_ref,
    pair_theirs_ref,
    *rest,
):
    edges_refs, (right_scr, products, edge_scr) = rest[:-3], rest[-3:]
    rows, columns, channels = couple_mine_ref.shape
    block = 2 * rows
    multiply(seqs, width, left_ref[...], other_ref, right_scr, products)
    scale = scale_ref[...]
    table = table_ref[1 - core_ref[0]]
    updates, norms = {}, {}

    def project(i):
        part = mm(table, jnp.concatenate([products[i], products[i + 1]], axis=1))
        updates[i] = own_update_ref[i // 2] + part

    def add(i):
        normed = []
        for d in range(2):
            piece = updates[i][:, d * columns : (d + 1) * columns] * scale[i + d : i + d + 1, :]
            couple_ref, pair_ref = (
                (couple_mine_ref, pair_mine_ref)
                if i + d < rows
                else (couple_theirs_ref, pair_theirs_ref)
            )
            r = (i + d) % rows
            pair = (couple_ref[r].astype(F32) + piece.T).astype(BF16)
            pair_ref[r] = pair
            normed.append(normalize(pair).astype(BF16))
        norms[i] = jnp.concatenate(normed, axis=0)

    def edge(i):
        values = mm(value_w_ref[...], norms[i], NT) * sigmoid(mm(gate_w_ref[...], norms[i], NT))
        for d in range(2):
            mark = marks_ref[i + d : i + d + 1, :]
            edge_scr[pl.ds(i + d, 2 * channels, stride=block), :] = (
                values[:, d * columns : (d + 1) * columns] * mark
            )

    for i in range(0, block + 4, 2):
        for stage, late in ((project, 0), (add, 2), (edge, 4)):
            if 0 <= i - late < block:
                stage(i - late)
    size = edges_refs[0].shape[0]
    for k, ref in enumerate(edges_refs):
        ref[...] = edge_scr[k * size : (k + 1) * size, :].astype(BF16)


def close_gate_kernel(mine_ref, theirs_ref, weight_ref, mine_gate_ref, theirs_gate_ref):
    for pair_ref, gate_ref in ((mine_ref, mine_gate_ref), (theirs_ref, theirs_gate_ref)):
        for i in range(pair_ref.shape[0]):
            normed = normalize(pair_ref[i]).astype(BF16)
            gate_ref[i] = sigmoid(mm(normed, weight_ref[...]))


def triangle_kernel(per, rows, places, in_ref, out_ref, in_scr, out_scr):
    n = in_ref.shape[0]
    residues = n * rows
    in_scr[...] = in_ref[...].astype(F32)

    def whole(at):
        tiles = []
        for t, (_, side, mate) in enumerate(places):
            pair = []
            for k in range(2):
                source, shift = (t, 0) if side == k else (mate, rows)
                pair.append(in_scr[source, at + shift : at + shift + rows, :])
            tiles.append(jnp.concatenate(pair, axis=1))
        return jnp.concatenate(tiles, axis=0).astype(BF16)

    for c in range(per):
        left = whole(c * 2 * rows)
        right = whole((per + c) * 2 * rows)
        out_scr[:, c * rows : (c + 1) * rows, :] = mm(left, right, NT).reshape(n, rows, residues)
    out_ref[...] = out_scr[...].astype(BF16)


def plain_triangle_kernel(left_ref, right_ref, out_ref):
    for c in range(left_ref.shape[0]):
        out_ref[c] = mm(left_ref[c], right_ref[c], NT).astype(BF16)


def close_kernel(
    side_ref, mine_ref, theirs_ref, mine_gate_ref, theirs_gate_ref, weight_ref, *rest
):
    count = (len(rest) - 1) // 2
    in_refs, out_ref, scrs = rest[:count], rest[count], rest[count + 1 :]
    rows, columns, channels = mine_ref.shape
    for ref, scr in zip(in_refs, scrs):
        fill(scr, ref[...].astype(F32))
    side = side_ref[0]
    for half, pair_ref, gate_ref in (
        (side, mine_ref, mine_gate_ref),
        (1 - side, theirs_ref, theirs_gate_ref),
    ):
        at = pl.multiple_of(half * columns, columns)
        for i in range(rows):
            piece = [scr[half, pl.ds(i, channels // count, stride=rows), :] for scr in scrs]
            piece = jnp.concatenate(piece, axis=0)
            update = mm(normalize(piece, axis=0).astype(BF16), weight_ref[...], TN)
            out_ref[i, pl.ds(at, columns), :] = (
                pair_ref[i].astype(F32) + gate_ref[i] * update
            ).astype(BF16)


def per_device(
    branch,
    dap,
    homolog_embedding,
    couple_embedding,
    homolog_present,
    observed_position,
    couple_logit_kernel,
    lookup_kernels,
    heads_sigmoid_kernel,
    heads_merge_kernel,
    tensor_halves_kernel,
    tensor_merge_kernel,
    edge_entry_kernel,
    closing_sigmoid_kernel,
    closing_merge_kernel,
):
    n = branch * dap
    rows, residues, channels = couple_embedding.shape
    seqs = homolog_embedding.shape[0]
    features = homolog_embedding.shape[2]
    heads = couple_logit_kernel.shape[1]
    inner = heads_sigmoid_kernel.shape[1]
    width = tensor_halves_kernel.shape[1] // 2
    per = channels // n
    half = residues // 2
    block = 2 * rows

    chunks = 1
    some = per // chunks
    places = [((t // dap) % 2, (t // dap // 2) % 2, (t // dap ^ 2) * dap + t % dap) for t in range(n)]
    me = lax.axis_index("branch").astype(jnp.int32)
    core = (me % 2).reshape(1)
    side = (me // 2 % 2).reshape(1)
    place = lax.axis_index("dap").astype(jnp.int32)
    first_mine = (me * dap + place) * rows
    first_theirs = ((me ^ 2) * dap + place) * rows
    chip = [(b, b ^ 1) for b in range(branch)]
    across = [(b, b ^ 2) for b in range(branch)]

    def exchange(values):
        return lax.all_to_all(values, EVERY, split_axis=0, concat_axis=0, tiled=True)

    def permute(values, pairs):
        return lax.ppermute(values, "branch", pairs)

    left_w, right_w, keep, ones = call(
        functools.partial(prepare_small_kernel, seqs, heads),
        (
            jax.ShapeDtypeStruct((seqs, features, seqs * width), BF16),
            jax.ShapeDtypeStruct((width, features), BF16),
            jax.ShapeDtypeStruct(homolog_present.shape, homolog_present.dtype),
            jax.ShapeDtypeStruct((heads // 2 * residues, inner // 2), BF16),
        ),
        (tensor_halves_kernel.T, stay(homolog_present)),
    )
    table, value_w, gate_w, final_w = call(
        functools.partial(prepare_large_kernel, chunks, per),
        (
            jax.ShapeDtypeStruct((2, channels, width // 2 * width), BF16),
            jax.ShapeDtypeStruct((2 * channels, channels), BF16),
            jax.ShapeDtypeStruct((2 * channels, channels), BF16),
            jax.ShapeDtypeStruct((channels, channels), BF16),
        ),
        (tensor_merge_kernel, edge_entry_kernel, closing_merge_kernel),
        [
            VMEM((width * width, channels), F32),
            VMEM((4 * channels, channels), F32),
            VMEM((2 * channels, channels), F32),
        ],
    )

    half_heads = heads // 2
    message, couple_mine, couple_send = call(
        functools.partial(bias_kernel, [place[0] for place in places]),
        (
            jax.ShapeDtypeStruct((n, half_heads * rows, residues), BF16),
            jax.ShapeDtypeStruct((rows, half, channels), BF16),
            jax.ShapeDtypeStruct((rows, half, channels), BF16),
        ),
        (side, stay(couple_embedding), stay(couple_logit_kernel.T)),
        [sheets(heads * rows, residues)],
        in_specs=[sspec(), vspec(), vspec()],
    )
    own_bias = exchange(message)
    raw = rows % 8 == 0
    if not raw:
        own_bias = own_bias.reshape(n, half_heads, rows, residues)
        own_bias = own_bias.transpose(1, 0, 2, 3).reshape(half_heads, residues, residues)
    other_bias = permute(own_bias, chip)
    couple_theirs = permute(couple_send, across)

    def whole(*shape):
        return pl.BlockSpec(shape, lambda s: (0,) * len(shape))

    def per_seq(batch, *shape):
        return pl.BlockSpec((batch, *shape), lambda s: (s,) + (0,) * len(shape))

    *parts, gates = pl.pallas_call(
        project_kernel,
        grid=(seqs,),
        out_shape=(
            jax.ShapeDtypeStruct((seqs, residues, inner), BF16),
            jax.ShapeDtypeStruct((seqs, inner, residues), BF16),
            jax.ShapeDtypeStruct((seqs, residues, inner), BF16),
            jax.ShapeDtypeStruct((seqs, residues, inner), F32),
        ),
        in_specs=[
            per_seq(1, residues, features),
            whole(features, 3 * inner),
            whole(features, inner),
        ],
        out_specs=(
            per_seq(1, residues, inner),
            per_seq(1, inner, residues),
            per_seq(1, residues, inner),
            per_seq(1, residues, inner),
        ),
        name="project",
        compiler_params=room(16),
        cost_estimate=pl.CostEstimate(flops=2**29, bytes_accessed=2**22, transcendentals=0),
    )(stay(homolog_embedding), stay(lookup_kernels), stay(heads_sigmoid_kernel))
    span = seqs * width // 2
    depth = span + block + 2 * seqs
    anywhere = pl.BlockSpec(memory_space=pl.ANY)
    new_shape = (seqs, residues, features)
    homolog_refreshed, message = pl.pallas_call(
        functools.partial(attend_kernel, heads, places, raw),
        out_shape=(
            jax.ShapeDtypeStruct(new_shape, BF16),
            jax.ShapeDtypeStruct((n, depth, half), BF16),
        ),
        in_specs=[sspec()] + [vspec()] * 7 + [anywhere] * 5,
        out_specs=(anywhere, anywhere),
        scratch_shapes=[
            VMEM(new_shape, BF16),
            VMEM((seqs, residues, inner), BF16),
            VMEM((seqs, inner, residues), BF16),
            VMEM((seqs, residues, inner), BF16),
            VMEM((seqs, residues, inner), F32),
            VMEM(new_shape, BF16),
            VMEM((n, depth, half), BF16),
            VMEM((residues, seqs * width), F32),
            VMEM((heads, residues, residues), F32),
            pltpu.SemaphoreType.DMA((5, seqs)),
            pltpu.SemaphoreType.DMA((seqs,)),
            pltpu.SemaphoreType.DMA((seqs + 1,)),
        ],
        name="attend",
        compiler_params=room(24),
        cost_estimate=pl.CostEstimate(flops=2**31, bytes_accessed=2**22, transcendentals=0),
    )(
        core,
        keep,
        own_bias,
        other_bias,
        heads_merge_kernel,
        left_w,
        right_w,
        ones,
        stay(homolog_embedding),
        *(stay(values) for values in parts),
        stay(gates),
    )

    own = exchange(message)
    other = permute(own, chip)
    firsts = (first_mine.reshape(1), first_theirs.reshape(1))
    left, scale, marks, update = call(
        functools.partial(outer_own_kernel, seqs, width, rows),
        (
            jax.ShapeDtypeStruct((block * width, n * seqs), BF16),
            jax.ShapeDtypeStruct((-(-block // 8) * 8, half), F32),
            jax.ShapeDtypeStruct((-(-block // 8) * 8, half), F32),
            jax.ShapeDtypeStruct((block // 2, channels, 2 * half), F32),
        ),
        (core, side, *firsts, own, table, stay(observed_position.reshape(1, residues))),
        [
            VMEM((n * span, half), F32),
            VMEM((n * (depth - span), half), F32),
            VMEM((block, width // 2 * width, half), BF16),
        ],
        need=16,
        in_specs=[sspec()] * 4 + [vspec()] * 3,
        flops=2**30,
    )
    piece = jax.ShapeDtypeStruct((rows, half, channels), BF16)
    pair_mine, pair_send, *edges = call(
        functools.partial(outer_kernel, seqs, width),
        (piece, piece)
        + (jax.ShapeDtypeStruct((2 * channels * block // chunks, half), BF16),) * chunks,
        (
            core,
            other,
            left,
            scale,
            marks,
            update,
            couple_mine,
            couple_theirs,
            table,
            value_w,
            gate_w,
        ),
        [
            VMEM((n * span, half), F32),
            VMEM((block, width // 2 * width, half), BF16),
            VMEM((2 * channels * block, half), F32),
        ],
        need=20,
        in_specs=[sspec()] + [vspec()] * 10,
        flops=2**31,
    )

    received = [exchange(values.reshape(n, 2 * some * block, half)) for values in edges]
    pair_theirs = permute(pair_send, across)
    gate_piece = jax.ShapeDtypeStruct((rows, half, channels), F32)
    gate_mine, gate_theirs = call(
        close_gate_kernel,
        (gate_piece, gate_piece),
        (pair_mine, pair_theirs, closing_sigmoid_kernel),
        flops=2**27,
    )

    def triangle(values):
        if rows % 8 == 0:
            return call(
                functools.partial(triangle_kernel, some, rows, places),
                jax.ShapeDtypeStruct((n, some * rows, residues), BF16),
                (values,),
                [
                    VMEM((n, 2 * some * block, half), F32),
                    VMEM((n, some * rows, residues), F32),
                ],
                need=12,
                flops=2**28,
            )
        both = values.reshape(branch // 4, 2, 2, dap, 2, some, 2, rows, half)
        both = jnp.stack([both[:, 0], both[:, 1, :, :, :, :, ::-1]], axis=1)
        both = both.transpose(4, 5, 0, 6, 2, 3, 7, 1, 8).reshape(2, some, residues, residues)
        combined = call(
            plain_triangle_kernel,
            jax.ShapeDtypeStruct((some, residues, residues), BF16),
            (both[0], both[1]),
            need=12,
            flops=2**28,
        )
        combined = combined.reshape(some, n, rows, residues).transpose(1, 0, 2, 3)
        return combined.reshape(n, some * rows, residues)

    returned = []
    for values in received:
        combined = triangle(values)
        combined = exchange(combined)
        returned.append(combined.reshape(n * some * rows, residues))
    pair_output = call(
        close_kernel,
        jax.ShapeDtypeStruct((rows, residues, channels), BF16),
        (side, pair_mine, pair_theirs, gate_mine, gate_theirs, final_w, *returned),
        [sheets(n * some * rows, residues) for _ in returned],
        in_specs=[sspec()] + [vspec()] * (5 + len(returned)),
        flops=2**27,
    )
    return (homolog_refreshed, pair_output)


def solution(mesh):
    split = P(EVERY, None, None)
    in_specs = (split, split, P(EVERY, None)) + (P(),) * 10

    def body(*args):
        return per_device(mesh.shape["branch"], mesh.shape["dap"], *args)

    return jax.shard_map(
        body, mesh=mesh, in_specs=in_specs, out_specs=(split, split), check_vma=False
    )
```

```python
import functools
import math

import jax
import jax.numpy as jnp
from jax import lax
from jax.experimental import pallas as pl
from jax.experimental.pallas import tpu as pltpu
from jax.sharding import PartitionSpec as P


EPSILON = 1e-05
LOG2E = 1.4426950408889634
EVERY = ("branch", "dap")
VMEM = pltpu.VMEM
F32 = jnp.float32
BF16 = jnp.bfloat16

NT = (((1,), (1,)), ((), ()))
TN = (((0,), (0,)), ((), ()))
NN = (((1,), (0,)), ((), ()))


def mm(a, b, dims=NN):
    return lax.dot_general(a, b, dims, preferred_element_type=F32)


def normalize(values, axis=-1):
    values = values.astype(F32)
    centred = values - jnp.mean(values, axis=axis, keepdims=True)
    spread = jnp.mean(centred * centred, axis=axis, keepdims=True)
    return centred * lax.rsqrt(spread + EPSILON)


def normalize_rows(values):
    channels = values.shape[-1]
    if channels & (channels - 1):
        return normalize(values)
    share = jnp.full((channels, channels), 1.0 / channels, BF16)
    centred = values.astype(F32) - mm(values, share)
    spread = jnp.mean(centred * centred, axis=-1, keepdims=True)
    return centred * lax.rsqrt(spread + EPSILON)


def vspec():
    return pl.BlockSpec(memory_space=VMEM)


def sspec():
    return pl.BlockSpec(memory_space=pltpu.SMEM)


LANES = 128


def room(mebibytes):
    return pltpu.CompilerParams(vmem_limit_bytes=mebibytes * 2**20)


def sheets(rows, columns):
    return VMEM((columns // LANES, rows, LANES), F32)


def put(scr, start, values, stride):
    for k in range(scr.shape[0]):
        part = values[:, k * LANES : (k + 1) * LANES]
        scr[k, pl.ds(start, values.shape[0], stride=stride), :] = part


def take(scr, start, count, stride=1):
    parts = [scr[k, pl.ds(start, count, stride=stride), :] for k in range(scr.shape[0])]
    return parts[0] if len(parts) == 1 else jnp.concatenate(parts, axis=1)


def fill(scr, values):
    for k in range(scr.shape[0]):
        scr[k] = values[:, k * LANES : (k + 1) * LANES]


def stay(values):
    return pltpu.with_memory_space_constraint(values, pltpu.MemorySpace.HBM)


def call(body, out, args, scratch=(), in_specs=None, flops=0, need=8, **kw):
    single = not isinstance(out, (tuple, list))
    return pl.pallas_call(
        body,
        out_shape=out,
        in_specs=in_specs or [vspec() for _ in args],
        out_specs=vspec() if single else tuple(vspec() for _ in out),
        scratch_shapes=list(scratch),
        cost_estimate=pl.CostEstimate(flops=flops, bytes_accessed=2**20, transcendentals=0),
        compiler_params=room(need),
        **kw,
    )(*args)


def sigmoid(values):
    return 0.5 * jnp.tanh(0.5 * values) + 0.5


def bias_kernel(cores, side_ref, couple_ref, weight_ref, out_ref, mine_ref, theirs_ref, scr):
    rows, residues, _ = couple_ref.shape
    heads = weight_ref.shape[0]
    half = residues // 2
    mine = pl.multiple_of(side_ref[0] * half, half)
    theirs = pl.multiple_of((1 - side_ref[0]) * half, half)
    channels = couple_ref.shape[2]
    exact = channels & (channels - 1) == 0
    share = jnp.full((channels, channels), 1.0 / channels, BF16)
    for i in range(rows):
        if exact:
            centred = couple_ref[i].astype(F32) - mm(couple_ref[i], share)
            spread = jnp.mean(centred * centred, axis=-1, keepdims=True)
            normed = (centred * lax.rsqrt(spread + EPSILON)).astype(BF16)
        else:
            normed = normalize(couple_ref[i]).astype(BF16)
        put(scr, i, mm(weight_ref[...], normed, NT), rows)
        mine_ref[i] = couple_ref[i, pl.ds(mine, half), :]
        theirs_ref[i] = couple_ref[i, pl.ds(theirs, half), :]
    part = heads // 2 * rows
    halves = [take(scr, k * part, part).astype(BF16) for k in range(2)]
    for t, core in enumerate(cores):
        out_ref[t] = halves[core]


def prepare_small_kernel(
    seqs, heads, halves_ref, present_ref, left_ref, right_ref, keep_ref, ones_ref
):
    keep_ref[...] = present_ref[...]
    residues, half = ones_ref.shape[0] // (heads // 2), ones_ref.shape[1]
    lane = lax.broadcasted_iota(jnp.int32, (residues, half), 1) // (half // (heads // 2))
    for h in range(heads // 2):
        mine = jnp.where(lane == h, jnp.ones((), BF16), jnp.zeros((), BF16))
        ones_ref[h * residues : (h + 1) * residues, :] = mine
    width = halves_ref.shape[0] // 2
    left = halves_ref[:width].astype(F32).T.astype(BF16)
    for s in range(seqs):
        parts = [left if u == s else jnp.zeros_like(left) for u in range(seqs)]
        left_ref[s] = jnp.concatenate(parts, axis=1)
    right_ref[...] = halves_ref[width:]


def prepare_large_kernel(
    chunks,
    per,
    merge_ref,
    entry_ref,
    close_ref,
    table_ref,
    value_ref,
    gate_ref,
    final_ref,
    merge_scr,
    entry_scr,
    edge_scr,
):
    channels = merge_ref.shape[1]
    width = math.isqrt(merge_ref.shape[0])
    part = width // 2
    merge_scr[...] = merge_ref[...].astype(F32)
    for k in range(2):
        rows = [merge_scr[pl.ds(k * part + q, width, stride=width), :] for q in range(part)]
        table_ref[k] = jnp.concatenate(rows, axis=0).T.astype(BF16)
    for k in range(4):
        entry_scr[k * channels : (k + 1) * channels, :] = (
            entry_ref[:, k * channels : (k + 1) * channels].astype(F32).T
        )
    some = per // chunks
    n = channels // per
    for kind, ref in enumerate((value_ref, gate_ref)):
        for k in range(2):
            for c in range(per):
                source = (2 * k + kind) * channels + c
                at = c // some * n * 2 * some + k * some + c % some
                edge_scr[pl.ds(at, n, stride=2 * some), :] = entry_scr[
                    pl.ds(source, n, stride=per), :
                ]
        ref[...] = edge_scr[...].astype(BF16)
    entry_scr[:channels, :] = close_ref[...].astype(F32)
    for c in range(per):
        at = c // some * n * some + c % some
        edge_scr[pl.ds(at, n, stride=some), :] = entry_scr[pl.ds(c, n, stride=per), :]
    final_ref[...] = edge_scr[:channels, :].astype(BF16)


def project_kernel(seq_ref, qkv_w_ref, gate_w_ref, query_ref, key_ref, value_ref, gate_ref):
    inner = gate_w_ref.shape[1]
    normed = normalize(seq_ref[0]).astype(BF16)
    projected = mm(normed, qkv_w_ref[...])
    query_ref[0] = projected[:, :inner].astype(BF16)
    key_ref[0] = projected[:, inner : 2 * inner].T.astype(BF16)
    value_ref[0] = projected[:, 2 * inner :].astype(BF16)
    gate_ref[0] = sigmoid(mm(normed, gate_w_ref[...]))


def attend_kernel(
    heads,
    places,
    raw,
    core_ref,
    keep_ref,
    own_ref,
    other_ref,
    merge_ref,
    left_w_ref,
    right_w_ref,
    ones_scr,
    *rest,
):
    sources, (new_out, message_out) = rest[:5], rest[5:7]
    seq_ref, query_ref, key_ref, value_ref, gate_ref = held_refs = rest[7:12]
    new_ref, message_ref, left_scr, bias_scr, in_sems, new_sems, message_sems = rest[12:]
    batch = seqs = keep_ref.shape[0]
    arrivals = [
        [
            pltpu.make_async_copy(source.at[u], held.at[u], in_sems.at[k, u])
            for k, (source, held) in enumerate(zip(sources, held_refs))
        ]
        for u in range(seqs)
    ]
    for copies in arrivals:
        for copy in copies:
            copy.start()
    core = core_ref[0]
    inner = gate_ref.shape[2]
    residues = gate_ref.shape[1]
    half = inner // 2
    head_width = inner // heads
    scale = head_width ** (-0.5)
    some_heads = heads // 2
    zero = jnp.zeros((), BF16)
    blank = jnp.zeros((head_width, residues), BF16)
    lane_half = lax.broadcasted_iota(jnp.int32, (residues, half), 1) // head_width

    width = right_w_ref.shape[0]
    part = width // 2
    columns = message_ref.shape[2]
    span = seqs * part
    first_lane = lax.broadcasted_iota(jnp.int32, (residues, half), 1) == 0
    flat = jnp.where(first_lane, jnp.ones((), BF16), zero)
    first_row = lax.broadcasted_iota(jnp.int32, (head_width, residues), 0) == 0

    pieces = message_ref.shape[1] % 8 == 0 and part % 16 == 0

    def departure(u):
        rows = pl.ds(u * part, part)
        return pltpu.make_async_copy(
            message_ref.at[:, rows, :], message_out.at[:, rows, :], message_sems.at[u]
        )

    def run(plain):
        waiting = []

        def advance():
            if waiting:
                waiting.pop(0)()

        def finish(u, mixed):
            s = u
            present = keep_ref[pl.ds(s, 1), :].astype(F32)
            held = {}

            def merge():
                first = jnp.where(core == 0, mixed[0], mixed[1])
                second = jnp.where(core == 0, mixed[1], mixed[0])
                attended = (jnp.concatenate([first, second], axis=1) * gate_ref[u]).astype(BF16)
                updated = seq_ref[u].astype(F32) + mm(attended, merge_ref[...])
                held["updated"] = updated.astype(BF16)
                new_ref[u] = held["updated"]
                pltpu.make_async_copy(new_ref.at[u], new_out.at[u], new_sems.at[u]).start()

            def norm():
                held["normed"] = normalize_rows(held["updated"]).astype(BF16)

            def right():
                values = (mm(right_w_ref[...], held["normed"], NT) * present).astype(BF16)
                for t, (core_of, side, _) in enumerate(places):
                    message_ref[t, s * part : (s + 1) * part, :] = values[
                        core_of * part : (core_of + 1) * part, side * columns : (side + 1) * columns
                    ]
                if pieces:
                    departure(s).start()

            def left():
                present_column = jnp.broadcast_to(present, (8, residues)).T[:, :1]
                left_scr[...] += mm(held["normed"], left_w_ref[s]) * present_column

            waiting.extend([merge, norm, right, left])

        for u in range(batch):
            for copy in arrivals[u]:
                copy.wait()
            keep = keep_ref[pl.ds(u, 1), :]
            if plain:
                masking = jnp.where(keep == 1, 0.0, -1000000000.0).astype(F32)
            else:
                mask = jnp.where(first_row & (keep == 0), -1e30, 0.0).astype(BF16)
            mixed = []
            for k, group in ((0, core), (1, 1 - core)):
                queries, values = (
                    jnp.where(group == 0, ref[u, :, :half], ref[u, :, half:])
                    for ref in (query_ref, value_ref)
                )
                keys = jnp.where(group == 0, key_ref[u, :half, :], key_ref[u, half:, :])
                if not plain:
                    queries = jnp.concatenate([queries, flat], axis=1)
                weights, tables = [], []
                for h in range(some_heads):
                    only = [
                        keys[g * head_width : (g + 1) * head_width] if g == h else blank
                        for g in range(some_heads)
                    ]
                    bias = bias_scr[k * some_heads + h]
                    if plain:
                        logits = mm(queries, jnp.concatenate(only, axis=0)) * scale
                        logits = logits + bias + masking
                        logits = logits - jnp.max(logits, axis=-1, keepdims=True)
                        weights.append(jnp.exp(logits).astype(BF16))
                    else:
                        only += [mask] + [blank] * (some_heads - 1)
                        logits = mm(queries, jnp.concatenate(only, axis=0)) * (scale * LOG2E)
                        logits = logits + bias
                        logits = logits - jnp.max(logits, axis=-1, keepdims=True)
                        weights.append(jnp.exp2(logits).astype(BF16))
                    tables.append(jnp.where(lane_half == h, values, zero))
                    if h % 2 == 1:
                        advance()
                table = jnp.concatenate([jnp.concatenate(tables, axis=0), ones_scr[...]], axis=1)
                total = mm(jnp.concatenate(weights, axis=1), table)
                mixed.append(total[:, :half] * (1.0 / total[:, half:]))
            finish(u, mixed)
        while waiting:
            advance()

    some = jnp.max(keep_ref[...].astype(F32), axis=1, keepdims=True)
    plain = jnp.min(some) == 0.0

    left_scr[...] = jnp.zeros_like(left_scr)
    unit = jnp.where(plain, 1.0, LOG2E)
    for k, ref in enumerate((own_ref, other_ref)):
        for h in range(some_heads):
            if raw:
                rows = residues // len(places)
                tile = ref[:, h * rows : (h + 1) * rows, :].astype(F32)
                tile = tile.reshape(residues, residues)
            else:
                tile = ref[h].astype(F32)
            bias_scr[k * some_heads + h] = tile * unit

    pl.when(plain)(functools.partial(run, True))
    pl.when(jnp.logical_not(plain))(functools.partial(run, False))

    rows = residues // len(places)
    marks = keep_ref[...].astype(F32)
    marks = jnp.concatenate(
        [marks[:, k * columns : (k + 1) * columns] for k in range(2)], axis=0
    ).astype(BF16)
    for t, (_, _, mate) in enumerate(places):
        tile = jnp.concatenate([left_scr[u * rows : (u + 1) * rows, :] for u in (t, mate)], axis=0)
        message_ref[t, span : span + 2 * rows, :] = tile.astype(BF16)
        message_ref[t, span + 2 * rows :, :] = marks
    if pieces:
        last = pltpu.make_async_copy(
            message_ref.at[:, span:, :], message_out.at[:, span:, :], message_sems.at[seqs]
        )
    else:
        last = pltpu.make_async_copy(message_ref, message_out, message_sems.at[seqs])
    last.start()
    for u in range(seqs):
        pltpu.make_async_copy(new_ref.at[u], new_out.at[u], new_sems.at[u]).wait()
        if pieces:
            departure(u).wait()
    last.wait()


def multiply(seqs, width, left, ref, scr, products):
    n, _, columns = ref.shape
    part = width // 2
    span = seqs * part
    block = left.shape[0] // width
    scr[...] = ref[:, :span, :].astype(F32).reshape(n * span, columns)
    for q in range(0, part, 2):
        pair = [
            jnp.concatenate(
                [scr[pl.ds(s * part + q + d, n, stride=span), :] for s in range(seqs)], axis=0
            ).astype(BF16)
            for d in range(2)
        ]
        outer = mm(left, jnp.concatenate(pair, axis=1)).astype(BF16)
        for d in range(2):
            at = (q + d) * width
            for i in range(block):
                products[i, at : at + width, :] = outer[
                    i * width : (i + 1) * width, d * columns : (d + 1) * columns
                ]


def outer_own_kernel(
    seqs,
    width,
    rows,
    core_ref,
    side_ref,
    first_mine_ref,
    first_theirs_ref,
    own_ref,
    table_ref,
    observed_ref,
    left_ref,
    scale_ref,
    marks_ref,
    update_ref,
    right_scr,
    small_scr,
    products,
):
    n, depth, columns = own_ref.shape
    block = 2 * rows
    total_seqs = n * seqs
    span = seqs * width // 2
    side, first_mine, first_theirs = side_ref[0], first_mine_ref[0], first_theirs_ref[0]
    extra = depth - span
    small_scr[...] = own_ref[:, span:, :].astype(F32).reshape(n * extra, columns)
    left_rows = []
    for i in range(block):
        piece = small_scr[pl.ds(i, n, stride=extra), :]
        for s in range(seqs):
            left_rows.append(piece[:, s * width : (s + 1) * width])
    left_all = jnp.concatenate(left_rows, axis=0).T
    left = jnp.concatenate(
        [left_all[:, i * total_seqs : (i + 1) * total_seqs] for i in range(block)], axis=0
    ).astype(BF16)
    left_ref[...] = left
    keep_halves = []
    for k in range(2):
        at = block + k * seqs
        keep_halves.append(
            jnp.concatenate(
                [small_scr[pl.ds(at + s, n, stride=extra), :] for s in range(seqs)], axis=0
            )
        )
    keep_columns = jnp.where(side == 0, keep_halves[0], keep_halves[1]).astype(BF16)
    keep = jnp.concatenate(keep_halves, axis=1).astype(BF16)
    pad = scale_ref.shape[0]
    order = lax.broadcasted_iota(jnp.int32, (pad, 2 * columns), 0)
    row_ids = jnp.where(order < rows, first_mine + order, first_theirs + order - rows)
    chosen = (row_ids == lax.broadcasted_iota(jnp.int32, (pad, 2 * columns), 1)).astype(BF16)
    counts = mm(mm(chosen, keep, NT).astype(BF16), keep_columns)
    scale_ref[...] = 1.0 / jnp.maximum(counts, 1.0)
    observed = observed_ref[...].astype(F32)
    row_marks = mm(chosen, jnp.broadcast_to(observed, (8, 2 * columns)).astype(BF16), NT)[:, :1]
    column_marks = jnp.where(side == 0, observed[:, :columns], observed[:, columns:])
    marks_ref[...] = row_marks * column_marks
    multiply(seqs, width, left, own_ref, right_scr, products)
    table = table_ref[core_ref[0]]
    for i in range(0, block, 2):
        update_ref[i // 2] = mm(table, jnp.concatenate([products[i], products[i + 1]], axis=1))


def outer_kernel(
    seqs,
    width,
    core_ref,
    other_ref,
    left_ref,
    scale_ref,
    marks_ref,
    own_update_ref,
    couple_mine_ref,
    couple_theirs_ref,
    table_ref,
    value_w_ref,
    gate_w_ref,
    pair_mine_ref,
    pair_theirs_ref,
    *rest,
):
    edges_refs, (right_scr, products, edge_scr) = rest[:-3], rest[-3:]
    rows, columns, channels = couple_mine_ref.shape
    block = 2 * rows
    multiply(seqs, width, left_ref[...], other_ref, right_scr, products)
    scale = scale_ref[...]
    table = table_ref[1 - core_ref[0]]
    updates, norms = {}, {}

    def project(i):
        part = mm(table, jnp.concatenate([products[i], products[i + 1]], axis=1))
        updates[i] = own_update_ref[i // 2] + part

    def add(i):
        normed = []
        for d in range(2):
            piece = updates[i][:, d * columns : (d + 1) * columns] * scale[i + d : i + d + 1, :]
            couple_ref, pair_ref = (
                (couple_mine_ref, pair_mine_ref)
                if i + d < rows
                else (couple_theirs_ref, pair_theirs_ref)
            )
            r = (i + d) % rows
            pair = (couple_ref[r].astype(F32) + piece.T).astype(BF16)
            pair_ref[r] = pair
            normed.append(normalize_rows(pair).astype(BF16))
        norms[i] = jnp.concatenate(normed, axis=0)

    def edge(i):
        values = mm(value_w_ref[...], norms[i], NT) * sigmoid(mm(gate_w_ref[...], norms[i], NT))
        for d in range(2):
            mark = marks_ref[i + d : i + d + 1, :]
            edge_scr[pl.ds(i + d, 2 * channels, stride=block), :] = (
                values[:, d * columns : (d + 1) * columns] * mark
            )

    for i in range(0, block + 4, 2):
        for stage, late in ((project, 0), (add, 2), (edge, 4)):
            if 0 <= i - late < block:
                stage(i - late)
    size = edges_refs[0].shape[0]
    for k, ref in enumerate(edges_refs):
        ref[...] = edge_scr[k * size : (k + 1) * size, :].astype(BF16)


def close_gate_kernel(mine_ref, theirs_ref, weight_ref, mine_gate_ref, theirs_gate_ref):
    for pair_ref, gate_ref in ((mine_ref, mine_gate_ref), (theirs_ref, theirs_gate_ref)):
        for i in range(pair_ref.shape[0]):
            normed = normalize(pair_ref[i]).astype(BF16)
            gate_ref[i] = sigmoid(mm(normed, weight_ref[...]))


def triangle_kernel(per, rows, places, in_ref, out_ref, in_scr, out_scr):
    n = in_ref.shape[0]
    residues = n * rows
    in_scr[...] = in_ref[...].astype(F32)

    def whole(at):
        tiles = []
        for t, (_, side, mate) in enumerate(places):
            pair = []
            for k in range(2):
                source, shift = (t, 0) if side == k else (mate, rows)
                pair.append(in_scr[source, at + shift : at + shift + rows, :])
            tiles.append(jnp.concatenate(pair, axis=1))
        return jnp.concatenate(tiles, axis=0).astype(BF16)

    for c in range(per):
        left = whole(c * 2 * rows)
        right = whole((per + c) * 2 * rows)
        out_scr[:, c * rows : (c + 1) * rows, :] = mm(left, right, NT).reshape(n, rows, residues)
    out_ref[...] = out_scr[...].astype(BF16)


def plain_triangle_kernel(left_ref, right_ref, out_ref):
    for c in range(left_ref.shape[0]):
        out_ref[c] = mm(left_ref[c], right_ref[c], NT).astype(BF16)


def close_kernel(
    side_ref, mine_ref, theirs_ref, mine_gate_ref, theirs_gate_ref, weight_ref, *rest
):
    count = (len(rest) - 1) // 2
    in_refs, out_ref, scrs = rest[:count], rest[count], rest[count + 1 :]
    rows, columns, channels = mine_ref.shape
    for ref, scr in zip(in_refs, scrs):
        fill(scr, ref[...].astype(F32))
    side = side_ref[0]
    for half, pair_ref, gate_ref in (
        (side, mine_ref, mine_gate_ref),
        (1 - side, theirs_ref, theirs_gate_ref),
    ):
        at = pl.multiple_of(half * columns, columns)
        for i in range(rows):
            piece = [scr[half, pl.ds(i, channels // count, stride=rows), :] for scr in scrs]
            piece = jnp.concatenate(piece, axis=0)
            update = mm(normalize(piece, axis=0).astype(BF16), weight_ref[...], TN)
            out_ref[i, pl.ds(at, columns), :] = (
                pair_ref[i].astype(F32) + gate_ref[i] * update
            ).astype(BF16)


def per_device(
    branch,
    dap,
    homolog_embedding,
    couple_embedding,
    homolog_present,
    observed_position,
    couple_logit_kernel,
    lookup_kernels,
    heads_sigmoid_kernel,
    heads_merge_kernel,
    tensor_halves_kernel,
    tensor_merge_kernel,
    edge_entry_kernel,
    closing_sigmoid_kernel,
    closing_merge_kernel,
):
    n = branch * dap
    rows, residues, channels = couple_embedding.shape
    seqs = homolog_embedding.shape[0]
    features = homolog_embedding.shape[2]
    heads = couple_logit_kernel.shape[1]
    inner = heads_sigmoid_kernel.shape[1]
    width = tensor_halves_kernel.shape[1] // 2
    per = channels // n
    half = residues // 2
    block = 2 * rows

    chunks = 1
    some = per // chunks
    places = [((t // dap) % 2, (t // dap // 2) % 2, (t // dap ^ 2) * dap + t % dap) for t in range(n)]
    me = lax.axis_index("branch").astype(jnp.int32)
    core = (me % 2).reshape(1)
    side = (me // 2 % 2).reshape(1)
    place = lax.axis_index("dap").astype(jnp.int32)
    first_mine = (me * dap + place) * rows
    first_theirs = ((me ^ 2) * dap + place) * rows
    chip = [(b, b ^ 1) for b in range(branch)]
    across = [(b, b ^ 2) for b in range(branch)]

    def exchange(values):
        return lax.all_to_all(values, EVERY, split_axis=0, concat_axis=0, tiled=True)

    def permute(values, pairs):
        return lax.ppermute(values, "branch", pairs)

    left_w, right_w, keep, ones = call(
        functools.partial(prepare_small_kernel, seqs, heads),
        (
            jax.ShapeDtypeStruct((seqs, features, seqs * width), BF16),
            jax.ShapeDtypeStruct((width, features), BF16),
            jax.ShapeDtypeStruct(homolog_present.shape, homolog_present.dtype),
            jax.ShapeDtypeStruct((heads // 2 * residues, inner // 2), BF16),
        ),
        (tensor_halves_kernel.T, stay(homolog_present)),
    )
    table, value_w, gate_w, final_w = call(
        functools.partial(prepare_large_kernel, chunks, per),
        (
            jax.ShapeDtypeStruct((2, channels, width // 2 * width), BF16),
            jax.ShapeDtypeStruct((2 * channels, channels), BF16),
            jax.ShapeDtypeStruct((2 * channels, channels), BF16),
            jax.ShapeDtypeStruct((channels, channels), BF16),
        ),
        (tensor_merge_kernel, edge_entry_kernel, closing_merge_kernel),
        [
            VMEM((width * width, channels), F32),
            VMEM((4 * channels, channels), F32),
            VMEM((2 * channels, channels), F32),
        ],
    )

    half_heads = heads // 2
    message, couple_mine, couple_send = call(
        functools.partial(bias_kernel, [place[0] for place in places]),
        (
            jax.ShapeDtypeStruct((n, half_heads * rows, residues), BF16),
            jax.ShapeDtypeStruct((rows, half, channels), BF16),
            jax.ShapeDtypeStruct((rows, half, channels), BF16),
        ),
        (side, stay(couple_embedding), stay(couple_logit_kernel.T)),
        [sheets(heads * rows, residues)],
        in_specs=[sspec(), vspec(), vspec()],
    )
    own_bias = exchange(message)
    raw = rows % 8 == 0
    if not raw:
        own_bias = own_bias.reshape(n, half_heads, rows, residues)
        own_bias = own_bias.transpose(1, 0, 2, 3).reshape(half_heads, residues, residues)
    other_bias = permute(own_bias, chip)
    couple_theirs = permute(couple_send, across)

    def whole(*shape):
        return pl.BlockSpec(shape, lambda s: (0,) * len(shape))

    def per_seq(batch, *shape):
        return pl.BlockSpec((batch, *shape), lambda s: (s,) + (0,) * len(shape))

    *parts, gates = pl.pallas_call(
        project_kernel,
        grid=(seqs,),
        out_shape=(
            jax.ShapeDtypeStruct((seqs, residues, inner), BF16),
            jax.ShapeDtypeStruct((seqs, inner, residues), BF16),
            jax.ShapeDtypeStruct((seqs, residues, inner), BF16),
            jax.ShapeDtypeStruct((seqs, residues, inner), F32),
        ),
        in_specs=[
            per_seq(1, residues, features),
            whole(features, 3 * inner),
            whole(features, inner),
        ],
        out_specs=(
            per_seq(1, residues, inner),
            per_seq(1, inner, residues),
            per_seq(1, residues, inner),
            per_seq(1, residues, inner),
        ),
        name="project",
        compiler_params=room(16),
        cost_estimate=pl.CostEstimate(flops=2**29, bytes_accessed=2**22, transcendentals=0),
    )(stay(homolog_embedding), stay(lookup_kernels), stay(heads_sigmoid_kernel))
    span = seqs * width // 2
    depth = span + block + 2 * seqs
    anywhere = pl.BlockSpec(memory_space=pl.ANY)
    new_shape = (seqs, residues, features)
    homolog_refreshed, message = pl.pallas_call(
        functools.partial(attend_kernel, heads, places, raw),
        out_shape=(
            jax.ShapeDtypeStruct(new_shape, BF16),
            jax.ShapeDtypeStruct((n, depth, half), BF16),
        ),
        in_specs=[sspec()] + [vspec()] * 7 + [anywhere] * 5,
        out_specs=(anywhere, anywhere),
        scratch_shapes=[
            VMEM(new_shape, BF16),
            VMEM((seqs, residues, inner), BF16),
            VMEM((seqs, inner, residues), BF16),
            VMEM((seqs, residues, inner), BF16),
            VMEM((seqs, residues, inner), F32),
            VMEM(new_shape, BF16),
            VMEM((n, depth, half), BF16),
            VMEM((residues, seqs * width), F32),
            VMEM((heads, residues, residues), F32),
            pltpu.SemaphoreType.DMA((5, seqs)),
            pltpu.SemaphoreType.DMA((seqs,)),
            pltpu.SemaphoreType.DMA((seqs + 1,)),
        ],
        name="attend",
        compiler_params=room(24),
        cost_estimate=pl.CostEstimate(flops=2**31, bytes_accessed=2**22, transcendentals=0),
    )(
        core,
        keep,
        own_bias,
        other_bias,
        heads_merge_kernel,
        left_w,
        right_w,
        ones,
        stay(homolog_embedding),
        *(stay(values) for values in parts),
        stay(gates),
    )

    own = exchange(message)
    other = permute(own, chip)
    firsts = (first_mine.reshape(1), first_theirs.reshape(1))
    left, scale, marks, update = call(
        functools.partial(outer_own_kernel, seqs, width, rows),
        (
            jax.ShapeDtypeStruct((block * width, n * seqs), BF16),
            jax.ShapeDtypeStruct((-(-block // 8) * 8, half), F32),
            jax.ShapeDtypeStruct((-(-block // 8) * 8, half), F32),
            jax.ShapeDtypeStruct((block // 2, channels, 2 * half), F32),
        ),
        (core, side, *firsts, own, table, stay(observed_position.reshape(1, residues))),
        [
            VMEM((n * span, half), F32),
            VMEM((n * (depth - span), half), F32),
            VMEM((block, width // 2 * width, half), BF16),
        ],
        need=16,
        in_specs=[sspec()] * 4 + [vspec()] * 3,
        flops=2**30,
    )
    piece = jax.ShapeDtypeStruct((rows, half, channels), BF16)
    pair_mine, pair_send, *edges = call(
        functools.partial(outer_kernel, seqs, width),
        (piece, piece)
        + (jax.ShapeDtypeStruct((2 * channels * block // chunks, half), BF16),) * chunks,
        (
            core,
            other,
            left,
            scale,
            marks,
            update,
            couple_mine,
            couple_theirs,
            table,
            value_w,
            gate_w,
        ),
        [
            VMEM((n * span, half), F32),
            VMEM((block, width // 2 * width, half), BF16),
            VMEM((2 * channels * block, half), F32),
        ],
        need=20,
        in_specs=[sspec()] + [vspec()] * 10,
        flops=2**31,
    )

    received = [exchange(values.reshape(n, 2 * some * block, half)) for values in edges]
    pair_theirs = permute(pair_send, across)
    gate_piece = jax.ShapeDtypeStruct((rows, half, channels), F32)
    gate_mine, gate_theirs = call(
        close_gate_kernel,
        (gate_piece, gate_piece),
        (pair_mine, pair_theirs, closing_sigmoid_kernel),
        flops=2**27,
    )

    def triangle(values):
        if rows % 8 == 0:
            return call(
                functools.partial(triangle_kernel, some, rows, places),
                jax.ShapeDtypeStruct((n, some * rows, residues), BF16),
                (values,),
                [
                    VMEM((n, 2 * some * block, half), F32),
                    VMEM((n, some * rows, residues), F32),
                ],
                need=12,
                flops=2**28,
            )
        both = values.reshape(branch // 4, 2, 2, dap, 2, some, 2, rows, half)
        both = jnp.stack([both[:, 0], both[:, 1, :, :, :, :, ::-1]], axis=1)
        both = both.transpose(4, 5, 0, 6, 2, 3, 7, 1, 8).reshape(2, some, residues, residues)
        combined = call(
            plain_triangle_kernel,
            jax.ShapeDtypeStruct((some, residues, residues), BF16),
            (both[0], both[1]),
            need=12,
            flops=2**28,
        )
        combined = combined.reshape(some, n, rows, residues).transpose(1, 0, 2, 3)
        return combined.reshape(n, some * rows, residues)

    returned = []
    for values in received:
        combined = triangle(values)
        combined = exchange(combined)
        returned.append(combined.reshape(n * some * rows, residues))
    pair_output = call(
        close_kernel,
        jax.ShapeDtypeStruct((rows, residues, channels), BF16),
        (side, pair_mine, pair_theirs, gate_mine, gate_theirs, final_w, *returned),
        [sheets(n * some * rows, residues) for _ in returned],
        in_specs=[sspec()] + [vspec()] * (5 + len(returned)),
        flops=2**27,
    )
    return (homolog_refreshed, pair_output)


def solution(mesh):
    split = P(EVERY, None, None)
    in_specs = (split, split, P(EVERY, None)) + (P(),) * 10

    def body(*args):
        return per_device(mesh.shape["branch"], mesh.shape["dap"], *args)

    return jax.shard_map(
        body, mesh=mesh, in_specs=in_specs, out_specs=(split, split), check_vma=False
    )
```
